128 devices in a mesh: expert: 4 (over y), dp: 32 (over x, z, core).
Axes of the slice: x: 4, y: 4, z: 4, core: 2. Of those that a mesh axis runs over, the one named last changes fastest.
Arguments:
- pool_tokens: bfloat16 [65536, 2048], P('dp', 'expert'), may hold values from -6 to 6
- pool_cotangent: bfloat16 [65536, 2048], P('dp', 'expert'), may hold values from -6 to 6
- token_ids: int32 [4, 16384], P('expert', 'dp'), may hold values from 0 to 2047, as said below
- route_weights: float32 [4, 16384], P('expert', 'dp'), may hold values from 0.1 to 1
- gate_weight: float32 [4, 2048, 512], P('expert', 'dp'), may hold values from -0.125 to 0.125
- up_weight: float32 [4, 2048, 512], P('expert', 'dp'), may hold values from -0.125 to 0.125
- down_weight: float32 [4, 512, 2048], P('expert', 'dp'), may hold values from -0.25 to 0.25
- momentum_gate: float32 [4, 2048, 512], P('expert', 'dp'), may hold values from -0.6 to 0.6
- momentum_up: float32 [4, 2048, 512], P('expert', 'dp'), may hold values from -0.6 to 0.6
- momentum_down: float32 [4, 512, 2048], P('expert', 'dp'), may hold values from -0.6 to 0.6
Outputs:
- new_gate: float32 [4, 2048, 512], P('expert', 'dp')
- new_up: float32 [4, 2048, 512], P('expert', 'dp')
- new_down: float32 [4, 512, 2048], P('expert', 'dp')
- new_momentum_gate: float32 [4, 2048, 512], P('expert', 'dp')
- new_momentum_up: float32 [4, 2048, 512], P('expert', 'dp')
- new_momentum_down: float32 [4, 512, 2048], P('expert', 'dp')
- pool_grad: float32 [65536, 2048], P('dp', 'expert')
The draws below stay inside these ranges and needn't reach their ends.
Inputs may be any that keep to these rules, and one draw needn't show every extreme that they name: `token_ids`: within one expert's 512 slots of one dp index the ids are distinct rows of that index's pool.
All inputs are finite; a program needn't handle non-finite values.
Results may differ from the reference program's by a relative error of at most 0.0066.
Values may be sent and summed in bfloat16 or wider, within the bound.
No kernel may reach another device: no remote copies, remote signals or barrier semaphores. Data moves between devices by JAX's collectives and lax.ppermute only.
A program may use at most 128 MiB of HBM per device.

```python
import math
import jax
import jax.numpy as jnp
from jax import lax

D = 2048
H = 512
TOK_DEV = 512
POOL = 2048
EXPERTS = 4
TOKENS = 16384
POOL_ALL = 65536
N_EXPERT = 4
N_DP = 32


def draw_token_ids(key, part):
    subkeys = jax.random.split(key, N_EXPERT * N_DP)
    orders = jax.vmap(lambda single: jax.random.permutation(single, POOL)[:TOK_DEV])(subkeys)
    return orders.reshape(N_EXPERT, N_DP * TOK_DEV).astype(jnp.int32)


def draw_pool_cotangent(key, part):
    column_mean = jax.random.normal(jax.random.fold_in(key, 11), (D,), jnp.float32)
    fluctuation = jax.random.normal(jax.random.fold_in(key, 12), (N_DP * POOL, D), jnp.float32)
    values = column_mean[None, :] + 0.5 * fluctuation
    return jnp.clip(values, -6.0, 6.0).astype(jnp.bfloat16)


def block_levels(rng, extent, shards, smallest, top_value):
    def one(axis_at, shards_of):
        heights = jax.random.uniform(jax.random.fold_in(jax.random.fold_in(rng, 6), axis_at), (shards_of,), jnp.float32, smallest / len(shards), top_value / len(shards))
        return jnp.repeat(jnp.exp(heights), extent[axis_at] // shards_of).reshape((-1,) + (1,) * (len(extent) - axis_at - 1))

    gain = one(*shards[0])
    for cut in shards[1:]:
        gain = gain * one(*cut)
    return gain


def scatter_about(rng, dims, spread, reach, pieces=(), kind=jnp.bfloat16):
    factor_of = block_levels(rng, dims, pieces, -0.22, 0.18) if pieces else 1.0
    array = jax.random.normal(rng, dims, jnp.float32) * spread * factor_of
    return jnp.minimum(jnp.maximum(array, -reach), reach).astype(kind)


def setup_inputs(seed: int = 0) -> dict:
    key_list = jax.random.split(jax.random.key(seed), 11)
    return {
        "pool_tokens": scatter_about(key_list[0], (POOL_ALL, D), 1.0, 6.0, ((0, 32), (1, 4))),
        "pool_cotangent": draw_pool_cotangent(jax.random.fold_in(key_list[10], 71), 0),
        "token_ids": draw_token_ids(jax.random.fold_in(key_list[10], 71), 0),
        "route_weights": jnp.clip(jnp.exp(math.log(1.0) - 2.3025851 * jax.random.uniform(key_list[3], (EXPERTS, TOKENS), jnp.float32) ** block_levels(key_list[3], (EXPERTS, TOKENS), ((0, 4), (1, 32)), -0.2, 0.2)), 0.1, 1.0),
        "gate_weight": scatter_about(key_list[4], (EXPERTS, D, H), D ** -0.5, 0.125, ((0, 4), (1, 32)), jnp.float32),
        "up_weight": scatter_about(key_list[5], (EXPERTS, D, H), D ** -0.5, 0.125, ((0, 4), (1, 32)), jnp.float32),
        "down_weight": scatter_about(key_list[6], (EXPERTS, H, D), H ** -0.5, 0.25, ((0, 4), (1, 32)), jnp.float32),
        "momentum_gate": scatter_about(key_list[7], (EXPERTS, D, H), 0.1, 0.6, ((0, 4), (1, 32)), jnp.float32),
        "momentum_up": scatter_about(key_list[8], (EXPERTS, D, H), 0.1, 0.6, ((0, 4), (1, 32)), jnp.float32),
        "momentum_down": scatter_about(key_list[9], (EXPERTS, H, D), 0.1, 0.6, ((0, 4), (1, 32)), jnp.float32),
    }


momentum_decay = 0.9
learning_rate = 0.05
epsilon = 1e-6


def expert_terms(gate_full, up_full, down_full, pool_x, pool_c, row_ids, route):
    routed = pool_x[row_ids]
    cot_rows = pool_c[row_ids]
    gate_pre = jnp.dot(routed, gate_full, preferred_element_type=jnp.float32)
    up_pre = jnp.dot(routed, up_full, preferred_element_type=jnp.float32)
    sig = jax.nn.sigmoid(gate_pre)
    act = gate_pre * sig
    hidden = (act * up_pre).astype(jnp.bfloat16)
    scaled_cot = (route[:, None] * cot_rows.astype(jnp.float32)).astype(jnp.bfloat16)
    grad_down = lax.dot_general(hidden, scaled_cot, (((0,), (0,)), ((), ())), preferred_element_type=jnp.float32) / TOK_DEV
    hidden_grad = lax.dot_general(scaled_cot, down_full, (((1,), (1,)), ((), ())), preferred_element_type=jnp.float32)
    gate_grad = (hidden_grad * up_pre * sig * (1.0 + gate_pre * (1.0 - sig))).astype(jnp.bfloat16)
    up_grad = (hidden_grad * act).astype(jnp.bfloat16)
    grad_gate = lax.dot_general(routed, gate_grad, (((0,), (0,)), ((), ())), preferred_element_type=jnp.float32) / TOK_DEV
    grad_up = lax.dot_general(routed, up_grad, (((0,), (0,)), ((), ())), preferred_element_type=jnp.float32) / TOK_DEV
    slot_grad = lax.dot_general(gate_grad, gate_full, (((1,), (1,)), ((), ())), preferred_element_type=jnp.float32)
    slot_grad = slot_grad + lax.dot_general(up_grad, up_full, (((1,), (1,)), ((), ())), preferred_element_type=jnp.float32)
    pool_term = jax.ops.segment_sum(slot_grad, row_ids, num_segments=POOL)
    grads = jnp.stack([grad_gate.reshape(-1), grad_up.reshape(-1), grad_down.reshape(-1)])
    return grads, pool_term


def adasum_merge(left_part, right_part):
    inner = jnp.sum(left_part * right_part, axis=-1)
    norm_left = jnp.sum(left_part * left_part, axis=-1)
    norm_right = jnp.sum(right_part * right_part, axis=-1)
    coef_left = 1.0 - inner / (2.0 * (norm_left + epsilon))
    coef_right = 1.0 - inner / (2.0 * (norm_right + epsilon))
    return coef_left[..., None] * left_part + coef_right[..., None] * right_part


def reference(pool_tokens, pool_cotangent, token_ids, route_weights, gate_weight, up_weight, down_weight, momentum_gate, momentum_up, momentum_down):
    pool_x = pool_tokens.reshape(N_DP, POOL, D)
    pool_c = pool_cotangent.reshape(N_DP, POOL, D)
    tiers = N_DP.bit_length() - 1

    def per_expert(running, expert_items):
        ids_e, route_e, gate_e, up_e, down_e, mom_gate, mom_up, mom_down = expert_items
        gate_full = gate_e.astype(jnp.bfloat16)
        up_full = up_e.astype(jnp.bfloat16)
        down_full = down_e.astype(jnp.bfloat16)

        def per_device(device_items):
            return expert_terms(gate_full, up_full, down_full, device_items[0], device_items[1], device_items[2], device_items[3])

        grads, pool_terms = lax.map(per_device, (pool_x, pool_c, ids_e.reshape(N_DP, TOK_DEV), route_e.reshape(N_DP, TOK_DEV)))
        running = running + pool_terms
        merged = grads
        for tier in range(tiers):
            paired = merged.reshape(merged.shape[0] // 2, 2, 3, D * H)
            merged = adasum_merge(paired[:, 0], paired[:, 1])
        merged = merged[0]
        next_gate = momentum_decay * mom_gate + merged[0].reshape(D, H)
        next_up = momentum_decay * mom_up + merged[1].reshape(D, H)
        next_down = momentum_decay * mom_down + merged[2].reshape(H, D)
        return running, (gate_e - learning_rate * next_gate, up_e - learning_rate * next_up, down_e - learning_rate * next_down, next_gate, next_up, next_down)

    start = jnp.zeros((N_DP, POOL, D), jnp.float32)
    running, updated = lax.scan(per_expert, start, (token_ids, route_weights, gate_weight, up_weight, down_weight, momentum_gate, momentum_up, momentum_down))
    return updated[0], updated[1], updated[2], updated[3], updated[4], updated[5], running.reshape(N_DP * POOL, D)
```

```python
import jax
import jax.numpy as jnp
from jax import lax
from jax.experimental import pallas as pl
from jax.experimental.pallas import tpu as pltpu
from jax.sharding import PartitionSpec as P

TOK_DEV = 512
POOL = 2048
D = 2048
H = 512
N_EXPERT = 4
N_CHIP = 16
SLICE = 512
ROWS = 192

momentum_decay = 0.9
learning_rate = 0.05
epsilon = 1e-06

MIB = 1 << 20
F32 = jnp.float32
BF16 = jnp.bfloat16
NT = (((1,), (1,)), ((), ()))


def vmem():
    return pl.BlockSpec(memory_space=pltpu.VMEM)


def call(body, name, n_in, out_shapes, flops, nbytes, scratch=(), limit=40):
    return pl.pallas_call(
        body,
        name=name,
        out_shape=out_shapes,
        in_specs=[vmem()] * n_in,
        out_specs=jax.tree.map(lambda _: vmem(), out_shapes),
        scratch_shapes=list(scratch),
        compiler_params=pltpu.CompilerParams(vmem_limit_bytes=limit * MIB),
        cost_estimate=pl.CostEstimate(flops=flops, bytes_accessed=nbytes, transcendentals=0),
    )


def struct(shape, dtype):
    return jax.ShapeDtypeStruct(shape, dtype)


def column(row):
    return jnp.broadcast_to(row, (128, row.shape[1])).T


def pick_rows(ids_rows, pools):
    n_ids, n_pool = len(ids_rows), len(pools)

    def body(*refs):
        ids, src = refs[:n_ids], refs[n_ids : n_ids + n_pool]
        out, hot = refs[n_ids + n_pool : -1], refs[-1]
        lane = lax.broadcasted_iota(jnp.int32, (TOK_DEV, 128), 1)
        for k in range(n_ids):
            named = column(ids[k][...])
            for j in range(POOL // 128):
                hot[:, 128 * j : 128 * (j + 1)] = jnp.where(named == lane + 128 * j, 1.0, 0.0).astype(BF16)
            for a in range(n_pool):
                rows = jnp.dot(hot[...], src[a][...], preferred_element_type=F32)
                out[k * n_pool + a][...] = rows.astype(BF16)

    shapes = [struct((TOK_DEV, SLICE), BF16)] * (n_ids * n_pool)
    return call(
        body,
        "pick_rows",
        n_ids + n_pool,
        shapes,
        2 * TOK_DEV * POOL * SLICE * n_ids * n_pool,
        (4 + 2 * n_ids) * MIB // 2,
        [pltpu.VMEM((TOK_DEV, POOL), BF16)],
    )(*ids_rows, *pools)


def slice_of(k):
    me = lax.axis_index("expert")
    return lax.rem(me + N_EXPERT - k, N_EXPERT)


def in_up_block(w, s):
    return w[pl.ds(pl.multiple_of(8 * s, 8), 8), 0:64, :].reshape(SLICE, 2 * H)


def down_block(w, s):
    row = pl.multiple_of(64 + 16 * (s // 2), 16)
    col = pl.multiple_of(SLICE * (s % 2), SLICE)
    return w[:, pl.ds(row, 16), pl.ds(col, SLICE)].reshape(H, SLICE)


def forward(tokens, weights):
    def body(x0, x1, x2, x3, w, hidden_t, gate_factor, act_out, xt, acc, hid):
        for k, x in enumerate((x0, x1, x2, x3)):
            part = jnp.dot(x[...], in_up_block(w, slice_of(k)), preferred_element_type=F32)
            if k == 0:
                acc[...] = part
            else:
                acc[...] += part
            xt[k] = x[...].T

        @pl.loop(0, TOK_DEV // 64)
        def _(i):
            rows = pl.ds(pl.multiple_of(i * 64, 64), 64)
            gate, up = acc[rows, :H], acc[rows, H:]
            sig = jax.nn.sigmoid(gate)
            act = gate * sig
            hid[rows, :] = (act * up).astype(BF16)
            gate_factor[rows, :] = up * sig * (1.0 + gate * (1.0 - sig))
            act_out[rows, :] = act

        hidden_t[...] = hid[...].T

    shapes = [
        struct((H, TOK_DEV), BF16),
        struct((TOK_DEV, H), F32),
        struct((TOK_DEV, H), F32),
        struct((N_EXPERT, SLICE, TOK_DEV), BF16),
    ]
    return call(
        body,
        "forward",
        5,
        shapes,
        2 * TOK_DEV * D * 2 * H,
        10 * MIB,
        [pltpu.VMEM((TOK_DEV, 2 * H), F32), pltpu.VMEM((TOK_DEV, H), BF16)],
    )(*tokens, weights)


def backward(cots, route, hidden_t, gate_factor, act, xt, weights):
    def body(c0, c1, c2, c3, route_ref, hid_t, factor, act_ref, xt_ref, w, keep, send, both, hg, scaled):
        first = lax.axis_index("dp") % 2 == 0
        scale = column(route_ref[...])
        for k, c in enumerate((c0, c1, c2, c3)):
            s = slice_of(k)
            for j in range(SLICE // 128):
                cols = slice(128 * j, 128 * (j + 1))
                scaled[:, cols] = (scale * c[:, cols].astype(F32)).astype(BF16)
            part = lax.dot_general(scaled[...], down_block(w, s), NT, preferred_element_type=F32)
            if k == 0:
                hg[...] = part
            else:
                hg[...] += part
            down = jnp.dot(hid_t[...], scaled[...], preferred_element_type=F32) / TOK_DEV
            down = down.astype(BF16).reshape(N_CHIP, 2, 16, SLICE)
            rows = pl.ds(pl.multiple_of(128 + 16 * s, 16), 16)
            keep[:, rows, :] = jnp.where(first, down[:, 0], down[:, 1])
            send[:, rows, :] = jnp.where(first, down[:, 1], down[:, 0])

        @pl.loop(0, TOK_DEV // 64)
        def _(i):
            rows = pl.ds(pl.multiple_of(i * 64, 64), 64)
            g = hg[rows, :]
            both[rows, :H] = (g * factor[rows, :]).astype(BF16)
            both[rows, H:] = (g * act_ref[rows, :]).astype(BF16)

        for k in range(N_EXPERT):
            chips = pl.ds(pl.multiple_of(4 * slice_of(k), 4), 4)
            grad = jnp.dot(xt_ref[k], both[...], preferred_element_type=F32) / TOK_DEV
            grad = grad.astype(BF16).reshape(4, 2, 64, 2 * H)
            for a in range(2):
                own = grad[:, 0, :, a * H : (a + 1) * H]
                other = grad[:, 1, :, a * H : (a + 1) * H]
                keep[chips, 64 * a : 64 * (a + 1), :] = jnp.where(first, own, other)
                send[chips, 64 * a : 64 * (a + 1), :] = jnp.where(first, other, own)

    shapes = [
        struct((N_CHIP, ROWS, SLICE), BF16),
        struct((N_CHIP, ROWS, SLICE), BF16),
        struct((TOK_DEV, 2 * H), BF16),
    ]
    return call(
        body,
        "backward",
        10,
        shapes,
        8 * TOK_DEV * D * H,
        20 * MIB,
        [pltpu.VMEM((TOK_DEV, H), F32), pltpu.VMEM((TOK_DEV, SLICE), BF16)],
    )(*cots, route, hidden_t, gate_factor, act, xt, weights)


def slot_gradients(both, weights):
    def body(both_ref, w, *out):
        for k in (2, 1, 3, 0):
            grad = lax.dot_general(both_ref[...], in_up_block(w, slice_of(k)), NT, preferred_element_type=F32)
            out[k][...] = grad.astype(BF16)

    shapes = [struct((TOK_DEV, SLICE), BF16)] * N_EXPERT
    return call(body, "slot_gradients", 2, shapes, 4 * TOK_DEV * D * H, 9 * MIB)(both, weights)


def pair_moments(own, other):
    def body(a_ref, b_ref, out):
        def step(q, sums):
            new = []
            for m in range(3):
                a = a_ref[q, 64 * m : 64 * (m + 1), :].astype(F32)
                b = b_ref[q, 64 * m : 64 * (m + 1), :].astype(F32)
                for t in (a * b, a * a, b * b):
                    t = jnp.sum(t.reshape(8, 8, SLICE), axis=0)
                    new.append(t[:, :128] + t[:, 128:256] + t[:, 256:384] + t[:, 384:])
            return tuple(s + n for s, n in zip(sums, new))

        sums = lax.fori_loop(0, N_CHIP, step, (jnp.zeros((8, 128), F32),) * 9)
        for j in range(9):
            out[j] = sums[j]

    return call(body, "pair_moments", 2, struct((9, 8, 128), F32), 9 * 2**20, 6 * MIB)(own, other)


def pair_merge(own, other, mine, theirs):
    def body(a_ref, b_ref, m_ref, t_ref, out):
        coefs = []
        for m in range(3):
            inner = jnp.sum(m_ref[3 * m] + t_ref[3 * m], keepdims=True)
            norm_a = jnp.sum(m_ref[3 * m + 1] + t_ref[3 * m + 2], keepdims=True)
            norm_b = jnp.sum(m_ref[3 * m + 2] + t_ref[3 * m + 1], keepdims=True)
            coef_a = 1.0 - inner / (2.0 * (norm_a + epsilon))
            coef_b = 1.0 - inner / (2.0 * (norm_b + epsilon))
            coefs.append((jnp.broadcast_to(coef_a, (64, SLICE)), jnp.broadcast_to(coef_b, (64, SLICE))))

        @pl.loop(0, N_CHIP)
        def _(q):
            for m in range(3):
                rows = slice(64 * m, 64 * (m + 1))
                a, b = a_ref[q, rows, :].astype(F32), b_ref[q, rows, :].astype(F32)
                out[q, rows, :] = (coefs[m][0] * a + coefs[m][1] * b).astype(BF16)

    return call(body, "pair_merge", 4, struct((N_CHIP, ROWS, SLICE), BF16), 9 * 2**20, 9 * MIB)(
        own, other, mine, theirs
    )


def gram(parts):
    def body(x, out):
        row = lax.broadcasted_iota(jnp.int32, (256, 256), 0)
        col = lax.broadcasted_iota(jnp.int32, (256, 256), 1)
        same = jnp.where(row % 16 == col % 16, 1.0, 0.0)
        fold = lax.broadcasted_iota(jnp.int32, (256, 128), 0) // 16
        fold = jnp.where(fold == lax.broadcasted_iota(jnp.int32, (256, 128), 1), 1.0, 0.0)
        for m in range(3):
            acc = None
            for b in range(4):
                at = 64 * m + 16 * b
                block = x[:, at : at + 16, :].reshape(256, SLICE)
                part = lax.dot_general(block, block, NT, preferred_element_type=F32)
                acc = part if acc is None else acc + part
            acc = jnp.sum((acc * same).reshape(16, 16, 256), axis=1)
            out[m] = jnp.dot(acc, fold, precision=lax.Precision.HIGHEST, preferred_element_type=F32)

    return call(body, "gram", 1, struct((3, 16, 128), F32), 12 * 2 * 256 * 256 * 512, 3 * MIB)(parts)


def finish(parts, products, gate, up, down, mom_gate, mom_up, mom_down):
    def body(x, g_ref, gate_w, up_w, down_w, gate_m, up_m, down_m, new_g, new_u, new_d, next_g, next_u, next_d):
        g = g_ref[...]
        i = lax.broadcasted_iota(jnp.int32, (3, 16, 128), 1)
        j = lax.broadcasted_iota(jnp.int32, (3, 16, 128), 2)
        c_col = jnp.ones((3, 16, 1), F32)
        c_row = jnp.ones((3, 1, 128), F32)
        for level in range(4):
            block_i, block_j = i >> level, j >> level
            same, sibling = block_i == block_j, (block_i ^ 1) == block_j
            weighted = g * c_col * c_row
            within = jnp.where(same, weighted, 0.0)
            across = jnp.where(sibling, weighted, 0.0)

            def coef(axis):
                norm = jnp.sum(jnp.where(same, jnp.sum(within, axis=3 - axis, keepdims=True), 0.0), axis=axis, keepdims=True)
                inner = jnp.sum(jnp.where(same, jnp.sum(across, axis=3 - axis, keepdims=True), 0.0), axis=axis, keepdims=True)
                return 1.0 - inner / (2.0 * (jnp.maximum(norm, 0.0) + epsilon))

            c_col, c_row = c_col * coef(2), c_row * coef(1)
        olds = ((gate_w, gate_m, new_g, next_g), (up_w, up_m, new_u, next_u))
        for m in range(3):
            merged = jnp.zeros((64, SLICE), F32)
            for q in range(16):
                scale = jnp.broadcast_to(c_col[m, q : q + 1, :], (64, SLICE))
                merged += scale * x[q, 64 * m : 64 * (m + 1), :].astype(F32)
            if m < 2:
                w, mom, new, after = olds[m]
                step = momentum_decay * mom[...] + merged
                after[...] = step
                new[...] = w[...] - learning_rate * step
            else:
                for k in range(4):
                    cols = slice(SLICE * k, SLICE * (k + 1))
                    step = momentum_decay * down_m[:, cols] + merged[16 * k : 16 * (k + 1), :]
                    next_d[:, cols] = step
                    new_d[:, cols] = down_w[:, cols] - learning_rate * step

    wide, tall = struct((64, H), F32), struct((16, D), F32)
    return call(body, "finish", 8, [wide, wide, tall, wide, wide, tall], 2**22, 6 * MIB)(
        parts, products, gate, up, down, mom_gate, mom_up, mom_down
    )


def scatter_rows(ids_rows, grads):
    block = 512

    def body(i0, i1, i2, i3, g0, g1, g2, g3, out):
        row = lax.broadcasted_iota(jnp.int32, (block, TOK_DEV), 0) + block * pl.program_id(0)
        acc = None
        for ids, g in zip((i0, i1, i2, i3), (g0, g1, g2, g3)):
            hot = jnp.where(jnp.broadcast_to(ids[...], row.shape) == row, 1.0, 0.0).astype(BF16)
            part = jnp.dot(hot, g[...], preferred_element_type=F32)
            acc = part if acc is None else acc + part
        out[...] = acc

    return pl.pallas_call(
        body,
        name="scatter_rows",
        grid=(POOL // block,),
        out_shape=struct((POOL, SLICE), F32),
        in_specs=[vmem()] * 8,
        out_specs=pl.BlockSpec((block, SLICE), lambda i: (i, 0)),
        compiler_params=pltpu.CompilerParams(vmem_limit_bytes=24 * MIB),
        cost_estimate=pl.CostEstimate(
            flops=2 * POOL * POOL * SLICE, bytes_accessed=6 * MIB, transcendentals=0
        ),
    )(*ids_rows, *grads)


def shift(block, axis, to):
    return lax.ppermute(block, axis, [(i, to(i)) for i in range(lax.axis_size(axis))])


def around_y(block, k):
    return shift(block, "expert", lambda i: (i + k) % N_EXPERT)


def around_z(block, k):
    return shift(block, "dp", lambda i: i // 8 * 8 + (i // 2 % 4 + k) % 4 * 2 + i % 2)


def around_x(block, k):
    return shift(block, "dp", lambda i: (i // 8 + k) % 4 * 8 + i % 8)


def other_core(block):
    return shift(block, "dp", lambda i: i ^ 1)


def sum_dp(value):
    for around in (around_z, around_x):
        value = value + sum(around(value, k) for k in (2, 1, 3))
    return value + other_core(value)


def local(
    pool_tokens,
    pool_cotangent,
    token_ids,
    route_weights,
    gate_weight,
    up_weight,
    down_weight,
    momentum_gate,
    momentum_up,
    momentum_down,
):
    down_halves = down_weight[0].astype(BF16)
    shard = jnp.concatenate(
        [
            jnp.concatenate([gate_weight[0].astype(BF16), up_weight[0].astype(BF16)], axis=1),
            down_halves[:, : D // 2],
            down_halves[:, D // 2 :],
        ],
        axis=0,
    )
    weights = lax.all_gather(shard, "dp", axis=0, tiled=False)

    ids = [token_ids] + [around_y(token_ids, N_EXPERT - k) for k in (1, 2, 3)]
    own_x, own_c = pick_rows(ids[:1], [pool_tokens, pool_cotangent])
    sent_x = pick_rows(ids[1:], [pool_tokens])
    sent_c = pick_rows(ids[1:], [pool_cotangent])
    tokens = [own_x] + [around_y(sent_x[k - 1], k) for k in (1, 2, 3)]
    cots = [own_c] + [around_y(sent_c[k - 1], k) for k in (1, 2, 3)]

    hidden_t, gate_factor, act, xt = forward(tokens, weights)
    keep, send, both = backward(cots, route_weights, hidden_t, gate_factor, act, xt, weights)
    received = other_core(send)
    slots = slot_gradients(both, weights)
    back = [slots[0]] + [around_y(slots[k], N_EXPERT - k) for k in (1, 2, 3)]
    received, _ = lax.optimization_barrier((received, slots))

    mine = pair_moments(keep, received)
    merged = pair_merge(keep, received, mine, other_core(mine))
    groups = [[2 * q + c for q in range(N_CHIP)] for c in range(2)]
    parts = lax.all_to_all(merged, "dp", 0, 0, tiled=True, axis_index_groups=groups)
    products = sum_dp(gram(parts))
    outs = finish(
        parts,
        products,
        gate_weight[0],
        up_weight[0],
        down_weight[0],
        momentum_gate[0],
        momentum_up[0],
        momentum_down[0],
    )
    pool_grad = scatter_rows(ids, back)
    return (*(a[None] for a in outs), pool_grad)


def solution(mesh):
    in_specs = (
        P("dp", "expert"),
        P("dp", "expert"),
        P("expert", "dp"),
        P("expert", "dp"),
        P("expert", "dp", None),
        P("expert", "dp", None),
        P("expert", "dp", None),
        P("expert", "dp", None),
        P("expert", "dp", None),
        P("expert", "dp", None),
    )
    out_specs = (
        P("expert", "dp", None),
        P("expert", "dp", None),
        P("expert", "dp", None),
        P("expert", "dp", None),
        P("expert", "dp", None),
        P("expert", "dp", None),
        P("dp", "expert"),
    )
    return jax.shard_map(local, mesh=mesh, in_specs=in_specs, out_specs=out_specs, check_vma=False)
```

```python
import jax
import jax.numpy as jnp
from jax import lax
from jax.experimental import pallas as pl
from jax.experimental.pallas import tpu as pltpu
from jax.sharding import PartitionSpec as P

TOK_DEV = 512
POOL = 2048
D = 2048
H = 512
N_EXPERT = 4
N_CHIP = 16
SLICE = 512
ROWS = 192

momentum_decay = 0.9
learning_rate = 0.05
epsilon = 1e-06

MIB = 1 << 20
F32 = jnp.float32
BF16 = jnp.bfloat16
NT = (((1,), (1,)), ((), ()))


def vmem():
    return pl.BlockSpec(memory_space=pltpu.VMEM)


def call(body, name, n_in, out_shapes, flops, nbytes, scratch=(), limit=20):
    return pl.pallas_call(
        body,
        name=name,
        out_shape=out_shapes,
        in_specs=[vmem()] * n_in,
        out_specs=jax.tree.map(lambda _: vmem(), out_shapes),
        scratch_shapes=list(scratch),
        compiler_params=pltpu.CompilerParams(vmem_limit_bytes=limit * MIB),
        cost_estimate=pl.CostEstimate(flops=flops, bytes_accessed=nbytes, transcendentals=0),
    )


def struct(shape, dtype):
    return jax.ShapeDtypeStruct(shape, dtype)


def column(row):
    return jnp.broadcast_to(row, (128, row.shape[1])).T


def pick_rows(ids_rows, pools):
    n_ids, n_pool = len(ids_rows), len(pools)

    def body(*refs):
        ids, src = refs[:n_ids], refs[n_ids : n_ids + n_pool]
        out, hot = refs[n_ids + n_pool : -1], refs[-1]
        lane = lax.broadcasted_iota(jnp.int32, (TOK_DEV, 128), 1)
        for k in range(n_ids):
            named = column(ids[k][...])
            for j in range(POOL // 128):
                hot[:, 128 * j : 128 * (j + 1)] = jnp.where(named == lane + 128 * j, 1.0, 0.0).astype(BF16)
            for a in range(n_pool):
                rows = jnp.dot(hot[...], src[a][...], preferred_element_type=F32)
                out[k * n_pool + a][...] = rows.astype(BF16)

    shapes = [struct((TOK_DEV, SLICE), BF16)] * (n_ids * n_pool)
    return call(
        body,
        "pick_rows",
        n_ids + n_pool,
        shapes,
        2 * TOK_DEV * POOL * SLICE * n_ids * n_pool,
        (4 + 2 * n_ids) * MIB // 2,
        [pltpu.VMEM((TOK_DEV, POOL), BF16)],
    )(*ids_rows, *pools)


def slice_of(k):
    me = lax.axis_index("expert")
    return lax.rem(me + N_EXPERT - k, N_EXPERT)


def in_up_block(w, s):
    return w[pl.ds(pl.multiple_of(8 * s, 8), 8), 0:64, :].reshape(SLICE, 2 * H)


def down_block(w, s):
    row = pl.multiple_of(64 + 16 * (s // 2), 16)
    col = pl.multiple_of(SLICE * (s % 2), SLICE)
    return w[:, pl.ds(row, 16), pl.ds(col, SLICE)].reshape(H, SLICE)


def forward(tokens, weights):
    def body(x0, x1, x2, x3, w, hidden_t, gate_factor, act_out, xt, acc, hid):
        for k, x in enumerate((x0, x1, x2, x3)):
            part = jnp.dot(x[...], in_up_block(w, slice_of(k)), preferred_element_type=F32)
            if k == 0:
                acc[...] = part
            else:
                acc[...] += part
            xt[k] = x[...].T

        @pl.loop(0, TOK_DEV // 64)
        def _(i):
            rows = pl.ds(pl.multiple_of(i * 64, 64), 64)
            gate, up = acc[rows, :H], acc[rows, H:]
            sig = jax.nn.sigmoid(gate)
            act = gate * sig
            hid[rows, :] = (act * up).astype(BF16)
            gate_factor[rows, :] = up * sig * (1.0 + gate * (1.0 - sig))
            act_out[rows, :] = act

        hidden_t[...] = hid[...].T

    shapes = [
        struct((H, TOK_DEV), BF16),
        struct((TOK_DEV, H), F32),
        struct((TOK_DEV, H), F32),
        struct((N_EXPERT, SLICE, TOK_DEV), BF16),
    ]
    return call(
        body,
        "forward",
        5,
        shapes,
        2 * TOK_DEV * D * 2 * H,
        10 * MIB,
        [pltpu.VMEM((TOK_DEV, 2 * H), F32), pltpu.VMEM((TOK_DEV, H), BF16)],
    )(*tokens, weights)


def backward(cots, route, hidden_t, gate_factor, act, xt, weights):
    def body(c0, c1, c2, c3, route_ref, hid_t, factor, act_ref, xt_ref, w, keep, send, both, hg, scaled):
        first = lax.axis_index("dp") % 2 == 0
        scale = column(route_ref[...])
        for k, c in enumerate((c0, c1, c2, c3)):
            s = slice_of(k)
            for j in range(SLICE // 128):
                cols = slice(128 * j, 128 * (j + 1))
                scaled[:, cols] = (scale * c[:, cols].astype(F32)).astype(BF16)
            part = lax.dot_general(scaled[...], down_block(w, s), NT, preferred_element_type=F32)
            if k == 0:
                hg[...] = part
            else:
                hg[...] += part
            down = jnp.dot(hid_t[...], scaled[...], preferred_element_type=F32) / TOK_DEV
            down = down.astype(BF16).reshape(N_CHIP, 2, 16, SLICE)
            rows = pl.ds(pl.multiple_of(128 + 16 * s, 16), 16)
            keep[:, rows, :] = jnp.where(first, down[:, 0], down[:, 1])
            send[:, rows, :] = jnp.where(first, down[:, 1], down[:, 0])

        @pl.loop(0, TOK_DEV // 64)
        def _(i):
            rows = pl.ds(pl.multiple_of(i * 64, 64), 64)
            g = hg[rows, :]
            both[rows, :H] = (g * factor[rows, :]).astype(BF16)
            both[rows, H:] = (g * act_ref[rows, :]).astype(BF16)

        for k in range(N_EXPERT):
            chips = pl.ds(pl.multiple_of(4 * slice_of(k), 4), 4)
            grad = jnp.dot(xt_ref[k], both[...], preferred_element_type=F32) / TOK_DEV
            grad = grad.astype(BF16).reshape(4, 2, 64, 2 * H)
            for a in range(2):
                own = grad[:, 0, :, a * H : (a + 1) * H]
                other = grad[:, 1, :, a * H : (a + 1) * H]
                keep[chips, 64 * a : 64 * (a + 1), :] = jnp.where(first, own, other)
                send[chips, 64 * a : 64 * (a + 1), :] = jnp.where(first, other, own)

    shapes = [
        struct((N_CHIP, ROWS, SLICE), BF16),
        struct((N_CHIP, ROWS, SLICE), BF16),
        struct((TOK_DEV, 2 * H), BF16),
    ]
    return call(
        body,
        "backward",
        10,
        shapes,
        8 * TOK_DEV * D * H,
        20 * MIB,
        [pltpu.VMEM((TOK_DEV, H), F32), pltpu.VMEM((TOK_DEV, SLICE), BF16)],
    )(*cots, route, hidden_t, gate_factor, act, xt, weights)


def slot_gradients(both, weights):
    def body(both_ref, w, *out):
        for k in (2, 1, 3, 0):
            grad = lax.dot_general(both_ref[...], in_up_block(w, slice_of(k)), NT, preferred_element_type=F32)
            out[k][...] = grad.astype(BF16)

    shapes = [struct((TOK_DEV, SLICE), BF16)] * N_EXPERT
    return call(body, "slot_gradients", 2, shapes, 4 * TOK_DEV * D * H, 9 * MIB)(both, weights)


def pair_moments(own, other):
    def body(a_ref, b_ref, out):
        def step(q, sums):
            new = []
            for m in range(3):
                a = a_ref[q, 64 * m : 64 * (m + 1), :].astype(F32)
                b = b_ref[q, 64 * m : 64 * (m + 1), :].astype(F32)
                for t in (a * b, a * a, b * b):
                    t = jnp.sum(t.reshape(8, 8, SLICE), axis=0)
                    new.append(t[:, :128] + t[:, 128:256] + t[:, 256:384] + t[:, 384:])
            return tuple(s + n for s, n in zip(sums, new))

        sums = lax.fori_loop(0, N_CHIP, step, (jnp.zeros((8, 128), F32),) * 9)
        for j in range(9):
            out[j] = sums[j]

    return call(body, "pair_moments", 2, struct((9, 8, 128), F32), 9 * 2**20, 6 * MIB)(own, other)


def pair_merge(own, other, mine, theirs):
    step = 4

    def body(a_ref, b_ref, m_ref, t_ref, out):
        coefs = []
        for m in range(3):
            inner = jnp.sum(m_ref[3 * m] + t_ref[3 * m], keepdims=True)
            norm_a = jnp.sum(m_ref[3 * m + 1] + t_ref[3 * m + 2], keepdims=True)
            norm_b = jnp.sum(m_ref[3 * m + 2] + t_ref[3 * m + 1], keepdims=True)
            coef_a = 1.0 - inner / (2.0 * (norm_a + epsilon))
            coef_b = 1.0 - inner / (2.0 * (norm_b + epsilon))
            coefs.append((jnp.broadcast_to(coef_a, (64, SLICE)), jnp.broadcast_to(coef_b, (64, SLICE))))

        for i in range(step):
            q = pl.program_id(0) * step + i
            for m in range(3):
                rows = slice(64 * m, 64 * (m + 1))
                a, b = a_ref[q, rows, :].astype(F32), b_ref[q, rows, :].astype(F32)
                out[i, rows, :] = (coefs[m][0] * a + coefs[m][1] * b).astype(BF16)

    return pl.pallas_call(
        body,
        name="pair_merge",
        grid=(N_CHIP // step,),
        out_shape=struct((N_CHIP, ROWS, SLICE), BF16),
        in_specs=[vmem()] * 4,
        out_specs=pl.BlockSpec((step, ROWS, SLICE), lambda i: (i, 0, 0)),
        compiler_params=pltpu.CompilerParams(vmem_limit_bytes=20 * MIB),
        cost_estimate=pl.CostEstimate(flops=9 * 2**20, bytes_accessed=9 * MIB, transcendentals=0),
    )(own, other, mine, theirs)


def gram(parts):
    def body(x, out):
        row = lax.broadcasted_iota(jnp.int32, (256, 256), 0)
        col = lax.broadcasted_iota(jnp.int32, (256, 256), 1)
        same = jnp.where(row % 16 == col % 16, 1.0, 0.0)
        fold = lax.broadcasted_iota(jnp.int32, (256, 128), 0) // 16
        fold = jnp.where(fold == lax.broadcasted_iota(jnp.int32, (256, 128), 1), 1.0, 0.0)
        for m in range(3):
            acc = None
            for b in range(4):
                at = 64 * m + 16 * b
                block = x[:, at : at + 16, :].reshape(256, SLICE)
                part = lax.dot_general(block, block, NT, preferred_element_type=F32)
                acc = part if acc is None else acc + part
            acc = jnp.sum((acc * same).reshape(16, 16, 256), axis=1)
            out[m] = jnp.dot(acc, fold, precision=lax.Precision.HIGHEST, preferred_element_type=F32)

    return call(body, "gram", 1, struct((3, 16, 128), F32), 12 * 2 * 256 * 256 * 512, 3 * MIB)(parts)


def finish(parts, products, gate, up, down, mom_gate, mom_up, mom_down):
    def body(x, g_ref, gate_w, up_w, down_w, gate_m, up_m, down_m, new_g, new_u, new_d, next_g, next_u, next_d):
        g = g_ref[...]
        i = lax.broadcasted_iota(jnp.int32, (3, 16, 128), 1)
        j = lax.broadcasted_iota(jnp.int32, (3, 16, 128), 2)
        c_col = jnp.ones((3, 16, 1), F32)
        c_row = jnp.ones((3, 1, 128), F32)
        for level in range(4):
            block_i, block_j = i >> level, j >> level
            same, sibling = block_i == block_j, (block_i ^ 1) == block_j
            weighted = g * c_col * c_row
            within = jnp.where(same, weighted, 0.0)
            across = jnp.where(sibling, weighted, 0.0)

            def coef(axis):
                norm = jnp.sum(jnp.where(same, jnp.sum(within, axis=3 - axis, keepdims=True), 0.0), axis=axis, keepdims=True)
                inner = jnp.sum(jnp.where(same, jnp.sum(across, axis=3 - axis, keepdims=True), 0.0), axis=axis, keepdims=True)
                return 1.0 - inner / (2.0 * (jnp.maximum(norm, 0.0) + epsilon))

            c_col, c_row = c_col * coef(2), c_row * coef(1)
        olds = ((gate_w, gate_m, new_g, next_g), (up_w, up_m, new_u, next_u))
        for m in range(3):
            merged = jnp.zeros((64, SLICE), F32)
            for q in range(16):
                scale = jnp.broadcast_to(c_col[m, q : q + 1, :], (64, SLICE))
                merged += scale * x[q, 64 * m : 64 * (m + 1), :].astype(F32)
            if m < 2:
                w, mom, new, after = olds[m]
                step = momentum_decay * mom[...] + merged
                after[...] = step
                new[...] = w[...] - learning_rate * step
            else:
                for k in range(4):
                    cols = slice(SLICE * k, SLICE * (k + 1))
                    step = momentum_decay * down_m[:, cols] + merged[16 * k : 16 * (k + 1), :]
                    next_d[:, cols] = step
                    new_d[:, cols] = down_w[:, cols] - learning_rate * step

    wide, tall = struct((64, H), F32), struct((16, D), F32)
    return call(body, "finish", 8, [wide, wide, tall, wide, wide, tall], 2**22, 6 * MIB)(
        parts, products, gate, up, down, mom_gate, mom_up, mom_down
    )


def scatter_rows(ids_rows, grads):
    block = 512

    def body(i0, i1, i2, i3, g0, g1, g2, g3, out):
        row = lax.broadcasted_iota(jnp.int32, (block, TOK_DEV), 0) + block * pl.program_id(0)
        acc = None
        for ids, g in zip((i0, i1, i2, i3), (g0, g1, g2, g3)):
            hot = jnp.where(jnp.broadcast_to(ids[...], row.shape) == row, 1.0, 0.0).astype(BF16)
            part = jnp.dot(hot, g[...], preferred_element_type=F32)
            acc = part if acc is None else acc + part
        out[...] = acc

    return pl.pallas_call(
        body,
        name="scatter_rows",
        grid=(POOL // block,),
        out_shape=struct((POOL, SLICE), F32),
        in_specs=[vmem()] * 8,
        out_specs=pl.BlockSpec((block, SLICE), lambda i: (i, 0)),
        compiler_params=pltpu.CompilerParams(vmem_limit_bytes=24 * MIB),
        cost_estimate=pl.CostEstimate(
            flops=2 * POOL * POOL * SLICE, bytes_accessed=6 * MIB, transcendentals=0
        ),
    )(*ids_rows, *grads)


def shift(block, axis, to):
    return lax.ppermute(block, axis, [(i, to(i)) for i in range(lax.axis_size(axis))])


def around_y(block, k):
    return shift(block, "expert", lambda i: (i + k) % N_EXPERT)


def around_z(block, k):
    return shift(block, "dp", lambda i: i // 8 * 8 + (i // 2 % 4 + k) % 4 * 2 + i % 2)


def around_x(block, k):
    return shift(block, "dp", lambda i: (i // 8 + k) % 4 * 8 + i % 8)


def other_core(block):
    return shift(block, "dp", lambda i: i ^ 1)


def sum_dp(value):
    for around in (around_z, around_x):
        value = value + sum(around(value, k) for k in (2, 1, 3))
    return value + other_core(value)


def local(
    pool_tokens,
    pool_cotangent,
    token_ids,
    route_weights,
    gate_weight,
    up_weight,
    down_weight,
    momentum_gate,
    momentum_up,
    momentum_down,
):
    down_halves = down_weight[0].astype(BF16)
    shard = jnp.concatenate(
        [
            jnp.concatenate([gate_weight[0].astype(BF16), up_weight[0].astype(BF16)], axis=1),
            down_halves[:, : D // 2],
            down_halves[:, D // 2 :],
        ],
        axis=0,
    )
    weights = lax.all_gather(shard, "dp", axis=0, tiled=False)

    ids = [token_ids] + [around_y(token_ids, N_EXPERT - k) for k in (1, 2, 3)]
    own_x, own_c = pick_rows(ids[:1], [pool_tokens, pool_cotangent])
    ids, own_x, own_c = lax.optimization_barrier((ids, own_x, own_c))
    sent_x, sent_c = [None] * 3, [None] * 3
    for sent, pool in ((sent_x, pool_tokens), (sent_c, pool_cotangent)):
        for k in (2, 1, 3):
            (sent[k - 1],) = pick_rows(ids[k : k + 1], [pool])
    tokens = [own_x] + [around_y(sent_x[k - 1], k) for k in (1, 2, 3)]
    cots = [own_c] + [around_y(sent_c[k - 1], k) for k in (1, 2, 3)]

    hidden_t, gate_factor, act, xt = forward(tokens, weights)
    keep, send, both = backward(cots, route_weights, hidden_t, gate_factor, act, xt, weights)
    received = other_core(send)
    slots = slot_gradients(both, weights)
    back = [slots[0]] + [around_y(slots[k], N_EXPERT - k) for k in (1, 2, 3)]
    received, _ = lax.optimization_barrier((received, slots))

    mine = pair_moments(keep, received)
    merged = pair_merge(keep, received, mine, other_core(mine))
    groups = [[2 * q + c for q in range(N_CHIP)] for c in range(2)]
    parts = lax.all_to_all(merged, "dp", 0, 0, tiled=True, axis_index_groups=groups)
    pool_grad = scatter_rows(ids, back)
    parts, pool_grad = lax.optimization_barrier((parts, pool_grad))
    products = sum_dp(gram(parts))
    outs = finish(
        parts,
        products,
        gate_weight[0],
        up_weight[0],
        down_weight[0],
        momentum_gate[0],
        momentum_up[0],
        momentum_down[0],
    )
    return (*(a[None] for a in outs), pool_grad)


def solution(mesh):
    in_specs = (
        P("dp", "expert"),
        P("dp", "expert"),
        P("expert", "dp"),
        P("expert", "dp"),
        P("expert", "dp", None),
        P("expert", "dp", None),
        P("expert", "dp", None),
        P("expert", "dp", None),
        P("expert", "dp", None),
        P("expert", "dp", None),
    )
    out_specs = (
        P("expert", "dp", None),
        P("expert", "dp", None),
        P("expert", "dp", None),
        P("expert", "dp", None),
        P("expert", "dp", None),
        P("expert", "dp", None),
        P("dp", "expert"),
    )
    return jax.shard_map(local, mesh=mesh, in_specs=in_specs, out_specs=out_specs, check_vma=False)
```

```python
import jax
import jax.numpy as jnp
from jax import lax
from jax.experimental import pallas as pl
from jax.experimental.pallas import tpu as pltpu
from jax.sharding import PartitionSpec as P

TOK_DEV = 512
POOL = 2048
D = 2048
H = 512
N_EXPERT = 4
N_CHIP = 16
SLICE = 512
ROWS = 192
EARLY = 160

momentum_decay = 0.9
learning_rate = 0.05
epsilon = 1e-06

MIB = 1 << 20
F32 = jnp.float32
BF16 = jnp.bfloat16
NT = (((1,), (1,)), ((), ()))


def vmem():
    return pl.BlockSpec(memory_space=pltpu.VMEM)


def call(body, name, n_in, out_shapes, flops, nbytes, scratch=(), limit=20):
    return pl.pallas_call(
        body,
        name=name,
        out_shape=out_shapes,
        in_specs=[vmem()] * n_in,
        out_specs=jax.tree.map(lambda _: vmem(), out_shapes),
        scratch_shapes=list(scratch),
        compiler_params=pltpu.CompilerParams(vmem_limit_bytes=limit * MIB),
        cost_estimate=pl.CostEstimate(flops=flops, bytes_accessed=nbytes, transcendentals=0),
    )


def struct(shape, dtype):
    return jax.ShapeDtypeStruct(shape, dtype)


def column(row):
    return jnp.broadcast_to(row, (128, row.shape[1])).T


def pick_rows(ids_rows, pools):
    n_ids, n_pool = len(ids_rows), len(pools)

    def body(*refs):
        ids, src = refs[:n_ids], refs[n_ids : n_ids + n_pool]
        out, hot = refs[n_ids + n_pool : -1], refs[-1]
        lane = lax.broadcasted_iota(jnp.int32, (TOK_DEV, 128), 1)
        for k in range(n_ids):
            named = column(ids[k][...])
            for j in range(POOL // 128):
                hot[:, 128 * j : 128 * (j + 1)] = jnp.where(named == lane + 128 * j, 1.0, 0.0).astype(BF16)
            for a in range(n_pool):
                rows = jnp.dot(hot[...], src[a][...], preferred_element_type=F32)
                out[k * n_pool + a][...] = rows.astype(BF16)

    shapes = [struct((TOK_DEV, SLICE), BF16)] * (n_ids * n_pool)
    return call(
        body,
        "pick_rows",
        n_ids + n_pool,
        shapes,
        2 * TOK_DEV * POOL * SLICE * n_ids * n_pool,
        (4 + 2 * n_ids) * MIB // 2,
        [pltpu.VMEM((TOK_DEV, POOL), BF16)],
    )(*ids_rows, *pools)


def slice_of(k):
    me = lax.axis_index("expert")
    return lax.rem(me + N_EXPERT - k, N_EXPERT)


def in_up_block(w, s):
    return w[pl.ds(pl.multiple_of(8 * s, 8), 8), 0:64, :].reshape(SLICE, 2 * H)


def down_block(w, s):
    row = pl.multiple_of(64 + 16 * (s // 2), 16)
    col = pl.multiple_of(SLICE * (s % 2), SLICE)
    return w[:, pl.ds(row, 16), pl.ds(col, SLICE)].reshape(H, SLICE)


def forward(tokens, weights):
    def body(x0, x1, x2, x3, w, hidden_t, gate_factor, act_out, xt, acc, hid):
        for k, x in enumerate((x0, x1, x2, x3)):
            part = jnp.dot(x[...], in_up_block(w, slice_of(k)), preferred_element_type=F32)
            if k == 0:
                acc[...] = part
            else:
                acc[...] += part
            xt[k] = x[...].T

        @pl.loop(0, TOK_DEV // 64)
        def _(i):
            rows = pl.ds(pl.multiple_of(i * 64, 64), 64)
            gate, up = acc[rows, :H], acc[rows, H:]
            sig = jax.nn.sigmoid(gate)
            act = gate * sig
            hid[rows, :] = (act * up).astype(BF16)
            gate_factor[rows, :] = up * sig * (1.0 + gate * (1.0 - sig))
            act_out[rows, :] = act

        hidden_t[...] = hid[...].T

    shapes = [
        struct((H, TOK_DEV), BF16),
        struct((TOK_DEV, H), F32),
        struct((TOK_DEV, H), F32),
        struct((N_EXPERT, SLICE, TOK_DEV), BF16),
    ]
    return call(
        body,
        "forward",
        5,
        shapes,
        2 * TOK_DEV * D * 2 * H,
        10 * MIB,
        [pltpu.VMEM((TOK_DEV, 2 * H), F32), pltpu.VMEM((TOK_DEV, H), BF16)],
    )(*tokens, weights)


def backward(cots, route, hidden_t, gate_factor, act, xt, weights):
    def body(*refs):
        early, late = refs[:4], refs[4:8]
        route_ref, hid_t, factor, act_ref, xt_ref, w, keep, send, both, hg, scaled = refs[8:]
        first = lax.axis_index("dp") % 2 == 0
        scale = column(route_ref[...])
        for k in range(N_EXPERT):
            s = slice_of(k)
            for j in range(SLICE // 128):
                cols = slice(128 * j, 128 * (j + 1))
                scaled[:EARLY, cols] = (scale[:EARLY] * early[k][:, cols].astype(F32)).astype(BF16)
                scaled[EARLY:, cols] = (scale[EARLY:] * late[k][:, cols].astype(F32)).astype(BF16)
            part = lax.dot_general(scaled[...], down_block(w, s), NT, preferred_element_type=F32)
            if k == 0:
                hg[...] = part
            else:
                hg[...] += part
            down = jnp.dot(hid_t[...], scaled[...], preferred_element_type=F32) / TOK_DEV
            down = down.astype(BF16).reshape(N_CHIP, 2, 16, SLICE)
            rows = pl.ds(pl.multiple_of(128 + 16 * s, 16), 16)
            keep[:, rows, :] = jnp.where(first, down[:, 0], down[:, 1])
            send[:, rows, :] = jnp.where(first, down[:, 1], down[:, 0])

        @pl.loop(0, TOK_DEV // 64)
        def _(i):
            rows = pl.ds(pl.multiple_of(i * 64, 64), 64)
            g = hg[rows, :]
            both[rows, :H] = (g * factor[rows, :]).astype(BF16)
            both[rows, H:] = (g * act_ref[rows, :]).astype(BF16)

        for k in range(N_EXPERT):
            chips = pl.ds(pl.multiple_of(4 * slice_of(k), 4), 4)
            grad = jnp.dot(xt_ref[k], both[...], preferred_element_type=F32) / TOK_DEV
            grad = grad.astype(BF16).reshape(4, 2, 64, 2 * H)
            for a in range(2):
                own = grad[:, 0, :, a * H : (a + 1) * H]
                other = grad[:, 1, :, a * H : (a + 1) * H]
                keep[chips, 64 * a : 64 * (a + 1), :] = jnp.where(first, own, other)
                send[chips, 64 * a : 64 * (a + 1), :] = jnp.where(first, other, own)

    shapes = [
        struct((N_CHIP, ROWS, SLICE), BF16),
        struct((N_CHIP, ROWS, SLICE), BF16),
        struct((TOK_DEV, 2 * H), BF16),
    ]
    return call(
        body,
        "backward",
        14,
        shapes,
        8 * TOK_DEV * D * H,
        20 * MIB,
        [pltpu.VMEM((TOK_DEV, H), F32), pltpu.VMEM((TOK_DEV, SLICE), BF16)],
    )(*cots, route, hidden_t, gate_factor, act, xt, weights)


def slot_gradients(both, weights):
    def body(both_ref, w, *out):
        for k in (2, 1, 3, 0):
            grad = lax.dot_general(both_ref[...], in_up_block(w, slice_of(k)), NT, preferred_element_type=F32)
            out[k][...] = grad.astype(BF16)

    shapes = [struct((TOK_DEV, SLICE), BF16)] * N_EXPERT
    return call(body, "slot_gradients", 2, shapes, 4 * TOK_DEV * D * H, 9 * MIB)(both, weights)


def pair_moments(own, other):
    def body(a_ref, b_ref, out):
        def step(q, sums):
            new = []
            for m in range(3):
                a = a_ref[q, 64 * m : 64 * (m + 1), :].astype(F32)
                b = b_ref[q, 64 * m : 64 * (m + 1), :].astype(F32)
                for t in (a * b, a * a, b * b):
                    t = jnp.sum(t.reshape(8, 8, SLICE), axis=0)
                    new.append(t[:, :128] + t[:, 128:256] + t[:, 256:384] + t[:, 384:])
            return tuple(s + n for s, n in zip(sums, new))

        sums = lax.fori_loop(0, N_CHIP, step, (jnp.zeros((8, 128), F32),) * 9)
        for j in range(9):
            out[j] = sums[j]

    return call(body, "pair_moments", 2, struct((9, 8, 128), F32), 9 * 2**20, 6 * MIB)(own, other)


def pair_merge(own, other, mine, theirs):
    step = 4

    def body(a_ref, b_ref, m_ref, t_ref, out):
        coefs = []
        for m in range(3):
            inner = jnp.sum(m_ref[3 * m] + t_ref[3 * m], keepdims=True)
            norm_a = jnp.sum(m_ref[3 * m + 1] + t_ref[3 * m + 2], keepdims=True)
            norm_b = jnp.sum(m_ref[3 * m + 2] + t_ref[3 * m + 1], keepdims=True)
            coef_a = 1.0 - inner / (2.0 * (norm_a + epsilon))
            coef_b = 1.0 - inner / (2.0 * (norm_b + epsilon))
            coefs.append((jnp.broadcast_to(coef_a, (64, SLICE)), jnp.broadcast_to(coef_b, (64, SLICE))))

        for i in range(step):
            q = pl.program_id(0) * step + i
            for m in range(3):
                rows = slice(64 * m, 64 * (m + 1))
                a, b = a_ref[q, rows, :].astype(F32), b_ref[q, rows, :].astype(F32)
                out[i, rows, :] = (coefs[m][0] * a + coefs[m][1] * b).astype(BF16)

    return pl.pallas_call(
        body,
        name="pair_merge",
        grid=(N_CHIP // step,),
        out_shape=struct((N_CHIP, ROWS, SLICE), BF16),
        in_specs=[vmem()] * 4,
        out_specs=pl.BlockSpec((step, ROWS, SLICE), lambda i: (i, 0, 0)),
        compiler_params=pltpu.CompilerParams(vmem_limit_bytes=20 * MIB),
        cost_estimate=pl.CostEstimate(flops=9 * 2**20, bytes_accessed=9 * MIB, transcendentals=0),
    )(own, other, mine, theirs)


def gram(parts):
    def body(x, out):
        row = lax.broadcasted_iota(jnp.int32, (256, 256), 0)
        col = lax.broadcasted_iota(jnp.int32, (256, 256), 1)
        same = jnp.where(row % 16 == col % 16, 1.0, 0.0)
        fold = lax.broadcasted_iota(jnp.int32, (256, 128), 0) // 16
        fold = jnp.where(fold == lax.broadcasted_iota(jnp.int32, (256, 128), 1), 1.0, 0.0)
        for m in range(3):
            acc = None
            for b in range(4):
                at = 64 * m + 16 * b
                block = x[:, at : at + 16, :].reshape(256, SLICE)
                part = lax.dot_general(block, block, NT, preferred_element_type=F32)
                acc = part if acc is None else acc + part
            acc = jnp.sum((acc * same).reshape(16, 16, 256), axis=1)
            out[m] = jnp.dot(acc, fold, precision=lax.Precision.HIGHEST, preferred_element_type=F32)

    return call(body, "gram", 1, struct((3, 16, 128), F32), 12 * 2 * 256 * 256 * 512, 3 * MIB)(parts)


def finish(parts, products, gate, up, down, mom_gate, mom_up, mom_down):
    def body(x, g_ref, gate_w, up_w, down_w, gate_m, up_m, down_m, new_g, new_u, new_d, next_g, next_u, next_d):
        g = g_ref[...]
        i = lax.broadcasted_iota(jnp.int32, (3, 16, 128), 1)
        j = lax.broadcasted_iota(jnp.int32, (3, 16, 128), 2)
        c_col = jnp.ones((3, 16, 1), F32)
        c_row = jnp.ones((3, 1, 128), F32)
        for level in range(4):
            block_i, block_j = i >> level, j >> level
            same, sibling = block_i == block_j, (block_i ^ 1) == block_j
            weighted = g * c_col * c_row
            within = jnp.where(same, weighted, 0.0)
            across = jnp.where(sibling, weighted, 0.0)

            def coef(axis):
                norm = jnp.sum(jnp.where(same, jnp.sum(within, axis=3 - axis, keepdims=True), 0.0), axis=axis, keepdims=True)
                inner = jnp.sum(jnp.where(same, jnp.sum(across, axis=3 - axis, keepdims=True), 0.0), axis=axis, keepdims=True)
                return 1.0 - inner / (2.0 * (jnp.maximum(norm, 0.0) + epsilon))

            c_col, c_row = c_col * coef(2), c_row * coef(1)
        olds = ((gate_w, gate_m, new_g, next_g), (up_w, up_m, new_u, next_u))
        for m in range(3):
            merged = jnp.zeros((64, SLICE), F32)
            for q in range(16):
                scale = jnp.broadcast_to(c_col[m, q : q + 1, :], (64, SLICE))
                merged += scale * x[q, 64 * m : 64 * (m + 1), :].astype(F32)
            if m < 2:
                w, mom, new, after = olds[m]
                step = momentum_decay * mom[...] + merged
                after[...] = step
                new[...] = w[...] - learning_rate * step
            else:
                for k in range(4):
                    cols = slice(SLICE * k, SLICE * (k + 1))
                    step = momentum_decay * down_m[:, cols] + merged[16 * k : 16 * (k + 1), :]
                    next_d[:, cols] = step
                    new_d[:, cols] = down_w[:, cols] - learning_rate * step

    wide, tall = struct((64, H), F32), struct((16, D), F32)
    return call(body, "finish", 8, [wide, wide, tall, wide, wide, tall], 2**22, 6 * MIB)(
        parts, products, gate, up, down, mom_gate, mom_up, mom_down
    )


def scatter_rows(ids_rows, grads):
    block = 512

    def body(i0, i1, i2, i3, g0, g1, g2, g3, out):
        row = lax.broadcasted_iota(jnp.int32, (block, TOK_DEV), 0) + block * pl.program_id(0)
        acc = None
        for ids, g in zip((i0, i1, i2, i3), (g0, g1, g2, g3)):
            hot = jnp.where(jnp.broadcast_to(ids[...], row.shape) == row, 1.0, 0.0).astype(BF16)
            part = jnp.dot(hot, g[...], preferred_element_type=F32)
            acc = part if acc is None else acc + part
        out[...] = acc

    return pl.pallas_call(
        body,
        name="scatter_rows",
        grid=(POOL // block,),
        out_shape=struct((POOL, SLICE), F32),
        in_specs=[vmem()] * 8,
        out_specs=pl.BlockSpec((block, SLICE), lambda i: (i, 0)),
        compiler_params=pltpu.CompilerParams(vmem_limit_bytes=24 * MIB),
        cost_estimate=pl.CostEstimate(
            flops=2 * POOL * POOL * SLICE, bytes_accessed=6 * MIB, transcendentals=0
        ),
    )(*ids_rows, *grads)


def shift(block, axis, to):
    return lax.ppermute(block, axis, [(i, to(i)) for i in range(lax.axis_size(axis))])


def around_y(block, k):
    return shift(block, "expert", lambda i: (i + k) % N_EXPERT)


def around_z(block, k):
    return shift(block, "dp", lambda i: i // 8 * 8 + (i // 2 % 4 + k) % 4 * 2 + i % 2)


def around_x(block, k):
    return shift(block, "dp", lambda i: (i // 8 + k) % 4 * 8 + i % 8)


def other_core(block):
    return shift(block, "dp", lambda i: i ^ 1)


def sum_dp(value):
    for around in (around_z, around_x):
        value = value + sum(around(value, k) for k in (2, 1, 3))
    return value + other_core(value)


def pack(gate, up, down):
    def body(g, u, d, out):
        out[0:64, 0:H] = g[...].astype(BF16)
        out[0:64, H:] = u[...].astype(BF16)
        out[64:80, :] = d[:, : D // 2].astype(BF16)
        out[80:96, :] = d[:, D // 2 :].astype(BF16)

    return call(body, "pack", 3, struct((96, 1024), BF16), 2**17, MIB)(gate, up, down)


def along(turn, step):
    def to(i):
        x, z, c = i // 8, i // 2 % 4, i % 2
        return x * 8 + (z + step) % 4 * 2 + c if c == turn else (x + step) % 4 * 8 + z * 2 + c

    return to


def ring_near(block, turn):
    return shift(block, "dp", along(turn, 1)), shift(block, "dp", along(turn, 3))


def ring_far(before, after, turn):
    half = before.shape[0] // 2
    return shift(before[:half], "dp", along(turn, 1)), shift(after[half:], "dp", along(turn, 3))


def place(turn):
    at = lax.axis_index("dp")
    x, z, c = at // 8, lax.rem(at // 2, 4), lax.rem(at, 2)
    return c, jnp.where(c == turn, z, x)


def bundle(blocks):
    def body(own, before, after, low, high, out):
        _, at = place(0)
        out[at] = own[...]
        out[lax.rem(at + 3, 4)] = before[...]
        out[lax.rem(at + 1, 4)] = after[...]
        far = lax.rem(at + 2, 4)
        out[far, 0:48, :] = low[...]
        out[far, 48:96, :] = high[...]

    return call(body, "bundle", 5, struct((4, 96, 1024), BF16), 2**10, 2 * MIB)(*blocks)


def half_of_weights(bundles):
    def body(own, before, after, low, high, out):
        c, at = place(1)

        def put(j, other, value):
            out[jnp.where(c == 0, other * 4 + j, j * 4 + other)] = value

        for j in range(4):
            put(j, at, own[j])
            put(j, lax.rem(at + 3, 4), before[j])
            put(j, lax.rem(at + 1, 4), after[j])
            put(j, lax.rem(at + 2, 4), (low, high)[j // 2][j % 2])

    return call(body, "half_of_weights", 5, struct((N_CHIP, 96, 1024), BF16), 2**10, 6 * MIB)(*bundles)


def whole_weights(own, other):
    def body(a, b, out):
        c = lax.rem(lax.axis_index("dp"), 2)

        @pl.loop(0, N_CHIP)
        def _(q):
            out[2 * q + c] = a[q]
            out[2 * q + 1 - c] = b[q]

    return call(body, "whole_weights", 2, struct((2 * N_CHIP, 96, 1024), BF16), 2**10, 12 * MIB)(own, other)


def local(
    pool_tokens,
    pool_cotangent,
    token_ids,
    route_weights,
    gate_weight,
    up_weight,
    down_weight,
    momentum_gate,
    momentum_up,
    momentum_down,
):
    tie = lax.optimization_barrier
    ids = [token_ids] + [around_y(token_ids, N_EXPERT - k) for k in (1, 2, 3)]
    packed = pack(gate_weight[0], up_weight[0], down_weight[0])
    near = ring_near(packed, 0)
    own_x, own_c = pick_rows(ids[:1], [pool_tokens, pool_cotangent])
    ids, own_x, own_c, near = tie((ids, own_x, own_c, near))

    far = ring_far(*near, 0)
    sent_x = [pick_rows(ids[k : k + 1], [pool_tokens])[0] for k in (1, 2, 3)]
    far, sent_x = tie((far, sent_x))

    tokens = [around_y(sent_x[k - 1], k) for k in (1, 2, 3)]
    block = bundle((packed, *near, *far))
    near = ring_near(block, 1)
    sent_c = [pick_rows(ids[k : k + 1], [pool_cotangent])[0] for k in (1, 2, 3)]
    near, tokens, sent_c = tie((near, tokens, sent_c))
    tokens = [own_x, *tokens]

    far = ring_far(*near, 1)
    early = [around_y(sent_c[k - 1][:EARLY], k) for k in (1, 2, 3)]
    late = [sent_c[k - 1][EARLY:] for k in (1, 2, 3)]
    far, early, late = tie((far, early, late))

    late = [around_y(late[k - 1], k) for k in (1, 2, 3)]
    cots = [own_c[:EARLY], *early, own_c[EARLY:], *late]
    mine = half_of_weights((block, *near, *far))
    weights = whole_weights(mine, other_core(mine))

    hidden_t, gate_factor, act, xt = forward(tokens, weights)
    keep, send, both = backward(cots, route_weights, hidden_t, gate_factor, act, xt, weights)
    received = other_core(send)
    slots = slot_gradients(both, weights)
    back = [slots[0]] + [around_y(slots[k], N_EXPERT - k) for k in (1, 2, 3)]
    received, _ = lax.optimization_barrier((received, slots))

    mine = pair_moments(keep, received)
    merged = pair_merge(keep, received, mine, other_core(mine))
    groups = [[2 * q + c for q in range(N_CHIP)] for c in range(2)]
    parts = lax.all_to_all(merged, "dp", 0, 0, tiled=True, axis_index_groups=groups)
    pool_grad = scatter_rows(ids, back)
    parts, pool_grad = lax.optimization_barrier((parts, pool_grad))
    products = sum_dp(gram(parts))
    outs = finish(
        parts,
        products,
        gate_weight[0],
        up_weight[0],
        down_weight[0],
        momentum_gate[0],
        momentum_up[0],
        momentum_down[0],
    )
    return (*(a[None] for a in outs), pool_grad)


def solution(mesh):
    in_specs = (
        P("dp", "expert"),
        P("dp", "expert"),
        P("expert", "dp"),
        P("expert", "dp"),
        P("expert", "dp", None),
        P("expert", "dp", None),
        P("expert", "dp", None),
        P("expert", "dp", None),
        P("expert", "dp", None),
        P("expert", "dp", None),
    )
    out_specs = (
        P("expert", "dp", None),
        P("expert", "dp", None),
        P("expert", "dp", None),
        P("expert", "dp", None),
        P("expert", "dp", None),
        P("expert", "dp", None),
        P("dp", "expert"),
    )
    return jax.shard_map(local, mesh=mesh, in_specs=in_specs, out_specs=out_specs, check_vma=False)
```

```python
import jax
import jax.numpy as jnp
from jax import lax
from jax.experimental import pallas as pl
from jax.experimental.pallas import tpu as pltpu
from jax.sharding import PartitionSpec as P

TOK_DEV = 512
POOL = 2048
D = 2048
H = 512
N_EXPERT = 4
N_CHIP = 16
SLICE = 512
ROWS = 192

momentum_decay = 0.9
learning_rate = 0.05
epsilon = 1e-06

MIB = 1 << 20
F32 = jnp.float32
BF16 = jnp.bfloat16
NT = (((1,), (1,)), ((), ()))


def vmem():
    return pl.BlockSpec(memory_space=pltpu.VMEM)


def call(body, name, n_in, out_shapes, flops, nbytes, scratch=(), limit=20):
    return pl.pallas_call(
        body,
        name=name,
        out_shape=out_shapes,
        in_specs=[vmem()] * n_in,
        out_specs=jax.tree.map(lambda _: vmem(), out_shapes),
        scratch_shapes=list(scratch),
        compiler_params=pltpu.CompilerParams(vmem_limit_bytes=limit * MIB),
        cost_estimate=pl.CostEstimate(flops=flops, bytes_accessed=nbytes, transcendentals=0),
    )


def struct(shape, dtype):
    return jax.ShapeDtypeStruct(shape, dtype)


def column(row):
    return jnp.broadcast_to(row, (128, row.shape[1])).T


def pick_rows(ids_rows, pools):
    n_ids, n_pool = len(ids_rows), len(pools)

    def body(*refs):
        ids, src = refs[:n_ids], refs[n_ids : n_ids + n_pool]
        out, hot = refs[n_ids + n_pool : -1], refs[-1]
        lane = lax.broadcasted_iota(jnp.int32, (TOK_DEV, 128), 1)
        for k in range(n_ids):
            named = column(ids[k][...])
            for j in range(POOL // 128):
                hot[:, 128 * j : 128 * (j + 1)] = jnp.where(named == lane + 128 * j, 1.0, 0.0).astype(BF16)
            for a in range(n_pool):
                rows = jnp.dot(hot[...], src[a][...], preferred_element_type=F32)
                out[k * n_pool + a][...] = rows.astype(BF16)

    shapes = [struct((TOK_DEV, SLICE), BF16)] * (n_ids * n_pool)
    return call(
        body,
        "pick_rows",
        n_ids + n_pool,
        shapes,
        2 * TOK_DEV * POOL * SLICE * n_ids * n_pool,
        (4 + 2 * n_ids) * MIB // 2,
        [pltpu.VMEM((TOK_DEV, POOL), BF16)],
    )(*ids_rows, *pools)


def slice_of(k):
    me = lax.axis_index("expert")
    return lax.rem(me + N_EXPERT - k, N_EXPERT)


def in_up_block(w, s):
    return w[pl.ds(pl.multiple_of(8 * s, 8), 8), 0:64, :].reshape(SLICE, 2 * H)


def down_block(w, s):
    row = pl.multiple_of(64 + 16 * (s // 2), 16)
    col = pl.multiple_of(SLICE * (s % 2), SLICE)
    return w[:, pl.ds(row, 16), pl.ds(col, SLICE)].reshape(H, SLICE)


def forward(tokens, weights):
    def body(x0, x1, x2, x3, w, hidden_t, gate_factor, act_out, xt, acc, hid):
        for k, x in enumerate((x0, x1, x2, x3)):
            part = jnp.dot(x[...], in_up_block(w, slice_of(k)), preferred_element_type=F32)
            if k == 0:
                acc[...] = part
            else:
                acc[...] += part
            xt[k] = x[...].T

        @pl.loop(0, TOK_DEV // 64)
        def _(i):
            rows = pl.ds(pl.multiple_of(i * 64, 64), 64)
            gate, up = acc[rows, :H], acc[rows, H:]
            sig = jax.nn.sigmoid(gate)
            act = gate * sig
            hid[rows, :] = (act * up).astype(BF16)
            gate_factor[rows, :] = up * sig * (1.0 + gate * (1.0 - sig))
            act_out[rows, :] = act

        hidden_t[...] = hid[...].T

    shapes = [
        struct((H, TOK_DEV), BF16),
        struct((TOK_DEV, H), F32),
        struct((TOK_DEV, H), F32),
        struct((N_EXPERT, SLICE, TOK_DEV), BF16),
    ]
    return call(
        body,
        "forward",
        5,
        shapes,
        2 * TOK_DEV * D * 2 * H,
        10 * MIB,
        [pltpu.VMEM((TOK_DEV, 2 * H), F32), pltpu.VMEM((TOK_DEV, H), BF16)],
    )(*tokens, weights)


def backward(cots, route, hidden_t, gate_factor, act, xt, weights):
    def body(c0, c1, c2, c3, route_ref, hid_t, factor, act_ref, xt_ref, w, keep, send, both, hg, scaled):
        first = lax.axis_index("dp") % 2 == 0
        scale = column(route_ref[...])
        for k, c in enumerate((c0, c1, c2, c3)):
            s = slice_of(k)
            for j in range(SLICE // 128):
                cols = slice(128 * j, 128 * (j + 1))
                scaled[:, cols] = (scale * c[:, cols].astype(F32)).astype(BF16)
            part = lax.dot_general(scaled[...], down_block(w, s), NT, preferred_element_type=F32)
            if k == 0:
                hg[...] = part
            else:
                hg[...] += part
            down = jnp.dot(hid_t[...], scaled[...], preferred_element_type=F32) / TOK_DEV
            down = down.astype(BF16).reshape(N_CHIP, 2, 16, SLICE)
            rows = pl.ds(pl.multiple_of(128 + 16 * s, 16), 16)
            keep[:, rows, :] = jnp.where(first, down[:, 0], down[:, 1])
            send[:, rows, :] = jnp.where(first, down[:, 1], down[:, 0])

        @pl.loop(0, TOK_DEV // 64)
        def _(i):
            rows = pl.ds(pl.multiple_of(i * 64, 64), 64)
            g = hg[rows, :]
            both[rows, :H] = (g * factor[rows, :]).astype(BF16)
            both[rows, H:] = (g * act_ref[rows, :]).astype(BF16)

        for k in range(N_EXPERT):
            chips = pl.ds(pl.multiple_of(4 * slice_of(k), 4), 4)
            grad = jnp.dot(xt_ref[k], both[...], preferred_element_type=F32) / TOK_DEV
            grad = grad.astype(BF16).reshape(4, 2, 64, 2 * H)
            for a in range(2):
                own = grad[:, 0, :, a * H : (a + 1) * H]
                other = grad[:, 1, :, a * H : (a + 1) * H]
                keep[chips, 64 * a : 64 * (a + 1), :] = jnp.where(first, own, other)
                send[chips, 64 * a : 64 * (a + 1), :] = jnp.where(first, other, own)

    shapes = [
        struct((N_CHIP, ROWS, SLICE), BF16),
        struct((N_CHIP, ROWS, SLICE), BF16),
        struct((TOK_DEV, 2 * H), BF16),
    ]
    return call(
        body,
        "backward",
        10,
        shapes,
        8 * TOK_DEV * D * H,
        20 * MIB,
        [pltpu.VMEM((TOK_DEV, H), F32), pltpu.VMEM((TOK_DEV, SLICE), BF16)],
    )(*cots, route, hidden_t, gate_factor, act, xt, weights)


def slot_gradients(both, weights):
    def body(both_ref, w, *out):
        for k in (2, 1, 3, 0):
            grad = lax.dot_general(both_ref[...], in_up_block(w, slice_of(k)), NT, preferred_element_type=F32)
            out[k][...] = grad.astype(BF16)

    shapes = [struct((TOK_DEV, SLICE), BF16)] * N_EXPERT
    return call(body, "slot_gradients", 2, shapes, 4 * TOK_DEV * D * H, 9 * MIB)(both, weights)


def pair_moments(own, other):
    def body(a_ref, b_ref, out):
        def step(q, sums):
            new = []
            for m in range(3):
                a = a_ref[q, 64 * m : 64 * (m + 1), :].astype(F32)
                b = b_ref[q, 64 * m : 64 * (m + 1), :].astype(F32)
                for t in (a * b, a * a, b * b):
                    t = jnp.sum(t.reshape(8, 8, SLICE), axis=0)
                    new.append(t[:, :128] + t[:, 128:256] + t[:, 256:384] + t[:, 384:])
            return tuple(s + n for s, n in zip(sums, new))

        sums = lax.fori_loop(0, N_CHIP, step, (jnp.zeros((8, 128), F32),) * 9)
        for j in range(9):
            out[j] = sums[j]

    return call(body, "pair_moments", 2, struct((9, 8, 128), F32), 9 * 2**20, 6 * MIB)(own, other)


def pair_merge(own, other, mine, theirs):
    step = 4

    def body(a_ref, b_ref, m_ref, t_ref, out):
        coefs = []
        for m in range(3):
            inner = jnp.sum(m_ref[3 * m] + t_ref[3 * m], keepdims=True)
            norm_a = jnp.sum(m_ref[3 * m + 1] + t_ref[3 * m + 2], keepdims=True)
            norm_b = jnp.sum(m_ref[3 * m + 2] + t_ref[3 * m + 1], keepdims=True)
            coef_a = 1.0 - inner / (2.0 * (norm_a + epsilon))
            coef_b = 1.0 - inner / (2.0 * (norm_b + epsilon))
            coefs.append((jnp.broadcast_to(coef_a, (64, SLICE)), jnp.broadcast_to(coef_b, (64, SLICE))))

        for i in range(step):
            q = pl.program_id(0) * step + i
            for m in range(3):
                rows = slice(64 * m, 64 * (m + 1))
                a, b = a_ref[q, rows, :].astype(F32), b_ref[q, rows, :].astype(F32)
                out[i, rows, :] = (coefs[m][0] * a + coefs[m][1] * b).astype(BF16)

    return pl.pallas_call(
        body,
        name="pair_merge",
        grid=(N_CHIP // step,),
        out_shape=struct((N_CHIP, ROWS, SLICE), BF16),
        in_specs=[vmem()] * 4,
        out_specs=pl.BlockSpec((step, ROWS, SLICE), lambda i: (i, 0, 0)),
        compiler_params=pltpu.CompilerParams(vmem_limit_bytes=20 * MIB),
        cost_estimate=pl.CostEstimate(flops=9 * 2**20, bytes_accessed=9 * MIB, transcendentals=0),
    )(own, other, mine, theirs)


def gram(parts):
    def body(x, out):
        row = lax.broadcasted_iota(jnp.int32, (256, 256), 0)
        col = lax.broadcasted_iota(jnp.int32, (256, 256), 1)
        same = jnp.where(row % 16 == col % 16, 1.0, 0.0)
        fold = lax.broadcasted_iota(jnp.int32, (256, 128), 0) // 16
        fold = jnp.where(fold == lax.broadcasted_iota(jnp.int32, (256, 128), 1), 1.0, 0.0)
        for m in range(3):
            acc = None
            for b in range(4):
                at = 64 * m + 16 * b
                block = x[:, at : at + 16, :].reshape(256, SLICE)
                part = lax.dot_general(block, block, NT, preferred_element_type=F32)
                acc = part if acc is None else acc + part
            acc = jnp.sum((acc * same).reshape(16, 16, 256), axis=1)
            out[m] = jnp.dot(acc, fold, precision=lax.Precision.HIGHEST, preferred_element_type=F32)

    return call(body, "gram", 1, struct((3, 16, 128), F32), 12 * 2 * 256 * 256 * 512, 3 * MIB)(parts)


def finish(parts, products, gate, up, down, mom_gate, mom_up, mom_down):
    def body(x, g_ref, gate_w, up_w, down_w, gate_m, up_m, down_m, new_g, new_u, new_d, next_g, next_u, next_d):
        g = g_ref[...]
        i = lax.broadcasted_iota(jnp.int32, (3, 16, 128), 1)
        j = lax.broadcasted_iota(jnp.int32, (3, 16, 128), 2)
        c_col = jnp.ones((3, 16, 1), F32)
        c_row = jnp.ones((3, 1, 128), F32)
        for level in range(4):
            block_i, block_j = i >> level, j >> level
            same, sibling = block_i == block_j, (block_i ^ 1) == block_j
            weighted = g * c_col * c_row
            within = jnp.where(same, weighted, 0.0)
            across = jnp.where(sibling, weighted, 0.0)

            def coef(axis):
                norm = jnp.sum(jnp.where(same, jnp.sum(within, axis=3 - axis, keepdims=True), 0.0), axis=axis, keepdims=True)
                inner = jnp.sum(jnp.where(same, jnp.sum(across, axis=3 - axis, keepdims=True), 0.0), axis=axis, keepdims=True)
                return 1.0 - inner / (2.0 * (jnp.maximum(norm, 0.0) + epsilon))

            c_col, c_row = c_col * coef(2), c_row * coef(1)
        olds = ((gate_w, gate_m, new_g, next_g), (up_w, up_m, new_u, next_u))
        for m in range(3):
            merged = jnp.zeros((64, SLICE), F32)
            for q in range(16):
                scale = jnp.broadcast_to(c_col[m, q : q + 1, :], (64, SLICE))
                merged += scale * x[q, 64 * m : 64 * (m + 1), :].astype(F32)
            if m < 2:
                w, mom, new, after = olds[m]
                step = momentum_decay * mom[...] + merged
                after[...] = step
                new[...] = w[...] - learning_rate * step
            else:
                for k in range(4):
                    cols = slice(SLICE * k, SLICE * (k + 1))
                    step = momentum_decay * down_m[:, cols] + merged[16 * k : 16 * (k + 1), :]
                    next_d[:, cols] = step
                    new_d[:, cols] = down_w[:, cols] - learning_rate * step

    wide, tall = struct((64, H), F32), struct((16, D), F32)
    return call(body, "finish", 8, [wide, wide, tall, wide, wide, tall], 2**22, 6 * MIB)(
        parts, products, gate, up, down, mom_gate, mom_up, mom_down
    )


def scatter_rows(ids_rows, grads):
    block = 512

    def body(i0, i1, i2, i3, g0, g1, g2, g3, out):
        row = lax.broadcasted_iota(jnp.int32, (block, TOK_DEV), 0) + block * pl.program_id(0)
        acc = None
        for ids, g in zip((i0, i1, i2, i3), (g0, g1, g2, g3)):
            hot = jnp.where(jnp.broadcast_to(ids[...], row.shape) == row, 1.0, 0.0).astype(BF16)
            part = jnp.dot(hot, g[...], preferred_element_type=F32)
            acc = part if acc is None else acc + part
        out[...] = acc

    return pl.pallas_call(
        body,
        name="scatter_rows",
        grid=(POOL // block,),
        out_shape=struct((POOL, SLICE), F32),
        in_specs=[vmem()] * 8,
        out_specs=pl.BlockSpec((block, SLICE), lambda i: (i, 0)),
        compiler_params=pltpu.CompilerParams(vmem_limit_bytes=24 * MIB),
        cost_estimate=pl.CostEstimate(
            flops=2 * POOL * POOL * SLICE, bytes_accessed=6 * MIB, transcendentals=0
        ),
    )(*ids_rows, *grads)


def shift(block, axis, to):
    return lax.ppermute(block, axis, [(i, to(i)) for i in range(lax.axis_size(axis))])


def around_y(block, k):
    return shift(block, "expert", lambda i: (i + k) % N_EXPERT)


def around_z(block, k):
    return shift(block, "dp", lambda i: i // 8 * 8 + (i // 2 % 4 + k) % 4 * 2 + i % 2)


def around_x(block, k):
    return shift(block, "dp", lambda i: (i // 8 + k) % 4 * 8 + i % 8)


def other_core(block):
    return shift(block, "dp", lambda i: i ^ 1)


def sum_dp(value):
    for around in (around_z, around_x):
        value = value + sum(around(value, k) for k in (2, 1, 3))
    return value + other_core(value)


def pack(gate, up, down, pool):
    def body(gate_hbm, up_hbm, down_hbm, pool_ref, out, g, u, d, sems):
        copies = [
            pltpu.make_async_copy(src, dst, sems.at[j])
            for j, (src, dst) in enumerate(((gate_hbm, g), (up_hbm, u), (down_hbm, d)))
        ]
        for copy in copies:
            copy.start()
        for copy in copies:
            copy.wait()
        out[0:64, 0:H] = g[...].astype(BF16)
        out[0:64, H:] = u[...].astype(BF16)
        out[64:80, :] = d[:, : D // 2].astype(BF16)
        out[80:96, :] = d[:, D // 2 :].astype(BF16)

    return pl.pallas_call(
        body,
        name="pack",
        out_shape=struct((96, 1024), BF16),
        in_specs=[pl.BlockSpec(memory_space=pltpu.HBM)] * 3 + [vmem()],
        out_specs=vmem(),
        scratch_shapes=[
            pltpu.VMEM((64, H), F32),
            pltpu.VMEM((64, H), F32),
            pltpu.VMEM((16, D), F32),
            pltpu.SemaphoreType.DMA((3,)),
        ],
        compiler_params=pltpu.CompilerParams(vmem_limit_bytes=8 * MIB),
        cost_estimate=pl.CostEstimate(flops=2**17, bytes_accessed=MIB, transcendentals=0),
    )(gate, up, down, pool)


def along(turn, step):
    def to(i):
        x, z, c = i // 8, i // 2 % 4, i % 2
        return x * 8 + (z + step) % 4 * 2 + c if c == turn else (x + step) % 4 * 8 + z * 2 + c

    return to


def spread(block, turn):
    return [shift(block, "dp", along(turn, k)) for k in (1, 2, 3)]


def place(turn):
    at = lax.axis_index("dp")
    x, z, c = at // 8, lax.rem(at // 2, 4), lax.rem(at, 2)
    return c, jnp.where(c == turn, z, x)


def bundle(blocks):
    def body(*refs):
        _, at = place(0)
        for k in range(4):
            refs[4][lax.rem(at + 4 - k, 4)] = refs[k][...]

    return call(body, "bundle", 4, struct((4, 96, 1024), BF16), 2**10, 2 * MIB)(*blocks)


def half_of_weights(bundles):
    def body(*refs):
        c, at = place(1)
        for k in range(4):
            other = lax.rem(at + 4 - k, 4)
            for j in range(4):
                refs[4][jnp.where(c == 0, other * 4 + j, j * 4 + other)] = refs[k][j]

    return call(body, "half_of_weights", 4, struct((N_CHIP, 96, 1024), BF16), 2**10, 6 * MIB)(*bundles)


def whole_weights(own, other):
    def body(a, b, out):
        c = lax.rem(lax.axis_index("dp"), 2)

        @pl.loop(0, N_CHIP)
        def _(q):
            out[2 * q + c] = a[q]
            out[2 * q + 1 - c] = b[q]

    return call(body, "whole_weights", 2, struct((2 * N_CHIP, 96, 1024), BF16), 2**10, 12 * MIB)(own, other)


def local(
    pool_tokens,
    pool_cotangent,
    token_ids,
    route_weights,
    gate_weight,
    up_weight,
    down_weight,
    momentum_gate,
    momentum_up,
    momentum_down,
):
    tie = lax.optimization_barrier

    def picked(k, pool):
        return pick_rows(ids[k : k + 1], [pool])[0]

    ids = [token_ids] + [around_y(token_ids, N_EXPERT - k) for k in (1, 2, 3)]
    packed = pack(gate_weight[0], up_weight[0], down_weight[0], pool_tokens)
    x, c = [None] * 4, [None] * 4
    x[1], x[3] = picked(1, pool_tokens), picked(3, pool_tokens)
    packed, x[1], x[3] = tie((packed, x[1], x[3]))

    x[1], x[3] = around_y(x[1], 1), around_y(x[3], 3)
    blocks = spread(packed, 0)
    x[2], c[2] = picked(2, pool_tokens), picked(2, pool_cotangent)
    x[0], c[0] = pick_rows(ids[:1], [pool_tokens, pool_cotangent])
    blocks, x, c[2], c[0] = tie((blocks, x, c[2], c[0]))

    x[2], c[2] = around_y(x[2], 2), around_y(c[2], 2)
    block = bundle((packed, *blocks))
    blocks = spread(block, 1)
    c[1], c[3] = picked(1, pool_cotangent), picked(3, pool_cotangent)
    blocks, x, c = tie((blocks, x, c))

    c[1], c[3] = around_y(c[1], 1), around_y(c[3], 3)
    mine = half_of_weights((block, *blocks))
    weights = whole_weights(mine, other_core(mine))
    tokens, cots = x, c

    hidden_t, gate_factor, act, xt = forward(tokens, weights)
    keep, send, both = backward(cots, route_weights, hidden_t, gate_factor, act, xt, weights)
    received = other_core(send)
    slots = slot_gradients(both, weights)
    back = [slots[0]] + [around_y(slots[k], N_EXPERT - k) for k in (1, 2, 3)]
    received, _ = lax.optimization_barrier((received, slots))

    mine = pair_moments(keep, received)
    merged = pair_merge(keep, received, mine, other_core(mine))
    groups = [[2 * q + c for q in range(N_CHIP)] for c in range(2)]
    parts = lax.all_to_all(merged, "dp", 0, 0, tiled=True, axis_index_groups=groups)
    pool_grad = scatter_rows(ids, back)
    parts, pool_grad = lax.optimization_barrier((parts, pool_grad))
    products = sum_dp(gram(parts))
    outs = finish(
        parts,
        products,
        gate_weight[0],
        up_weight[0],
        down_weight[0],
        momentum_gate[0],
        momentum_up[0],
        momentum_down[0],
    )
    return (*(a[None] for a in outs), pool_grad)


def solution(mesh):
    in_specs = (
        P("dp", "expert"),
        P("dp", "expert"),
        P("expert", "dp"),
        P("expert", "dp"),
        P("expert", "dp", None),
        P("expert", "dp", None),
        P("expert", "dp", None),
        P("expert", "dp", None),
        P("expert", "dp", None),
        P("expert", "dp", None),
    )
    out_specs = (
        P("expert", "dp", None),
        P("expert", "dp", None),
        P("expert", "dp", None),
        P("expert", "dp", None),
        P("expert", "dp", None),
        P("expert", "dp", None),
        P("dp", "expert"),
    )
    return jax.shard_map(local, mesh=mesh, in_specs=in_specs, out_specs=out_specs, check_vma=False)
```

```python
import jax
import jax.numpy as jnp
from jax import lax
from jax.experimental import pallas as pl
from jax.experimental.pallas import tpu as pltpu
from jax.sharding import PartitionSpec as P

TOK_DEV = 512
POOL = 2048
D = 2048
H = 512
N_EXPERT = 4
N_CHIP = 16
SLICE = 512
ROWS = 192

momentum_decay = 0.9
learning_rate = 0.05
epsilon = 1e-06

MIB = 1 << 20
F32 = jnp.float32
BF16 = jnp.bfloat16
NT = (((1,), (1,)), ((), ()))


def vmem():
    return pl.BlockSpec(memory_space=pltpu.VMEM)


def call(body, name, n_in, out_shapes, flops, nbytes, scratch=(), limit=20):
    return pl.pallas_call(
        body,
        name=name,
        out_shape=out_shapes,
        in_specs=[vmem()] * n_in,
        out_specs=jax.tree.map(lambda _: vmem(), out_shapes),
        scratch_shapes=list(scratch),
        compiler_params=pltpu.CompilerParams(vmem_limit_bytes=limit * MIB),
        cost_estimate=pl.CostEstimate(flops=flops, bytes_accessed=nbytes, transcendentals=0),
    )


def struct(shape, dtype):
    return jax.ShapeDtypeStruct(shape, dtype)


def column(row):
    return jnp.broadcast_to(row, (128, row.shape[1])).T


def pick_rows(ids_rows, pools):
    n_ids, n_pool = len(ids_rows), len(pools)

    def body(*refs):
        ids, src = refs[:n_ids], refs[n_ids : n_ids + n_pool]
        out, hot = refs[n_ids + n_pool : -1], refs[-1]
        lane = lax.broadcasted_iota(jnp.int32, (TOK_DEV, 128), 1)
        for k in range(n_ids):
            named = column(ids[k][...])
            for j in range(POOL // 128):
                hot[:, 128 * j : 128 * (j + 1)] = jnp.where(named == lane + 128 * j, 1.0, 0.0).astype(BF16)
            for a in range(n_pool):
                rows = jnp.dot(hot[...], src[a][...], preferred_element_type=F32)
                out[k * n_pool + a][...] = rows.astype(BF16)

    shapes = [struct((TOK_DEV, SLICE), BF16)] * (n_ids * n_pool)
    return call(
        body,
        "pick_rows",
        n_ids + n_pool,
        shapes,
        2 * TOK_DEV * POOL * SLICE * n_ids * n_pool,
        (4 + 2 * n_ids) * MIB // 2,
        [pltpu.VMEM((TOK_DEV, POOL), BF16)],
    )(*ids_rows, *pools)


def slice_of(k):
    me = lax.axis_index("expert")
    return lax.rem(me + N_EXPERT - k, N_EXPERT)


def in_up_block(w, s):
    return w[pl.ds(pl.multiple_of(8 * s, 8), 8), 0:64, :].reshape(SLICE, 2 * H)


def down_block(w, s):
    row = pl.multiple_of(64 + 16 * (s // 2), 16)
    col = pl.multiple_of(SLICE * (s % 2), SLICE)
    return w[:, pl.ds(row, 16), pl.ds(col, SLICE)].reshape(H, SLICE)


def forward(tokens, weights):
    def body(x0, x1, x2, x3, w, hidden_t, gate_factor, act_out, xt, acc, hid):
        for k, x in enumerate((x0, x1, x2, x3)):
            part = jnp.dot(x[...], in_up_block(w, slice_of(k)), preferred_element_type=F32)
            if k == 0:
                acc[...] = part
            else:
                acc[...] += part
            xt[k] = x[...].T

        @pl.loop(0, TOK_DEV // 64)
        def _(i):
            rows = pl.ds(pl.multiple_of(i * 64, 64), 64)
            gate, up = acc[rows, :H], acc[rows, H:]
            sig = jax.nn.sigmoid(gate)
            act = gate * sig
            hid[rows, :] = (act * up).astype(BF16)
            gate_factor[rows, :] = up * sig * (1.0 + gate * (1.0 - sig))
            act_out[rows, :] = act

        hidden_t[...] = hid[...].T

    shapes = [
        struct((H, TOK_DEV), BF16),
        struct((TOK_DEV, H), F32),
        struct((TOK_DEV, H), F32),
        struct((N_EXPERT, SLICE, TOK_DEV), BF16),
    ]
    return call(
        body,
        "forward",
        5,
        shapes,
        2 * TOK_DEV * D * 2 * H,
        10 * MIB,
        [pltpu.VMEM((TOK_DEV, 2 * H), F32), pltpu.VMEM((TOK_DEV, H), BF16)],
    )(*tokens, weights)


def backward(cots, route, hidden_t, gate_factor, act, xt, weights):
    def body(c0, c1, c2, c3, route_ref, hid_t, factor, act_ref, xt_ref, w, keep, send, both, hg, scaled):
        first = lax.axis_index("dp") % 2 == 0
        scale = column(route_ref[...])
        for k, c in enumerate((c0, c1, c2, c3)):
            s = slice_of(k)
            for j in range(SLICE // 128):
                cols = slice(128 * j, 128 * (j + 1))
                scaled[:, cols] = (scale * c[:, cols].astype(F32)).astype(BF16)
            part = lax.dot_general(scaled[...], down_block(w, s), NT, preferred_element_type=F32)
            if k == 0:
                hg[...] = part
            else:
                hg[...] += part
            down = jnp.dot(hid_t[...], scaled[...], preferred_element_type=F32) / TOK_DEV
            down = down.astype(BF16).reshape(N_CHIP, 2, 16, SLICE)
            rows = pl.ds(pl.multiple_of(128 + 16 * s, 16), 16)
            keep[:, rows, :] = jnp.where(first, down[:, 0], down[:, 1])
            send[:, rows, :] = jnp.where(first, down[:, 1], down[:, 0])

        @pl.loop(0, TOK_DEV // 64)
        def _(i):
            rows = pl.ds(pl.multiple_of(i * 64, 64), 64)
            g = hg[rows, :]
            both[rows, :H] = (g * factor[rows, :]).astype(BF16)
            both[rows, H:] = (g * act_ref[rows, :]).astype(BF16)

        for k in range(N_EXPERT):
            chips = pl.ds(pl.multiple_of(4 * slice_of(k), 4), 4)
            grad = jnp.dot(xt_ref[k], both[...], preferred_element_type=F32) / TOK_DEV
            grad = grad.astype(BF16).reshape(4, 2, 64, 2 * H)
            for a in range(2):
                own = grad[:, 0, :, a * H : (a + 1) * H]
                other = grad[:, 1, :, a * H : (a + 1) * H]
                keep[chips, 64 * a : 64 * (a + 1), :] = jnp.where(first, own, other)
                send[chips, 64 * a : 64 * (a + 1), :] = jnp.where(first, other, own)

    shapes = [
        struct((N_CHIP, ROWS, SLICE), BF16),
        struct((N_CHIP, ROWS, SLICE), BF16),
        struct((TOK_DEV, 2 * H), BF16),
    ]
    return call(
        body,
        "backward",
        10,
        shapes,
        8 * TOK_DEV * D * H,
        20 * MIB,
        [pltpu.VMEM((TOK_DEV, H), F32), pltpu.VMEM((TOK_DEV, SLICE), BF16)],
    )(*cots, route, hidden_t, gate_factor, act, xt, weights)


def slot_gradients(both, weights):
    def body(both_ref, w, *out):
        for k in (2, 1, 3, 0):
            grad = lax.dot_general(both_ref[...], in_up_block(w, slice_of(k)), NT, preferred_element_type=F32)
            out[k][...] = grad.astype(BF16)

    shapes = [struct((TOK_DEV, SLICE), BF16)] * N_EXPERT
    return call(body, "slot_gradients", 2, shapes, 4 * TOK_DEV * D * H, 9 * MIB)(both, weights)


def pair_moments(own, other):
    def body(a_ref, b_ref, out):
        def step(q, sums):
            new = []
            for m in range(3):
                a = a_ref[q, 64 * m : 64 * (m + 1), :].astype(F32)
                b = b_ref[q, 64 * m : 64 * (m + 1), :].astype(F32)
                for t in (a * b, a * a, b * b):
                    t = jnp.sum(t.reshape(8, 8, SLICE), axis=0)
                    new.append(t[:, :128] + t[:, 128:256] + t[:, 256:384] + t[:, 384:])
            return tuple(s + n for s, n in zip(sums, new))

        sums = lax.fori_loop(0, N_CHIP, step, (jnp.zeros((8, 128), F32),) * 9)
        for j in range(9):
            out[j] = sums[j]

    return call(body, "pair_moments", 2, struct((9, 8, 128), F32), 9 * 2**20, 6 * MIB)(own, other)


def pair_merge(own, other, mine, theirs):
    step = 4

    def body(a_ref, b_ref, m_ref, t_ref, out):
        coefs = []
        for m in range(3):
            inner = jnp.sum(m_ref[3 * m] + t_ref[3 * m], keepdims=True)
            norm_a = jnp.sum(m_ref[3 * m + 1] + t_ref[3 * m + 2], keepdims=True)
            norm_b = jnp.sum(m_ref[3 * m + 2] + t_ref[3 * m + 1], keepdims=True)
            coef_a = 1.0 - inner / (2.0 * (norm_a + epsilon))
            coef_b = 1.0 - inner / (2.0 * (norm_b + epsilon))
            coefs.append((jnp.broadcast_to(coef_a, (64, SLICE)), jnp.broadcast_to(coef_b, (64, SLICE))))

        for i in range(step):
            q = pl.program_id(0) * step + i
            for m in range(3):
                rows = slice(64 * m, 64 * (m + 1))
                a, b = a_ref[q, rows, :].astype(F32), b_ref[q, rows, :].astype(F32)
                out[i, rows, :] = (coefs[m][0] * a + coefs[m][1] * b).astype(BF16)

    return pl.pallas_call(
        body,
        name="pair_merge",
        grid=(N_CHIP // step,),
        out_shape=struct((N_CHIP, ROWS, SLICE), BF16),
        in_specs=[vmem()] * 4,
        out_specs=pl.BlockSpec((step, ROWS, SLICE), lambda i: (i, 0, 0)),
        compiler_params=pltpu.CompilerParams(vmem_limit_bytes=20 * MIB),
        cost_estimate=pl.CostEstimate(flops=9 * 2**20, bytes_accessed=9 * MIB, transcendentals=0),
    )(own, other, mine, theirs)


def gram(parts):
    def body(x, out):
        row = lax.broadcasted_iota(jnp.int32, (256, 256), 0)
        col = lax.broadcasted_iota(jnp.int32, (256, 256), 1)
        same = jnp.where(row % 16 == col % 16, 1.0, 0.0)
        fold = lax.broadcasted_iota(jnp.int32, (256, 128), 0) // 16
        fold = jnp.where(fold == lax.broadcasted_iota(jnp.int32, (256, 128), 1), 1.0, 0.0)
        for m in range(3):
            acc = None
            for b in range(4):
                at = 64 * m + 16 * b
                block = x[:, at : at + 16, :].reshape(256, SLICE)
                part = lax.dot_general(block, block, NT, preferred_element_type=F32)
                acc = part if acc is None else acc + part
            acc = jnp.sum((acc * same).reshape(16, 16, 256), axis=1)
            out[m] = jnp.dot(acc, fold, precision=lax.Precision.HIGHEST, preferred_element_type=F32)

    return call(body, "gram", 1, struct((3, 16, 128), F32), 12 * 2 * 256 * 256 * 512, 3 * MIB)(parts)


def finish(parts, products, gate, up, down, mom_gate, mom_up, mom_down):
    def body(x, g_ref, gate_w, up_w, down_w, gate_m, up_m, down_m, new_g, new_u, new_d, next_g, next_u, next_d):
        g = g_ref[...]
        i = lax.broadcasted_iota(jnp.int32, (3, 16, 128), 1)
        j = lax.broadcasted_iota(jnp.int32, (3, 16, 128), 2)
        c_col = jnp.ones((3, 16, 1), F32)
        c_row = jnp.ones((3, 1, 128), F32)
        for level in range(4):
            block_i, block_j = i >> level, j >> level
            same, sibling = block_i == block_j, (block_i ^ 1) == block_j
            weighted = g * c_col * c_row
            within = jnp.where(same, weighted, 0.0)
            across = jnp.where(sibling, weighted, 0.0)

            def coef(axis):
                norm = jnp.sum(jnp.where(same, jnp.sum(within, axis=3 - axis, keepdims=True), 0.0), axis=axis, keepdims=True)
                inner = jnp.sum(jnp.where(same, jnp.sum(across, axis=3 - axis, keepdims=True), 0.0), axis=axis, keepdims=True)
                return 1.0 - inner / (2.0 * (jnp.maximum(norm, 0.0) + epsilon))

            c_col, c_row = c_col * coef(2), c_row * coef(1)
        olds = ((gate_w, gate_m, new_g, next_g), (up_w, up_m, new_u, next_u))
        for m in range(3):
            merged = jnp.zeros((64, SLICE), F32)
            for q in range(16):
                scale = jnp.broadcast_to(c_col[m, q : q + 1, :], (64, SLICE))
                merged += scale * x[q, 64 * m : 64 * (m + 1), :].astype(F32)
            if m < 2:
                w, mom, new, after = olds[m]
                step = momentum_decay * mom[...] + merged
                after[...] = step
                new[...] = w[...] - learning_rate * step
            else:
                for k in range(4):
                    cols = slice(SLICE * k, SLICE * (k + 1))
                    step = momentum_decay * down_m[:, cols] + merged[16 * k : 16 * (k + 1), :]
                    next_d[:, cols] = step
                    new_d[:, cols] = down_w[:, cols] - learning_rate * step

    wide, tall = struct((64, H), F32), struct((16, D), F32)
    return call(body, "finish", 8, [wide, wide, tall, wide, wide, tall], 2**22, 6 * MIB)(
        parts, products, gate, up, down, mom_gate, mom_up, mom_down
    )


def scatter_rows(ids_rows, grads):
    block = 512

    def body(i0, i1, i2, i3, g0, g1, g2, g3, out):
        row = lax.broadcasted_iota(jnp.int32, (block, TOK_DEV), 0) + block * pl.program_id(0)
        acc = None
        for ids, g in zip((i0, i1, i2, i3), (g0, g1, g2, g3)):
            hot = jnp.where(jnp.broadcast_to(ids[...], row.shape) == row, 1.0, 0.0).astype(BF16)
            part = jnp.dot(hot, g[...], preferred_element_type=F32)
            acc = part if acc is None else acc + part
        out[...] = acc

    return pl.pallas_call(
        body,
        name="scatter_rows",
        grid=(POOL // block,),
        out_shape=struct((POOL, SLICE), F32),
        in_specs=[vmem()] * 8,
        out_specs=pl.BlockSpec((block, SLICE), lambda i: (i, 0)),
        compiler_params=pltpu.CompilerParams(vmem_limit_bytes=24 * MIB),
        cost_estimate=pl.CostEstimate(
            flops=2 * POOL * POOL * SLICE, bytes_accessed=6 * MIB, transcendentals=0
        ),
    )(*ids_rows, *grads)


def shift(block, axis, to):
    return lax.ppermute(block, axis, [(i, to(i)) for i in range(lax.axis_size(axis))])


def around_y(block, k):
    return shift(block, "expert", lambda i: (i + k) % N_EXPERT)


def around_z(block, k):
    return shift(block, "dp", lambda i: i // 8 * 8 + (i // 2 % 4 + k) % 4 * 2 + i % 2)


def around_x(block, k):
    return shift(block, "dp", lambda i: (i // 8 + k) % 4 * 8 + i % 8)


def other_core(block):
    return shift(block, "dp", lambda i: i ^ 1)


def sum_dp(value):
    for around in (around_z, around_x):
        value = value + sum(around(value, k) for k in (2, 1, 3))
    return value + other_core(value)


def pack(gate, up, down):
    def body(gate_hbm, up_hbm, down_hbm, out, g, u, d, sems):
        copies = [
            pltpu.make_async_copy(src, dst, sems.at[j])
            for j, (src, dst) in enumerate(((gate_hbm, g), (up_hbm, u), (down_hbm, d)))
        ]
        for copy in copies:
            copy.start()
        for copy in copies:
            copy.wait()
        out[0:64, 0:H] = g[...].astype(BF16)
        out[0:64, H:] = u[...].astype(BF16)
        out[64:80, :] = d[:, : D // 2].astype(BF16)
        out[80:96, :] = d[:, D // 2 :].astype(BF16)

    return pl.pallas_call(
        body,
        name="pack",
        out_shape=struct((96, 1024), BF16),
        in_specs=[pl.BlockSpec(memory_space=pl.ANY)] * 3,
        out_specs=vmem(),
        scratch_shapes=[
            pltpu.VMEM((64, H), F32),
            pltpu.VMEM((64, H), F32),
            pltpu.VMEM((16, D), F32),
            pltpu.SemaphoreType.DMA((3,)),
        ],
        compiler_params=pltpu.CompilerParams(vmem_limit_bytes=8 * MIB),
        cost_estimate=pl.CostEstimate(flops=2**17, bytes_accessed=MIB, transcendentals=0),
    )(gate, up, down)


def along(turn, step):
    def to(i):
        x, z, c = i // 8, i // 2 % 4, i % 2
        return x * 8 + (z + step) % 4 * 2 + c if c == turn else (x + step) % 4 * 8 + z * 2 + c

    return to


def spread(block, turn):
    return [shift(block, "dp", along(turn, k)) for k in (1, 2, 3)]


def place(turn):
    at = lax.axis_index("dp")
    x, z, c = at // 8, lax.rem(at // 2, 4), lax.rem(at, 2)
    return c, jnp.where(c == turn, z, x)


def bundle(blocks):
    def body(*refs):
        _, at = place(0)
        for k in range(4):
            refs[4][lax.rem(at + 4 - k, 4)] = refs[k][...]

    return call(body, "bundle", 4, struct((4, 96, 1024), BF16), 2**10, 2 * MIB)(*blocks)


def half_of_weights(bundles):
    def body(*refs):
        c, at = place(1)
        for k in range(4):
            other = lax.rem(at + 4 - k, 4)
            for j in range(4):
                refs[4][jnp.where(c == 0, other * 4 + j, j * 4 + other)] = refs[k][j]

    return call(body, "half_of_weights", 4, struct((N_CHIP, 96, 1024), BF16), 2**10, 6 * MIB)(*bundles)


def whole_weights(own, other):
    def body(a, b, out):
        c = lax.rem(lax.axis_index("dp"), 2)

        @pl.loop(0, N_CHIP)
        def _(q):
            out[2 * q + c] = a[q]
            out[2 * q + 1 - c] = b[q]

    return call(body, "whole_weights", 2, struct((2 * N_CHIP, 96, 1024), BF16), 2**10, 12 * MIB)(own, other)


def local(
    pool_tokens,
    pool_cotangent,
    token_ids,
    route_weights,
    gate_weight,
    up_weight,
    down_weight,
    momentum_gate,
    momentum_up,
    momentum_down,
):
    tie = lax.optimization_barrier

    def picked(k, pool):
        return pick_rows(ids[k : k + 1], [pool])[0]

    ids = [token_ids] + [around_y(token_ids, N_EXPERT - k) for k in (1, 2, 3)]
    packed = pack(gate_weight[0], up_weight[0], down_weight[0])
    x, c = [None] * 4, [None] * 4
    x[1], x[3] = picked(1, pool_tokens), picked(3, pool_tokens)
    ids, packed, x[1], x[3] = tie((ids, packed, x[1], x[3]))

    blocks = spread(packed, 0)
    x[1], x[3] = around_y(x[1], 1), around_y(x[3], 3)
    x[2], c[2] = picked(2, pool_tokens), picked(2, pool_cotangent)
    ids, blocks, x[1:], c[2] = tie((ids, blocks, x[1:], c[2]))

    block = bundle((packed, *blocks))
    blocks = spread(block, 1)
    x[2], c[2] = around_y(x[2], 2), around_y(c[2], 2)
    c[1], c[3] = picked(1, pool_cotangent), picked(3, pool_cotangent)
    x[0], c[0] = pick_rows(ids[:1], [pool_tokens, pool_cotangent])
    blocks, x, c = tie((blocks, x, c))

    mine = half_of_weights((block, *blocks))
    weights = whole_weights(mine, other_core(mine))
    c[1], c[3] = around_y(c[1], 1), around_y(c[3], 3)
    tokens, cots = x, c

    hidden_t, gate_factor, act, xt = forward(tokens, weights)
    keep, send, both = backward(cots, route_weights, hidden_t, gate_factor, act, xt, weights)
    received = other_core(send)
    slots = slot_gradients(both, weights)
    back = [slots[0]] + [around_y(slots[k], N_EXPERT - k) for k in (1, 2, 3)]
    received, _ = lax.optimization_barrier((received, slots))

    mine = pair_moments(keep, received)
    merged = pair_merge(keep, received, mine, other_core(mine))
    merged = pltpu.with_memory_space_constraint(merged, pltpu.HBM)
    groups = [[2 * q + c for q in range(N_CHIP)] for c in range(2)]
    parts = lax.all_to_all(merged, "dp", 0, 0, tiled=True, axis_index_groups=groups)
    pool_grad = scatter_rows(ids, back)
    parts, pool_grad = lax.optimization_barrier((parts, pool_grad))
    products = sum_dp(gram(parts))
    outs = finish(
        parts,
        products,
        gate_weight[0],
        up_weight[0],
        down_weight[0],
        momentum_gate[0],
        momentum_up[0],
        momentum_down[0],
    )
    return (*(a[None] for a in outs), pool_grad)


def solution(mesh):
    in_specs = (
        P("dp", "expert"),
        P("dp", "expert"),
        P("expert", "dp"),
        P("expert", "dp"),
        P("expert", "dp", None),
        P("expert", "dp", None),
        P("expert", "dp", None),
        P("expert", "dp", None),
        P("expert", "dp", None),
        P("expert", "dp", None),
    )
    out_specs = (
        P("expert", "dp", None),
        P("expert", "dp", None),
        P("expert", "dp", None),
        P("expert", "dp", None),
        P("expert", "dp", None),
        P("expert", "dp", None),
        P("dp", "expert"),
    )
    return jax.shard_map(local, mesh=mesh, in_specs=in_specs, out_specs=out_specs, check_vma=False)
```

```python
import jax
import jax.numpy as jnp
from jax import lax
from jax.experimental import pallas as pl
from jax.experimental.pallas import tpu as pltpu
from jax.sharding import PartitionSpec as P

TOK_DEV = 512
POOL = 2048
D = 2048
H = 512
N_EXPERT = 4
N_CHIP = 16
SLICE = 512
ROWS = 192

momentum_decay = 0.9
learning_rate = 0.05
epsilon = 1e-06

MIB = 1 << 20
F32 = jnp.float32
BF16 = jnp.bfloat16
NT = (((1,), (1,)), ((), ()))


def vmem():
    return pl.BlockSpec(memory_space=pltpu.VMEM)


def call(body, name, n_in, out_shapes, flops, nbytes, scratch=(), limit=20):
    return pl.pallas_call(
        body,
        name=name,
        out_shape=out_shapes,
        in_specs=[vmem()] * n_in,
        out_specs=jax.tree.map(lambda _: vmem(), out_shapes),
        scratch_shapes=list(scratch),
        compiler_params=pltpu.CompilerParams(vmem_limit_bytes=limit * MIB),
        cost_estimate=pl.CostEstimate(flops=flops, bytes_accessed=nbytes, transcendentals=0),
    )


def struct(shape, dtype):
    return jax.ShapeDtypeStruct(shape, dtype)


def column(row):
    return jnp.broadcast_to(row, (128, row.shape[1])).T


def pick_rows(ids_rows, pools):
    n_ids, n_pool = len(ids_rows), len(pools)

    def body(*refs):
        ids, src = refs[:n_ids], refs[n_ids : n_ids + n_pool]
        out, hot = refs[n_ids + n_pool : -1], refs[-1]
        lane = lax.broadcasted_iota(jnp.int32, (TOK_DEV, 128), 1)
        for k in range(n_ids):
            named = column(ids[k][...])
            for j in range(POOL // 128):
                hot[:, 128 * j : 128 * (j + 1)] = jnp.where(named == lane + 128 * j, 1.0, 0.0).astype(BF16)
            for a in range(n_pool):
                rows = jnp.dot(hot[...], src[a][...], preferred_element_type=F32)
                out[k * n_pool + a][...] = rows.astype(BF16)

    shapes = [struct((TOK_DEV, SLICE), BF16)] * (n_ids * n_pool)
    return call(
        body,
        "pick_rows",
        n_ids + n_pool,
        shapes,
        2 * TOK_DEV * POOL * SLICE * n_ids * n_pool,
        (4 + 2 * n_ids) * MIB // 2,
        [pltpu.VMEM((TOK_DEV, POOL), BF16)],
    )(*ids_rows, *pools)


def slice_of(k):
    me = lax.axis_index("expert")
    return lax.rem(me + N_EXPERT - k, N_EXPERT)


def in_up_block(w, s):
    return w[pl.ds(pl.multiple_of(8 * s, 8), 8), 0:64, :].reshape(SLICE, 2 * H)


def down_block(w, s):
    row = pl.multiple_of(64 + 16 * (s // 2), 16)
    col = pl.multiple_of(SLICE * (s % 2), SLICE)
    return w[:, pl.ds(row, 16), pl.ds(col, SLICE)].reshape(H, SLICE)


def forward(tokens, weights):
    def body(x0, x1, x2, x3, w, hidden_t, gate_factor, act_out, xt, acc, hid):
        for k, x in enumerate((x0, x1, x2, x3)):
            part = jnp.dot(x[...], in_up_block(w, slice_of(k)), preferred_element_type=F32)
            if k == 0:
                acc[...] = part
            else:
                acc[...] += part
            xt[k] = x[...].T

        @pl.loop(0, TOK_DEV // 64)
        def _(i):
            rows = pl.ds(pl.multiple_of(i * 64, 64), 64)
            gate, up = acc[rows, :H], acc[rows, H:]
            sig = jax.nn.sigmoid(gate)
            act = gate * sig
            hid[rows, :] = (act * up).astype(BF16)
            gate_factor[rows, :] = up * sig * (1.0 + gate * (1.0 - sig))
            act_out[rows, :] = act

        hidden_t[...] = hid[...].T

    shapes = [
        struct((H, TOK_DEV), BF16),
        struct((TOK_DEV, H), F32),
        struct((TOK_DEV, H), F32),
        struct((N_EXPERT, SLICE, TOK_DEV), BF16),
    ]
    return call(
        body,
        "forward",
        5,
        shapes,
        2 * TOK_DEV * D * 2 * H,
        10 * MIB,
        [pltpu.VMEM((TOK_DEV, 2 * H), F32), pltpu.VMEM((TOK_DEV, H), BF16)],
    )(*tokens, weights)


def backward(cots, route, hidden_t, gate_factor, act, xt, weights):
    def body(c0, c1, c2, c3, route_ref, hid_t, factor, act_ref, xt_ref, w, keep, send, both, hg, scaled):
        first = lax.axis_index("dp") % 2 == 0
        scale = column(route_ref[...])
        for k, c in enumerate((c0, c1, c2, c3)):
            s = slice_of(k)
            for j in range(SLICE // 128):
                cols = slice(128 * j, 128 * (j + 1))
                scaled[:, cols] = (scale * c[:, cols].astype(F32)).astype(BF16)
            part = lax.dot_general(scaled[...], down_block(w, s), NT, preferred_element_type=F32)
            if k == 0:
                hg[...] = part
            else:
                hg[...] += part
            down = jnp.dot(hid_t[...], scaled[...], preferred_element_type=F32) / TOK_DEV
            down = down.astype(BF16).reshape(N_CHIP, 2, 16, SLICE)
            rows = pl.ds(pl.multiple_of(128 + 16 * s, 16), 16)
            keep[:, rows, :] = jnp.where(first, down[:, 0], down[:, 1])
            send[:, rows, :] = jnp.where(first, down[:, 1], down[:, 0])

        @pl.loop(0, TOK_DEV // 64)
        def _(i):
            rows = pl.ds(pl.multiple_of(i * 64, 64), 64)
            g = hg[rows, :]
            both[rows, :H] = (g * factor[rows, :]).astype(BF16)
            both[rows, H:] = (g * act_ref[rows, :]).astype(BF16)

        for k in range(N_EXPERT):
            chips = pl.ds(pl.multiple_of(4 * slice_of(k), 4), 4)
            grad = jnp.dot(xt_ref[k], both[...], preferred_element_type=F32) / TOK_DEV
            grad = grad.astype(BF16).reshape(4, 2, 64, 2 * H)
            for a in range(2):
                own = grad[:, 0, :, a * H : (a + 1) * H]
                other = grad[:, 1, :, a * H : (a + 1) * H]
                keep[chips, 64 * a : 64 * (a + 1), :] = jnp.where(first, own, other)
                send[chips, 64 * a : 64 * (a + 1), :] = jnp.where(first, other, own)

    shapes = [
        struct((N_CHIP, ROWS, SLICE), BF16),
        struct((N_CHIP, ROWS, SLICE), BF16),
        struct((TOK_DEV, 2 * H), BF16),
    ]
    return call(
        body,
        "backward",
        10,
        shapes,
        8 * TOK_DEV * D * H,
        20 * MIB,
        [pltpu.VMEM((TOK_DEV, H), F32), pltpu.VMEM((TOK_DEV, SLICE), BF16)],
    )(*cots, route, hidden_t, gate_factor, act, xt, weights)


def slot_gradients(both, weights):
    def body(both_ref, w, *out):
        for k in (2, 1, 3, 0):
            grad = lax.dot_general(both_ref[...], in_up_block(w, slice_of(k)), NT, preferred_element_type=F32)
            out[k][...] = grad.astype(BF16)

    shapes = [struct((TOK_DEV, SLICE), BF16)] * N_EXPERT
    return call(body, "slot_gradients", 2, shapes, 4 * TOK_DEV * D * H, 9 * MIB)(both, weights)


def pair_moments(own, other):
    def body(a_ref, b_ref, out):
        def step(q, sums):
            new = []
            for m in range(3):
                a = a_ref[q, 64 * m : 64 * (m + 1), :].astype(F32)
                b = b_ref[q, 64 * m : 64 * (m + 1), :].astype(F32)
                for t in (a * b, a * a, b * b):
                    t = jnp.sum(t.reshape(8, 8, SLICE), axis=0)
                    new.append(t[:, :128] + t[:, 128:256] + t[:, 256:384] + t[:, 384:])
            return tuple(s + n for s, n in zip(sums, new))

        sums = lax.fori_loop(0, N_CHIP, step, (jnp.zeros((8, 128), F32),) * 9)
        for j in range(9):
            out[j] = sums[j]

    return call(body, "pair_moments", 2, struct((9, 8, 128), F32), 9 * 2**20, 6 * MIB)(own, other)


def pair_merge(own, other, mine, theirs):
    def body(a_ref, b_ref, m_ref, t_ref, *out):
        coefs = []
        for m in range(3):
            inner = jnp.sum(m_ref[3 * m] + t_ref[3 * m], keepdims=True)
            norm_a = jnp.sum(m_ref[3 * m + 1] + t_ref[3 * m + 2], keepdims=True)
            norm_b = jnp.sum(m_ref[3 * m + 2] + t_ref[3 * m + 1], keepdims=True)
            coef_a = 1.0 - inner / (2.0 * (norm_a + epsilon))
            coef_b = 1.0 - inner / (2.0 * (norm_b + epsilon))
            coefs.append((jnp.broadcast_to(coef_a, (64, SLICE)), jnp.broadcast_to(coef_b, (64, SLICE))))
        c, at = place(0)

        @pl.loop(0, 4)
        def _(j):
            for k in range(4):
                first = lax.rem(at + k, 4)
                q = jnp.where(c == 0, 4 * j + first, 4 * first + j)
                for m in range(3):
                    rows = slice(64 * m, 64 * (m + 1))
                    a, b = a_ref[q, rows, :].astype(F32), b_ref[q, rows, :].astype(F32)
                    out[k][j, rows, :] = (coefs[m][0] * a + coefs[m][1] * b).astype(BF16)

    return call(body, "pair_merge", 4, [struct((4, ROWS, SLICE), BF16)] * 4, 9 * 2**20, 9 * MIB)(
        own, other, mine, theirs
    )


def turn_over(parts):
    def body(*refs):
        (_, first), (_, second) = place(0), place(1)
        for k in range(4):
            for m in range(4):
                refs[4 + k][lax.rem(first + 4 - m, 4)] = refs[m][lax.rem(second + k, 4)]

    return call(body, "turn_over", 4, [struct((4, ROWS, SLICE), BF16)] * 4, 2**10, 6 * MIB)(*parts)


def origin(index):
    c, second = place(1)
    other = (second + 4 - (index >> 2)) & 3
    return jnp.where(c == 0, other * 4 + (index & 3), (index & 3) * 4 + other)


def gram(parts):
    def body(*refs):
        x, out = refs[:4], refs[4]
        row = lax.broadcasted_iota(jnp.int32, (256, 256), 0)
        col = lax.broadcasted_iota(jnp.int32, (256, 256), 1)
        same = jnp.where(row % 16 == col % 16, 1.0, 0.0)
        fold = origin(lax.broadcasted_iota(jnp.int32, (256, 128), 0) // 16)
        fold = jnp.where(fold == lax.broadcasted_iota(jnp.int32, (256, 128), 1), 1.0, 0.0)
        order = origin(lax.broadcasted_iota(jnp.int32, (16, 16), 1))
        order = jnp.where(order == lax.broadcasted_iota(jnp.int32, (16, 16), 0), 1.0, 0.0)
        exact = dict(precision=lax.Precision.HIGHEST, preferred_element_type=F32)
        for m in range(3):
            acc = None
            for b in range(4):
                at = 64 * m + 16 * b
                block = jnp.concatenate([r[:, at : at + 16, :].reshape(64, SLICE) for r in x], axis=0)
                part = lax.dot_general(block, block, NT, preferred_element_type=F32)
                acc = part if acc is None else acc + part
            acc = jnp.sum((acc * same).reshape(16, 16, 256), axis=1)
            out[m] = jnp.dot(order, jnp.dot(acc, fold, **exact), **exact)

    return call(body, "gram", 4, struct((3, 16, 128), F32), 12 * 2 * 256 * 256 * 512, 3 * MIB)(*parts)


def finish(parts, products, gate, up, down, mom_gate, mom_up, mom_down):
    def body(x0, x1, x2, x3, g_ref, gate_w, up_w, down_w, gate_m, up_m, down_m, new_g, new_u, new_d, next_g, next_u, next_d):
        g = g_ref[...]
        i = lax.broadcasted_iota(jnp.int32, (3, 16, 128), 1)
        j = lax.broadcasted_iota(jnp.int32, (3, 16, 128), 2)
        c_col = jnp.ones((3, 16, 1), F32)
        c_row = jnp.ones((3, 1, 128), F32)
        for level in range(4):
            block_i, block_j = i >> level, j >> level
            same, sibling = block_i == block_j, (block_i ^ 1) == block_j
            weighted = g * c_col * c_row
            within = jnp.where(same, weighted, 0.0)
            across = jnp.where(sibling, weighted, 0.0)

            def coef(axis):
                norm = jnp.sum(jnp.where(same, jnp.sum(within, axis=3 - axis, keepdims=True), 0.0), axis=axis, keepdims=True)
                inner = jnp.sum(jnp.where(same, jnp.sum(across, axis=3 - axis, keepdims=True), 0.0), axis=axis, keepdims=True)
                return 1.0 - inner / (2.0 * (jnp.maximum(norm, 0.0) + epsilon))

            c_col, c_row = c_col * coef(2), c_row * coef(1)
        chip = origin(lax.broadcasted_iota(jnp.int32, (16, 128), 0))
        chip = chip == lax.broadcasted_iota(jnp.int32, (16, 128), 1)
        c_col = jnp.sum(jnp.where(chip, c_row, 0.0), axis=2, keepdims=True)
        olds = ((gate_w, gate_m, new_g, next_g), (up_w, up_m, new_u, next_u))
        for m in range(3):
            merged = jnp.zeros((64, SLICE), F32)
            for q in range(16):
                scale = jnp.broadcast_to(c_col[m, q : q + 1, :], (64, SLICE))
                x = (x0, x1, x2, x3)[q // 4]
                merged += scale * x[q % 4, 64 * m : 64 * (m + 1), :].astype(F32)
            if m < 2:
                w, mom, new, after = olds[m]
                step = momentum_decay * mom[...] + merged
                after[...] = step
                new[...] = w[...] - learning_rate * step
            else:
                for k in range(4):
                    cols = slice(SLICE * k, SLICE * (k + 1))
                    step = momentum_decay * down_m[:, cols] + merged[16 * k : 16 * (k + 1), :]
                    next_d[:, cols] = step
                    new_d[:, cols] = down_w[:, cols] - learning_rate * step

    wide, tall = struct((64, H), F32), struct((16, D), F32)
    return call(body, "finish", 11, [wide, wide, tall, wide, wide, tall], 2**22, 6 * MIB)(
        *parts, products, gate, up, down, mom_gate, mom_up, mom_down
    )


def scatter_rows(ids_rows, grads):
    block = 512

    def body(i0, i1, i2, i3, g0, g1, g2, g3, out):
        row = lax.broadcasted_iota(jnp.int32, (block, TOK_DEV), 0) + block * pl.program_id(0)
        acc = None
        for ids, g in zip((i0, i1, i2, i3), (g0, g1, g2, g3)):
            hot = jnp.where(jnp.broadcast_to(ids[...], row.shape) == row, 1.0, 0.0).astype(BF16)
            part = jnp.dot(hot, g[...], preferred_element_type=F32)
            acc = part if acc is None else acc + part
        out[...] = acc

    return pl.pallas_call(
        body,
        name="scatter_rows",
        grid=(POOL // block,),
        out_shape=struct((POOL, SLICE), F32),
        in_specs=[vmem()] * 8,
        out_specs=pl.BlockSpec((block, SLICE), lambda i: (i, 0)),
        compiler_params=pltpu.CompilerParams(vmem_limit_bytes=24 * MIB),
        cost_estimate=pl.CostEstimate(
            flops=2 * POOL * POOL * SLICE, bytes_accessed=6 * MIB, transcendentals=0
        ),
    )(*ids_rows, *grads)


def shift(block, axis, to):
    return lax.ppermute(block, axis, [(i, to(i)) for i in range(lax.axis_size(axis))])


def around_y(block, k):
    return shift(block, "expert", lambda i: (i + k) % N_EXPERT)


def around_z(block, k):
    return shift(block, "dp", lambda i: i // 8 * 8 + (i // 2 % 4 + k) % 4 * 2 + i % 2)


def around_x(block, k):
    return shift(block, "dp", lambda i: (i // 8 + k) % 4 * 8 + i % 8)


def other_core(block):
    return shift(block, "dp", lambda i: i ^ 1)


def sum_dp(value):
    for around in (around_z, around_x):
        value = value + sum(around(value, k) for k in (2, 1, 3))
    return value + other_core(value)


def pack(gate, up, down):
    def body(gate_hbm, up_hbm, down_hbm, out, g, u, d, sems):
        copies = [
            pltpu.make_async_copy(src, dst, sems.at[j])
            for j, (src, dst) in enumerate(((gate_hbm, g), (up_hbm, u), (down_hbm, d)))
        ]
        for copy in copies:
            copy.start()
        for copy in copies:
            copy.wait()
        out[0:64, 0:H] = g[...].astype(BF16)
        out[0:64, H:] = u[...].astype(BF16)
        out[64:80, :] = d[:, : D // 2].astype(BF16)
        out[80:96, :] = d[:, D // 2 :].astype(BF16)

    return pl.pallas_call(
        body,
        name="pack",
        out_shape=struct((96, 1024), BF16),
        in_specs=[pl.BlockSpec(memory_space=pl.ANY)] * 3,
        out_specs=vmem(),
        scratch_shapes=[
            pltpu.VMEM((64, H), F32),
            pltpu.VMEM((64, H), F32),
            pltpu.VMEM((16, D), F32),
            pltpu.SemaphoreType.DMA((3,)),
        ],
        compiler_params=pltpu.CompilerParams(vmem_limit_bytes=8 * MIB),
        cost_estimate=pl.CostEstimate(flops=2**17, bytes_accessed=MIB, transcendentals=0),
    )(gate, up, down)


def along(turn, step):
    def to(i):
        x, z, c = i // 8, i // 2 % 4, i % 2
        return x * 8 + (z + step) % 4 * 2 + c if c == turn else (x + step) % 4 * 8 + z * 2 + c

    return to


def spread(block, turn):
    return [shift(block, "dp", along(turn, k)) for k in (1, 2, 3)]


def place(turn):
    at = lax.axis_index("dp")
    x, z, c = at // 8, lax.rem(at // 2, 4), lax.rem(at, 2)
    return c, jnp.where(c == turn, z, x)


def bundle(blocks):
    def body(*refs):
        _, at = place(0)
        for k in range(4):
            refs[4][lax.rem(at + 4 - k, 4)] = refs[k][...]

    return call(body, "bundle", 4, struct((4, 96, 1024), BF16), 2**10, 2 * MIB)(*blocks)


def half_of_weights(bundles):
    def body(*refs):
        c, at = place(1)
        for k in range(4):
            other = lax.rem(at + 4 - k, 4)
            for j in range(4):
                refs[4][jnp.where(c == 0, other * 4 + j, j * 4 + other)] = refs[k][j]

    return call(body, "half_of_weights", 4, struct((N_CHIP, 96, 1024), BF16), 2**10, 6 * MIB)(*bundles)


def whole_weights(own, other):
    def body(a, b, out):
        c = lax.rem(lax.axis_index("dp"), 2)

        @pl.loop(0, N_CHIP)
        def _(q):
            out[2 * q + c] = a[q]
            out[2 * q + 1 - c] = b[q]

    return call(body, "whole_weights", 2, struct((2 * N_CHIP, 96, 1024), BF16), 2**10, 12 * MIB)(own, other)


def local(
    pool_tokens,
    pool_cotangent,
    token_ids,
    route_weights,
    gate_weight,
    up_weight,
    down_weight,
    momentum_gate,
    momentum_up,
    momentum_down,
):
    tie = lax.optimization_barrier

    def picked(k, pool):
        return pick_rows(ids[k : k + 1], [pool])[0]

    ids = [token_ids] + [around_y(token_ids, N_EXPERT - k) for k in (1, 2, 3)]
    packed = pack(gate_weight[0], up_weight[0], down_weight[0])
    x, c = [None] * 4, [None] * 4
    x[1], x[3] = picked(1, pool_tokens), picked(3, pool_tokens)
    ids, packed, x[1], x[3] = tie((ids, packed, x[1], x[3]))

    blocks = spread(packed, 0)
    x[1], x[3] = around_y(x[1], 1), around_y(x[3], 3)
    x[2], c[2] = picked(2, pool_tokens), picked(2, pool_cotangent)
    ids, blocks, x[1:], c[2] = tie((ids, blocks, x[1:], c[2]))

    block = bundle((packed, *blocks))
    blocks = spread(block, 1)
    x[2], c[2] = around_y(x[2], 2), around_y(c[2], 2)
    c[1], c[3] = picked(1, pool_cotangent), picked(3, pool_cotangent)
    x[0], c[0] = pick_rows(ids[:1], [pool_tokens, pool_cotangent])
    blocks, x, c = tie((blocks, x, c))

    mine = half_of_weights((block, *blocks))
    weights = whole_weights(mine, other_core(mine))
    c[1], c[3] = around_y(c[1], 1), around_y(c[3], 3)
    tokens, cots = x, c

    hidden_t, gate_factor, act, xt = forward(tokens, weights)
    keep, send, both = backward(cots, route_weights, hidden_t, gate_factor, act, xt, weights)
    received = other_core(send)
    slots = slot_gradients(both, weights)
    received, slots = lax.optimization_barrier((received, slots))

    mine = pair_moments(keep, received)
    sent = pair_merge(keep, received, mine, other_core(mine))
    parts = [sent[0]] + [shift(sent[k], "dp", along(0, k)) for k in (1, 2, 3)]
    back = [slots[0]] + [around_y(slots[k], N_EXPERT - k) for k in (1, 2, 3)]
    parts, back[1], back[3] = tie((parts, back[1], back[3]))
    sent = turn_over(parts)
    parts = [sent[0]] + [shift(sent[k], "dp", along(1, k)) for k in (1, 2, 3)]
    pool_grad = scatter_rows(ids, back)
    parts, pool_grad = tie((parts, pool_grad))
    products = sum_dp(gram(parts))
    outs = finish(
        parts,
        products,
        gate_weight[0],
        up_weight[0],
        down_weight[0],
        momentum_gate[0],
        momentum_up[0],
        momentum_down[0],
    )
    return (*(a[None] for a in outs), pool_grad)


def solution(mesh):
    in_specs = (
        P("dp", "expert"),
        P("dp", "expert"),
        P("expert", "dp"),
        P("expert", "dp"),
        P("expert", "dp", None),
        P("expert", "dp", None),
        P("expert", "dp", None),
        P("expert", "dp", None),
        P("expert", "dp", None),
        P("expert", "dp", None),
    )
    out_specs = (
        P("expert", "dp", None),
        P("expert", "dp", None),
        P("expert", "dp", None),
        P("expert", "dp", None),
        P("expert", "dp", None),
        P("expert", "dp", None),
        P("dp", "expert"),
    )
    return jax.shard_map(local, mesh=mesh, in_specs=in_specs, out_specs=out_specs, check_vma=False)
```

```python
import jax
import jax.numpy as jnp
from jax import lax
from jax.experimental import pallas as pl
from jax.experimental.pallas import tpu as pltpu
from jax.sharding import PartitionSpec as P

TOK_DEV = 512
POOL = 2048
D = 2048
H = 512
N_EXPERT = 4
N_CHIP = 16
SLICE = 512
ROWS = 192

momentum_decay = 0.9
learning_rate = 0.05
epsilon = 1e-06

MIB = 1 << 20
F32 = jnp.float32
BF16 = jnp.bfloat16
NT = (((1,), (1,)), ((), ()))


def vmem():
    return pl.BlockSpec(memory_space=pltpu.VMEM)


def call(body, name, n_in, out_shapes, flops, nbytes, scratch=(), limit=20):
    return pl.pallas_call(
        body,
        name=name,
        out_shape=out_shapes,
        in_specs=[vmem()] * n_in,
        out_specs=jax.tree.map(lambda _: vmem(), out_shapes),
        scratch_shapes=list(scratch),
        compiler_params=pltpu.CompilerParams(vmem_limit_bytes=limit * MIB),
        cost_estimate=pl.CostEstimate(flops=flops, bytes_accessed=nbytes, transcendentals=0),
    )


def struct(shape, dtype):
    return jax.ShapeDtypeStruct(shape, dtype)


def column(row):
    return jnp.broadcast_to(row, (128, row.shape[1])).T


def pick_rows(ids_rows, pools):
    n_ids, n_pool = len(ids_rows), len(pools)

    def body(*refs):
        ids, src = refs[:n_ids], refs[n_ids : n_ids + n_pool]
        out, hot = refs[n_ids + n_pool : -1], refs[-1]
        lane = lax.broadcasted_iota(jnp.int32, (TOK_DEV, 128), 1)
        for k in range(n_ids):
            named = column(ids[k][...])
            for j in range(POOL // 128):
                hot[:, 128 * j : 128 * (j + 1)] = jnp.where(named == lane + 128 * j, 1.0, 0.0).astype(BF16)
            for a in range(n_pool):
                rows = jnp.dot(hot[...], src[a][...], preferred_element_type=F32)
                out[k * n_pool + a][...] = rows.astype(BF16)

    shapes = [struct((TOK_DEV, SLICE), BF16)] * (n_ids * n_pool)
    return call(
        body,
        "pick_rows",
        n_ids + n_pool,
        shapes,
        2 * TOK_DEV * POOL * SLICE * n_ids * n_pool,
        (4 + 2 * n_ids) * MIB // 2,
        [pltpu.VMEM((TOK_DEV, POOL), BF16)],
    )(*ids_rows, *pools)


def slice_of(k):
    me = lax.axis_index("expert")
    return lax.rem(me + N_EXPERT - k, N_EXPERT)


def in_up_block(w, s):
    return w[pl.ds(pl.multiple_of(8 * s, 8), 8), 0:64, :].reshape(SLICE, 2 * H)


def down_block(w, s):
    row = pl.multiple_of(64 + 16 * (s // 2), 16)
    col = pl.multiple_of(SLICE * (s % 2), SLICE)
    return w[:, pl.ds(row, 16), pl.ds(col, SLICE)].reshape(H, SLICE)


def forward(tokens, weights):
    def body(x0, x1, x2, x3, w, hidden_t, gate_factor, act_out, xt, acc, hid):
        for k, x in enumerate((x0, x1, x2, x3)):
            part = jnp.dot(x[...], in_up_block(w, slice_of(k)), preferred_element_type=F32)
            if k == 0:
                acc[...] = part
            else:
                acc[...] += part
            xt[k] = x[...].T

        @pl.loop(0, TOK_DEV // 64)
        def _(i):
            rows = pl.ds(pl.multiple_of(i * 64, 64), 64)
            gate, up = acc[rows, :H], acc[rows, H:]
            sig = jax.nn.sigmoid(gate)
            act = gate * sig
            hid[rows, :] = (act * up).astype(BF16)
            gate_factor[rows, :] = up * sig * (1.0 + gate * (1.0 - sig))
            act_out[rows, :] = act

        hidden_t[...] = hid[...].T

    shapes = [
        struct((H, TOK_DEV), BF16),
        struct((TOK_DEV, H), F32),
        struct((TOK_DEV, H), F32),
        struct((N_EXPERT, SLICE, TOK_DEV), BF16),
    ]
    return call(
        body,
        "forward",
        5,
        shapes,
        2 * TOK_DEV * D * 2 * H,
        10 * MIB,
        [pltpu.VMEM((TOK_DEV, 2 * H), F32), pltpu.VMEM((TOK_DEV, H), BF16)],
    )(*tokens, weights)


def of_cotangents(first, ks, cots, route, hid_t, w, hg, scaled, put):
    scale = column(route[...])
    for k, c in zip(ks, cots):
        for j in range(SLICE // 128):
            cols = slice(128 * j, 128 * (j + 1))
            scaled[:, cols] = (scale * c[:, cols].astype(F32)).astype(BF16)
        part = lax.dot_general(scaled[...], down_block(w, slice_of(k)), NT, preferred_element_type=F32)
        if first and k == ks[0]:
            hg[...] = part
        else:
            hg[...] += part
        down = jnp.dot(hid_t[...], scaled[...], preferred_element_type=F32) / TOK_DEV
        put(k, down.astype(BF16))


def backward_early(cots, route, hidden_t, weights):
    def body(c0, c2, route_ref, hid_t, w, hg, downs, scaled):
        def put(k, down):
            downs[k // 2] = down

        of_cotangents(True, (0, 2), (c0, c2), route_ref, hid_t, w, hg, scaled, put)

    shapes = [struct((TOK_DEV, H), F32), struct((2, H, SLICE), BF16)]
    scratch = [pltpu.VMEM((TOK_DEV, SLICE), BF16)]
    return call(body, "backward_early", 5, shapes, 2 * TOK_DEV * D * H, 8 * MIB, scratch)(
        *cots, route, hidden_t, weights
    )


def backward(cots, route, hidden_t, early, downs, gate_factor, act, xt, weights):
    def body(c1, c3, route_ref, hid_t, hg0, down_ref, factor, act_ref, xt_ref, w, keep, send, both, hg, scaled):
        first = lax.axis_index("dp") % 2 == 0

        def put(k, down):
            down = down.reshape(N_CHIP, 2, 16, SLICE)
            rows = pl.ds(pl.multiple_of(128 + 16 * slice_of(k), 16), 16)
            keep[:, rows, :] = jnp.where(first, down[:, 0], down[:, 1])
            send[:, rows, :] = jnp.where(first, down[:, 1], down[:, 0])

        hg[...] = hg0[...]
        of_cotangents(False, (1, 3), (c1, c3), route_ref, hid_t, w, hg, scaled, put)
        put(0, down_ref[0])
        put(2, down_ref[1])

        @pl.loop(0, TOK_DEV // 64)
        def _(i):
            rows = pl.ds(pl.multiple_of(i * 64, 64), 64)
            g = hg[rows, :]
            both[rows, :H] = (g * factor[rows, :]).astype(BF16)
            both[rows, H:] = (g * act_ref[rows, :]).astype(BF16)

        for k in range(N_EXPERT):
            chips = pl.ds(pl.multiple_of(4 * slice_of(k), 4), 4)
            grad = jnp.dot(xt_ref[k], both[...], preferred_element_type=F32) / TOK_DEV
            grad = grad.astype(BF16).reshape(4, 2, 64, 2 * H)
            for a in range(2):
                own = grad[:, 0, :, a * H : (a + 1) * H]
                other = grad[:, 1, :, a * H : (a + 1) * H]
                keep[chips, 64 * a : 64 * (a + 1), :] = jnp.where(first, own, other)
                send[chips, 64 * a : 64 * (a + 1), :] = jnp.where(first, other, own)

    shapes = [
        struct((N_CHIP, ROWS, SLICE), BF16),
        struct((N_CHIP, ROWS, SLICE), BF16),
        struct((TOK_DEV, 2 * H), BF16),
    ]
    return call(
        body,
        "backward",
        10,
        shapes,
        6 * TOK_DEV * D * H,
        20 * MIB,
        [pltpu.VMEM((TOK_DEV, H), F32), pltpu.VMEM((TOK_DEV, SLICE), BF16)],
    )(*cots, route, hidden_t, early, downs, gate_factor, act, xt, weights)


def slot_gradients(both, weights):
    def body(both_ref, w, *out):
        for k in (2, 1, 3, 0):
            grad = lax.dot_general(both_ref[...], in_up_block(w, slice_of(k)), NT, preferred_element_type=F32)
            out[k][...] = grad.astype(BF16)

    shapes = [struct((TOK_DEV, SLICE), BF16)] * N_EXPERT
    return call(body, "slot_gradients", 2, shapes, 4 * TOK_DEV * D * H, 9 * MIB)(both, weights)


def pair_moments(own, other):
    def body(a_ref, b_ref, out):
        def step(q, sums):
            new = []
            for m in range(3):
                a = a_ref[q, 64 * m : 64 * (m + 1), :].astype(F32)
                b = b_ref[q, 64 * m : 64 * (m + 1), :].astype(F32)
                for t in (a * b, a * a, b * b):
                    t = jnp.sum(t.reshape(8, 8, SLICE), axis=0)
                    new.append(t[:, :128] + t[:, 128:256] + t[:, 256:384] + t[:, 384:])
            return tuple(s + n for s, n in zip(sums, new))

        sums = lax.fori_loop(0, N_CHIP, step, (jnp.zeros((8, 128), F32),) * 9)
        for j in range(9):
            out[j] = sums[j]

    return call(body, "pair_moments", 2, struct((9, 8, 128), F32), 9 * 2**20, 6 * MIB)(own, other)


def pair_merge(own, other, mine, theirs):
    def body(a_ref, b_ref, m_ref, t_ref, *out):
        coefs = []
        for m in range(3):
            inner = jnp.sum(m_ref[3 * m] + t_ref[3 * m], keepdims=True)
            norm_a = jnp.sum(m_ref[3 * m + 1] + t_ref[3 * m + 2], keepdims=True)
            norm_b = jnp.sum(m_ref[3 * m + 2] + t_ref[3 * m + 1], keepdims=True)
            coef_a = 1.0 - inner / (2.0 * (norm_a + epsilon))
            coef_b = 1.0 - inner / (2.0 * (norm_b + epsilon))
            coefs.append((jnp.broadcast_to(coef_a, (64, SLICE)), jnp.broadcast_to(coef_b, (64, SLICE))))
        c, at = place(0)

        @pl.loop(0, 4)
        def _(j):
            for k in range(4):
                first = lax.rem(at + k, 4)
                q = jnp.where(c == 0, 4 * j + first, 4 * first + j)
                for m in range(3):
                    rows = slice(64 * m, 64 * (m + 1))
                    a, b = a_ref[q, rows, :].astype(F32), b_ref[q, rows, :].astype(F32)
                    out[k][j, rows, :] = (coefs[m][0] * a + coefs[m][1] * b).astype(BF16)

    return call(body, "pair_merge", 4, [struct((4, ROWS, SLICE), BF16)] * 4, 9 * 2**20, 9 * MIB)(
        own, other, mine, theirs
    )


def turn_over(parts):
    def body(*refs):
        (_, first), (_, second) = place(0), place(1)
        for k in range(4):
            for m in range(4):
                refs[4 + k][lax.rem(first + 4 - m, 4)] = refs[m][lax.rem(second + k, 4)]

    return call(body, "turn_over", 4, [struct((4, ROWS, SLICE), BF16)] * 4, 2**10, 6 * MIB)(*parts)


def origin(index):
    c, second = place(1)
    other = (second + 4 - (index >> 2)) & 3
    return jnp.where(c == 0, other * 4 + (index & 3), (index & 3) * 4 + other)


def gram(parts):
    def body(*refs):
        x, out = refs[:4], refs[4]
        row = lax.broadcasted_iota(jnp.int32, (256, 256), 0)
        col = lax.broadcasted_iota(jnp.int32, (256, 256), 1)
        same = jnp.where(row % 16 == col % 16, 1.0, 0.0)
        fold = origin(lax.broadcasted_iota(jnp.int32, (256, 128), 0) // 16)
        fold = jnp.where(fold == lax.broadcasted_iota(jnp.int32, (256, 128), 1), 1.0, 0.0)
        order = origin(lax.broadcasted_iota(jnp.int32, (16, 16), 1))
        order = jnp.where(order == lax.broadcasted_iota(jnp.int32, (16, 16), 0), 1.0, 0.0)
        exact = dict(precision=lax.Precision.HIGHEST, preferred_element_type=F32)
        for m in range(3):
            acc = None
            for b in range(4):
                at = 64 * m + 16 * b
                block = jnp.concatenate([r[:, at : at + 16, :].reshape(64, SLICE) for r in x], axis=0)
                part = lax.dot_general(block, block, NT, preferred_element_type=F32)
                acc = part if acc is None else acc + part
            acc = jnp.sum((acc * same).reshape(16, 16, 256), axis=1)
            out[m] = jnp.dot(order, jnp.dot(acc, fold, **exact), **exact)

    return call(body, "gram", 4, struct((3, 16, 128), F32), 12 * 2 * 256 * 256 * 512, 3 * MIB)(*parts)


def finish(parts, products, gate, up, down, mom_gate, mom_up, mom_down):
    def body(x0, x1, x2, x3, g_ref, gate_w, up_w, down_w, gate_m, up_m, down_m, new_g, new_u, new_d, next_g, next_u, next_d):
        g = g_ref[...]
        i = lax.broadcasted_iota(jnp.int32, (3, 16, 128), 1)
        j = lax.broadcasted_iota(jnp.int32, (3, 16, 128), 2)
        c_col = jnp.ones((3, 16, 1), F32)
        c_row = jnp.ones((3, 1, 128), F32)
        for level in range(4):
            block_i, block_j = i >> level, j >> level
            same, sibling = block_i == block_j, (block_i ^ 1) == block_j
            weighted = g * c_col * c_row
            within = jnp.where(same, weighted, 0.0)
            across = jnp.where(sibling, weighted, 0.0)

            def coef(axis):
                norm = jnp.sum(jnp.where(same, jnp.sum(within, axis=3 - axis, keepdims=True), 0.0), axis=axis, keepdims=True)
                inner = jnp.sum(jnp.where(same, jnp.sum(across, axis=3 - axis, keepdims=True), 0.0), axis=axis, keepdims=True)
                return 1.0 - inner / (2.0 * (jnp.maximum(norm, 0.0) + epsilon))

            c_col, c_row = c_col * coef(2), c_row * coef(1)
        chip = origin(lax.broadcasted_iota(jnp.int32, (16, 128), 0))
        chip = chip == lax.broadcasted_iota(jnp.int32, (16, 128), 1)
        c_col = jnp.sum(jnp.where(chip, c_row, 0.0), axis=2, keepdims=True)
        olds = ((gate_w, gate_m, new_g, next_g), (up_w, up_m, new_u, next_u))
        for m in range(3):
            merged = jnp.zeros((64, SLICE), F32)
            for q in range(16):
                scale = jnp.broadcast_to(c_col[m, q : q + 1, :], (64, SLICE))
                x = (x0, x1, x2, x3)[q // 4]
                merged += scale * x[q % 4, 64 * m : 64 * (m + 1), :].astype(F32)
            if m < 2:
                w, mom, new, after = olds[m]
                step = momentum_decay * mom[...] + merged
                after[...] = step
                new[...] = w[...] - learning_rate * step
            else:
                for k in range(4):
                    cols = slice(SLICE * k, SLICE * (k + 1))
                    step = momentum_decay * down_m[:, cols] + merged[16 * k : 16 * (k + 1), :]
                    next_d[:, cols] = step
                    new_d[:, cols] = down_w[:, cols] - learning_rate * step

    wide, tall = struct((64, H), F32), struct((16, D), F32)
    return call(body, "finish", 11, [wide, wide, tall, wide, wide, tall], 2**22, 6 * MIB)(
        *parts, products, gate, up, down, mom_gate, mom_up, mom_down
    )


def scatter_rows(ids_rows, grads):
    block = 512

    def body(i0, i1, i2, i3, g0, g1, g2, g3, out):
        row = lax.broadcasted_iota(jnp.int32, (block, TOK_DEV), 0) + block * pl.program_id(0)
        acc = None
        for ids, g in zip((i0, i1, i2, i3), (g0, g1, g2, g3)):
            hot = jnp.where(jnp.broadcast_to(ids[...], row.shape) == row, 1.0, 0.0).astype(BF16)
            part = jnp.dot(hot, g[...], preferred_element_type=F32)
            acc = part if acc is None else acc + part
        out[...] = acc

    return pl.pallas_call(
        body,
        name="scatter_rows",
        grid=(POOL // block,),
        out_shape=struct((POOL, SLICE), F32),
        in_specs=[vmem()] * 8,
        out_specs=pl.BlockSpec((block, SLICE), lambda i: (i, 0)),
        compiler_params=pltpu.CompilerParams(vmem_limit_bytes=24 * MIB),
        cost_estimate=pl.CostEstimate(
            flops=2 * POOL * POOL * SLICE, bytes_accessed=6 * MIB, transcendentals=0
        ),
    )(*ids_rows, *grads)


def shift(block, axis, to):
    return lax.ppermute(block, axis, [(i, to(i)) for i in range(lax.axis_size(axis))])


def around_y(block, k):
    return shift(block, "expert", lambda i: (i + k) % N_EXPERT)


def around_z(block, k):
    return shift(block, "dp", lambda i: i // 8 * 8 + (i // 2 % 4 + k) % 4 * 2 + i % 2)


def around_x(block, k):
    return shift(block, "dp", lambda i: (i // 8 + k) % 4 * 8 + i % 8)


def other_core(block):
    return shift(block, "dp", lambda i: i ^ 1)


def sum_dp(value):
    for around in (around_z, around_x):
        value = value + sum(around(value, k) for k in (2, 1, 3))
    return value + other_core(value)


def pack(gate, up, down):
    def body(gate_hbm, up_hbm, down_hbm, out, g, u, d, sems):
        copies = [
            pltpu.make_async_copy(src, dst, sems.at[j])
            for j, (src, dst) in enumerate(((gate_hbm, g), (up_hbm, u), (down_hbm, d)))
        ]
        for copy in copies:
            copy.start()
        for copy in copies:
            copy.wait()
        out[0:64, 0:H] = g[...].astype(BF16)
        out[0:64, H:] = u[...].astype(BF16)
        out[64:80, :] = d[:, : D // 2].astype(BF16)
        out[80:96, :] = d[:, D // 2 :].astype(BF16)

    return pl.pallas_call(
        body,
        name="pack",
        out_shape=struct((96, 1024), BF16),
        in_specs=[pl.BlockSpec(memory_space=pl.ANY)] * 3,
        out_specs=vmem(),
        scratch_shapes=[
            pltpu.VMEM((64, H), F32),
            pltpu.VMEM((64, H), F32),
            pltpu.VMEM((16, D), F32),
            pltpu.SemaphoreType.DMA((3,)),
        ],
        compiler_params=pltpu.CompilerParams(vmem_limit_bytes=8 * MIB),
        cost_estimate=pl.CostEstimate(flops=2**17, bytes_accessed=MIB, transcendentals=0),
    )(gate, up, down)


def along(turn, step):
    def to(i):
        x, z, c = i // 8, i // 2 % 4, i % 2
        return x * 8 + (z + step) % 4 * 2 + c if c == turn else (x + step) % 4 * 8 + z * 2 + c

    return to


def spread(block, turn):
    return [shift(block, "dp", along(turn, k)) for k in (1, 2, 3)]


def place(turn):
    at = lax.axis_index("dp")
    x, z, c = at // 8, lax.rem(at // 2, 4), lax.rem(at, 2)
    return c, jnp.where(c == turn, z, x)


def bundle(blocks):
    def body(*refs):
        _, at = place(0)
        for k in range(4):
            refs[4][lax.rem(at + 4 - k, 4)] = refs[k][...]

    return call(body, "bundle", 4, struct((4, 96, 1024), BF16), 2**10, 2 * MIB)(*blocks)


def half_of_weights(bundles):
    def body(*refs):
        c, at = place(1)
        for k in range(4):
            other = lax.rem(at + 4 - k, 4)
            for j in range(4):
                refs[4][jnp.where(c == 0, other * 4 + j, j * 4 + other)] = refs[k][j]

    return call(body, "half_of_weights", 4, struct((N_CHIP, 96, 1024), BF16), 2**10, 6 * MIB)(*bundles)


def whole_weights(own, other):
    def body(a, b, out):
        c = lax.rem(lax.axis_index("dp"), 2)

        @pl.loop(0, N_CHIP)
        def _(q):
            out[2 * q + c] = a[q]
            out[2 * q + 1 - c] = b[q]

    return call(body, "whole_weights", 2, struct((2 * N_CHIP, 96, 1024), BF16), 2**10, 12 * MIB)(own, other)


def local(
    pool_tokens,
    pool_cotangent,
    token_ids,
    route_weights,
    gate_weight,
    up_weight,
    down_weight,
    momentum_gate,
    momentum_up,
    momentum_down,
):
    tie = lax.optimization_barrier

    def picked(k, pool):
        return pick_rows(ids[k : k + 1], [pool])[0]

    ids = [token_ids] + [around_y(token_ids, N_EXPERT - k) for k in (1, 2, 3)]
    x, c = [None] * 4, [None] * 4
    x[1], x[3] = picked(1, pool_tokens), picked(3, pool_tokens)
    ids, x[1], x[3], shards = tie((ids, x[1], x[3], (gate_weight[0], up_weight[0], down_weight[0])))

    packed = pack(*shards)
    blocks = spread(packed, 0)
    x[1], x[3] = around_y(x[1], 1), around_y(x[3], 3)
    x[2], c[2] = picked(2, pool_tokens), picked(2, pool_cotangent)
    ids, blocks, x[1:], c[2] = tie((ids, blocks, x[1:], c[2]))

    block = bundle((packed, *blocks))
    blocks = spread(block, 1)
    x[2], c[2] = around_y(x[2], 2), around_y(c[2], 2)
    c[1], c[3] = picked(1, pool_cotangent), picked(3, pool_cotangent)
    x[0], c[0] = pick_rows(ids[:1], [pool_tokens, pool_cotangent])
    blocks, x, c = tie((blocks, x, c))

    mine = half_of_weights((block, *blocks))
    weights = whole_weights(mine, other_core(mine))
    c[1], c[3] = around_y(c[1], 1), around_y(c[3], 3)

    hidden_t, gate_factor, act, xt = forward(x, weights)
    early, downs = backward_early((c[0], c[2]), route_weights, hidden_t, weights)
    keep, send, both = backward(
        (c[1], c[3]), route_weights, hidden_t, early, downs, gate_factor, act, xt, weights
    )
    received = other_core(send)
    slots = slot_gradients(both, weights)
    received, slots = lax.optimization_barrier((received, list(slots)))

    mine = pair_moments(keep, received)
    sent = pair_merge(keep, received, mine, other_core(mine))
    parts = [sent[0]] + [shift(sent[k], "dp", along(0, k)) for k in (1, 2, 3)]
    back = [slots[0], around_y(slots[1], 3), None, around_y(slots[3], 1)]
    parts, back[1], back[3], slots[2] = tie((parts, back[1], back[3], slots[2]))
    back[2] = around_y(slots[2], 2)
    sent = turn_over(parts)
    parts = [sent[0]] + [shift(sent[k], "dp", along(1, k)) for k in (1, 2, 3)]
    pool_grad = scatter_rows(ids, back)
    parts, pool_grad = tie((parts, pool_grad))
    products = sum_dp(gram(parts))
    outs = finish(
        parts,
        products,
        gate_weight[0],
        up_weight[0],
        down_weight[0],
        momentum_gate[0],
        momentum_up[0],
        momentum_down[0],
    )
    return (*(a[None] for a in outs), pool_grad)


def solution(mesh):
    in_specs = (
        P("dp", "expert"),
        P("dp", "expert"),
        P("expert", "dp"),
        P("expert", "dp"),
        P("expert", "dp", None),
        P("expert", "dp", None),
        P("expert", "dp", None),
        P("expert", "dp", None),
        P("expert", "dp", None),
        P("expert", "dp", None),
    )
    out_specs = (
        P("expert", "dp", None),
        P("expert", "dp", None),
        P("expert", "dp", None),
        P("expert", "dp", None),
        P("expert", "dp", None),
        P("expert", "dp", None),
        P("dp", "expert"),
    )
    return jax.shard_map(local, mesh=mesh, in_specs=in_specs, out_specs=out_specs, check_vma=False)
```

```python
import jax
import jax.numpy as jnp
from jax import lax
from jax.experimental import pallas as pl
from jax.experimental.pallas import tpu as pltpu
from jax.sharding import PartitionSpec as P

TOK_DEV = 512
POOL = 2048
D = 2048
H = 512
N_EXPERT = 4
N_CHIP = 16
SLICE = 512
ROWS = 192

momentum_decay = 0.9
learning_rate = 0.05
epsilon = 1e-06

MIB = 1 << 20
F32 = jnp.float32
BF16 = jnp.bfloat16
NT = (((1,), (1,)), ((), ()))


def vmem():
    return pl.BlockSpec(memory_space=pltpu.VMEM)


def call(body, name, n_in, out_shapes, flops, nbytes, scratch=(), limit=20):
    return pl.pallas_call(
        body,
        name=name,
        out_shape=out_shapes,
        in_specs=[vmem()] * n_in,
        out_specs=jax.tree.map(lambda _: vmem(), out_shapes),
        scratch_shapes=list(scratch),
        compiler_params=pltpu.CompilerParams(vmem_limit_bytes=limit * MIB),
        cost_estimate=pl.CostEstimate(flops=flops, bytes_accessed=nbytes, transcendentals=0),
    )


def struct(shape, dtype):
    return jax.ShapeDtypeStruct(shape, dtype)


def column(row):
    return jnp.broadcast_to(row, (128, row.shape[1])).T


def pick_rows(ids_rows, pools, stacked=False):
    n_ids, n_pool = len(ids_rows), len(pools)

    def body(*refs):
        ids, src = refs[:n_ids], refs[n_ids : n_ids + n_pool]
        out, hot = refs[n_ids + n_pool : -1], refs[-1]
        lane = lax.broadcasted_iota(jnp.int32, (TOK_DEV, 128), 1)
        for k in range(n_ids):
            named = column(ids[k][...])
            for j in range(POOL // 128):
                hot[:, 128 * j : 128 * (j + 1)] = jnp.where(named == lane + 128 * j, 1.0, 0.0).astype(BF16)
            for a in range(n_pool):
                rows = jnp.dot(hot[...], src[a][...], preferred_element_type=F32).astype(BF16)
                if stacked:
                    out[k][TOK_DEV * a : TOK_DEV * (a + 1), :] = rows
                else:
                    out[k * n_pool + a][...] = rows

    shapes = [struct((TOK_DEV, SLICE), BF16)] * (n_ids * n_pool)
    if stacked:
        shapes = [struct((n_pool * TOK_DEV, SLICE), BF16)] * n_ids
    return call(
        body,
        "pick_rows",
        n_ids + n_pool,
        shapes,
        2 * TOK_DEV * POOL * SLICE * n_ids * n_pool,
        (4 + 2 * n_ids) * MIB // 2,
        [pltpu.VMEM((TOK_DEV, POOL), BF16)],
    )(*ids_rows, *pools)


def slice_of(k):
    me = lax.axis_index("expert")
    return lax.rem(me + N_EXPERT - k, N_EXPERT)


def in_up_block(w, s):
    return w[pl.ds(pl.multiple_of(8 * s, 8), 8), 0:64, :].reshape(SLICE, 2 * H)


def down_block(w, s):
    row = pl.multiple_of(64 + 16 * (s // 2), 16)
    col = pl.multiple_of(SLICE * (s % 2), SLICE)
    return w[:, pl.ds(row, 16), pl.ds(col, SLICE)].reshape(H, SLICE)


def forward(tokens, weights):
    def body(x0, x1, x2, x3, w, hidden_t, gate_factor, act_out, xt, acc, hid):
        for k, x in enumerate((x0, x1, x2, x3)):
            part = jnp.dot(x[0:TOK_DEV, :], in_up_block(w, slice_of(k)), preferred_element_type=F32)
            if k == 0:
                acc[...] = part
            else:
                acc[...] += part
            xt[k] = x[0:TOK_DEV, :].T

        @pl.loop(0, TOK_DEV // 64)
        def _(i):
            rows = pl.ds(pl.multiple_of(i * 64, 64), 64)
            gate, up = acc[rows, :H], acc[rows, H:]
            sig = jax.nn.sigmoid(gate)
            act = gate * sig
            hid[rows, :] = (act * up).astype(BF16)
            gate_factor[rows, :] = up * sig * (1.0 + gate * (1.0 - sig))
            act_out[rows, :] = act

        hidden_t[...] = hid[...].T

    shapes = [
        struct((H, TOK_DEV), BF16),
        struct((TOK_DEV, H), F32),
        struct((TOK_DEV, H), F32),
        struct((N_EXPERT, SLICE, TOK_DEV), BF16),
    ]
    return call(
        body,
        "forward",
        5,
        shapes,
        2 * TOK_DEV * D * 2 * H,
        10 * MIB,
        [pltpu.VMEM((TOK_DEV, 2 * H), F32), pltpu.VMEM((TOK_DEV, H), BF16)],
    )(*tokens, weights)


def of_cotangents(first, ks, cots, route, hid_t, w, hg, scaled, put):
    scale = column(route[...])
    for k, c in zip(ks, cots):
        for j in range(SLICE // 128):
            cols = slice(128 * j, 128 * (j + 1))
            rows = slice(c.shape[0] - TOK_DEV, c.shape[0])
            scaled[:, cols] = (scale * c[rows, cols].astype(F32)).astype(BF16)
        part = lax.dot_general(scaled[...], down_block(w, slice_of(k)), NT, preferred_element_type=F32)
        if first and k == ks[0]:
            hg[...] = part
        else:
            hg[...] += part
        down = jnp.dot(hid_t[...], scaled[...], preferred_element_type=F32) / TOK_DEV
        put(k, down.astype(BF16))


def backward_early(cots, route, hidden_t, weights):
    def body(c0, c2, route_ref, hid_t, w, hg, downs, scaled):
        def put(k, down):
            downs[k // 2] = down

        of_cotangents(True, (0, 2), (c0, c2), route_ref, hid_t, w, hg, scaled, put)

    shapes = [struct((TOK_DEV, H), F32), struct((2, H, SLICE), BF16)]
    scratch = [pltpu.VMEM((TOK_DEV, SLICE), BF16)]
    return call(body, "backward_early", 5, shapes, 2 * TOK_DEV * D * H, 8 * MIB, scratch)(
        *cots, route, hidden_t, weights
    )


def backward_down(cots, route, hidden_t, early, downs, weights):
    def body(c1, c3, route_ref, hid_t, hg0, down_ref, w, keep, send, hg, scaled):
        first = lax.axis_index("dp") % 2 == 0

        def put(k, down):
            down = down.reshape(N_CHIP, 2, 16, SLICE)
            rows = pl.ds(pl.multiple_of(16 * slice_of(k), 16), 16)
            keep[:, rows, :] = jnp.where(first, down[:, 0], down[:, 1])
            send[:, rows, :] = jnp.where(first, down[:, 1], down[:, 0])

        hg[...] = hg0[...]
        of_cotangents(False, (1, 3), (c1, c3), route_ref, hid_t, w, hg, scaled, put)
        put(0, down_ref[0])
        put(2, down_ref[1])

    half = struct((N_CHIP, 64, SLICE), BF16)
    shapes = [half, half, struct((TOK_DEV, H), F32)]
    scratch = [pltpu.VMEM((TOK_DEV, SLICE), BF16)]
    return call(body, "backward_down", 7, shapes, 2 * TOK_DEV * D * H, 10 * MIB, scratch)(
        *cots, route, hidden_t, early, downs, weights
    )


def backward_in(hidden_grad, gate_factor, act, xt):
    def body(hg, factor, act_ref, xt_ref, keep, send, both):
        first = lax.axis_index("dp") % 2 == 0

        @pl.loop(0, TOK_DEV // 64)
        def _(i):
            rows = pl.ds(pl.multiple_of(i * 64, 64), 64)
            g = hg[rows, :]
            both[rows, :H] = (g * factor[rows, :]).astype(BF16)
            both[rows, H:] = (g * act_ref[rows, :]).astype(BF16)

        for k in range(N_EXPERT):
            chips = pl.ds(pl.multiple_of(4 * slice_of(k), 4), 4)
            grad = jnp.dot(xt_ref[k], both[...], preferred_element_type=F32) / TOK_DEV
            grad = grad.astype(BF16).reshape(4, 2, 64, 2 * H)
            for a in range(2):
                own = grad[:, 0, :, a * H : (a + 1) * H]
                other = grad[:, 1, :, a * H : (a + 1) * H]
                keep[chips, 64 * a : 64 * (a + 1), :] = jnp.where(first, own, other)
                send[chips, 64 * a : 64 * (a + 1), :] = jnp.where(first, other, own)

    half = struct((N_CHIP, 128, SLICE), BF16)
    shapes = [half, half, struct((TOK_DEV, 2 * H), BF16)]
    return call(body, "backward_in", 4, shapes, 4 * TOK_DEV * D * H, 10 * MIB)(hidden_grad, gate_factor, act, xt)


def slot_gradients(both, weights):
    def body(both_ref, w, *out):
        for k in (2, 1, 3, 0):
            grad = lax.dot_general(both_ref[...], in_up_block(w, slice_of(k)), NT, preferred_element_type=F32)
            out[k][...] = grad.astype(BF16)

    shapes = [struct((TOK_DEV, SLICE), BF16)] * N_EXPERT
    return call(body, "slot_gradients", 2, shapes, 4 * TOK_DEV * D * H, 9 * MIB)(both, weights)


def rows_of(of_in, of_down, q, m):
    return of_down[q] if m == 2 else of_in[q, 64 * m : 64 * (m + 1), :]


def pair_moments(own, other):
    def body(a_in, a_down, b_in, b_down, out):
        def step(q, sums):
            new = []
            for m in range(3):
                a = rows_of(a_in, a_down, q, m).astype(F32)
                b = rows_of(b_in, b_down, q, m).astype(F32)
                for t in (a * b, a * a, b * b):
                    t = jnp.sum(t.reshape(8, 8, SLICE), axis=0)
                    new.append(t[:, :128] + t[:, 128:256] + t[:, 256:384] + t[:, 384:])
            return tuple(s + n for s, n in zip(sums, new))

        sums = lax.fori_loop(0, N_CHIP, step, (jnp.zeros((8, 128), F32),) * 9)
        for j in range(9):
            out[j] = sums[j]

    return call(body, "pair_moments", 4, struct((9, 8, 128), F32), 9 * 2**20, 6 * MIB)(*own, *other)


def pair_merge(own, other, mine, theirs):
    def body(a_in, a_down, b_in, b_down, m_ref, t_ref, *out):
        coefs = []
        for m in range(3):
            inner = jnp.sum(m_ref[3 * m] + t_ref[3 * m], keepdims=True)
            norm_a = jnp.sum(m_ref[3 * m + 1] + t_ref[3 * m + 2], keepdims=True)
            norm_b = jnp.sum(m_ref[3 * m + 2] + t_ref[3 * m + 1], keepdims=True)
            coef_a = 1.0 - inner / (2.0 * (norm_a + epsilon))
            coef_b = 1.0 - inner / (2.0 * (norm_b + epsilon))
            coefs.append((jnp.broadcast_to(coef_a, (64, SLICE)), jnp.broadcast_to(coef_b, (64, SLICE))))
        c, at = place(0)

        @pl.loop(0, 4)
        def _(j):
            for k in range(4):
                first = lax.rem(at + k, 4)
                q = jnp.where(c == 0, 4 * j + first, 4 * first + j)
                for m in range(3):
                    rows = slice(64 * m, 64 * (m + 1))
                    a = rows_of(a_in, a_down, q, m).astype(F32)
                    b = rows_of(b_in, b_down, q, m).astype(F32)
                    out[k][j, rows, :] = (coefs[m][0] * a + coefs[m][1] * b).astype(BF16)

    return call(body, "pair_merge", 6, [struct((4, ROWS, SLICE), BF16)] * 4, 9 * 2**20, 9 * MIB)(
        *own, *other, mine, theirs
    )


def turn_over(parts):
    def body(*refs):
        (_, first), (_, second) = place(0), place(1)
        for k in range(4):
            for m in range(4):
                refs[4 + k][lax.rem(first + 4 - m, 4)] = refs[m][lax.rem(second + k, 4)]

    return call(body, "turn_over", 4, [struct((4, ROWS, SLICE), BF16)] * 4, 2**10, 6 * MIB)(*parts)


def origin(index):
    c, second = place(1)
    other = (second + 4 - (index >> 2)) & 3
    return jnp.where(c == 0, other * 4 + (index & 3), (index & 3) * 4 + other)


def gram(parts):
    def body(*refs):
        x, out = refs[:4], refs[4]
        row = lax.broadcasted_iota(jnp.int32, (256, 256), 0)
        col = lax.broadcasted_iota(jnp.int32, (256, 256), 1)
        same = jnp.where(row % 16 == col % 16, 1.0, 0.0)
        fold = origin(lax.broadcasted_iota(jnp.int32, (256, 128), 0) // 16)
        fold = jnp.where(fold == lax.broadcasted_iota(jnp.int32, (256, 128), 1), 1.0, 0.0)
        order = origin(lax.broadcasted_iota(jnp.int32, (16, 16), 1))
        order = jnp.where(order == lax.broadcasted_iota(jnp.int32, (16, 16), 0), 1.0, 0.0)
        exact = dict(precision=lax.Precision.HIGHEST, preferred_element_type=F32)
        for m in range(3):
            acc = None
            for b in range(4):
                at = 64 * m + 16 * b
                block = jnp.concatenate([r[:, at : at + 16, :].reshape(64, SLICE) for r in x], axis=0)
                part = lax.dot_general(block, block, NT, preferred_element_type=F32)
                acc = part if acc is None else acc + part
            acc = jnp.sum((acc * same).reshape(16, 16, 256), axis=1)
            out[m] = jnp.dot(order, jnp.dot(acc, fold, **exact), **exact)

    return call(body, "gram", 4, struct((3, 16, 128), F32), 12 * 2 * 256 * 256 * 512, 3 * MIB)(*parts)


def finish(parts, products, gate, up, down, mom_gate, mom_up, mom_down):
    def body(x0, x1, x2, x3, g_ref, gate_w, up_w, down_w, gate_m, up_m, down_m, new_g, new_u, new_d, next_g, next_u, next_d):
        g = g_ref[...]
        i = lax.broadcasted_iota(jnp.int32, (3, 16, 128), 1)
        j = lax.broadcasted_iota(jnp.int32, (3, 16, 128), 2)
        c_col = jnp.ones((3, 16, 1), F32)
        c_row = jnp.ones((3, 1, 128), F32)
        for level in range(4):
            block_i, block_j = i >> level, j >> level
            same, sibling = block_i == block_j, (block_i ^ 1) == block_j
            weighted = g * c_col * c_row
            within = jnp.where(same, weighted, 0.0)
            across = jnp.where(sibling, weighted, 0.0)

            def coef(axis):
                norm = jnp.sum(jnp.where(same, jnp.sum(within, axis=3 - axis, keepdims=True), 0.0), axis=axis, keepdims=True)
                inner = jnp.sum(jnp.where(same, jnp.sum(across, axis=3 - axis, keepdims=True), 0.0), axis=axis, keepdims=True)
                return 1.0 - inner / (2.0 * (jnp.maximum(norm, 0.0) + epsilon))

            c_col, c_row = c_col * coef(2), c_row * coef(1)
        chip = origin(lax.broadcasted_iota(jnp.int32, (16, 128), 0))
        chip = chip == lax.broadcasted_iota(jnp.int32, (16, 128), 1)
        c_col = jnp.sum(jnp.where(chip, c_row, 0.0), axis=2, keepdims=True)
        olds = ((gate_w, gate_m, new_g, next_g), (up_w, up_m, new_u, next_u))
        for m in range(3):
            merged = jnp.zeros((64, SLICE), F32)
            for q in range(16):
                scale = jnp.broadcast_to(c_col[m, q : q + 1, :], (64, SLICE))
                x = (x0, x1, x2, x3)[q // 4]
                merged += scale * x[q % 4, 64 * m : 64 * (m + 1), :].astype(F32)
            if m < 2:
                w, mom, new, after = olds[m]
                step = momentum_decay * mom[...] + merged
                after[...] = step
                new[...] = w[...] - learning_rate * step
            else:
                for k in range(4):
                    cols = slice(SLICE * k, SLICE * (k + 1))
                    step = momentum_decay * down_m[:, cols] + merged[16 * k : 16 * (k + 1), :]
                    next_d[:, cols] = step
                    new_d[:, cols] = down_w[:, cols] - learning_rate * step

    wide, tall = struct((64, H), F32), struct((16, D), F32)
    return call(body, "finish", 11, [wide, wide, tall, wide, wide, tall], 2**22, 6 * MIB)(
        *parts, products, gate, up, down, mom_gate, mom_up, mom_down
    )


def scatter_rows(ids_rows, grads):
    block = 512

    def body(i0, i1, i2, i3, g0, g1, g2, g3, out):
        row = lax.broadcasted_iota(jnp.int32, (block, TOK_DEV), 0) + block * pl.program_id(0)
        acc = None
        for ids, g in zip((i0, i1, i2, i3), (g0, g1, g2, g3)):
            hot = jnp.where(jnp.broadcast_to(ids[...], row.shape) == row, 1.0, 0.0).astype(BF16)
            part = jnp.dot(hot, g[...], preferred_element_type=F32)
            acc = part if acc is None else acc + part
        out[...] = acc

    return pl.pallas_call(
        body,
        name="scatter_rows",
        grid=(POOL // block,),
        out_shape=struct((POOL, SLICE), F32),
        in_specs=[vmem()] * 8,
        out_specs=pl.BlockSpec((block, SLICE), lambda i: (i, 0)),
        compiler_params=pltpu.CompilerParams(vmem_limit_bytes=24 * MIB),
        cost_estimate=pl.CostEstimate(
            flops=2 * POOL * POOL * SLICE, bytes_accessed=6 * MIB, transcendentals=0
        ),
    )(*ids_rows, *grads)


def shift(block, axis, to):
    return lax.ppermute(block, axis, [(i, to(i)) for i in range(lax.axis_size(axis))])


def around_y(block, k):
    return shift(block, "expert", lambda i: (i + k) % N_EXPERT)


def around_z(block, k):
    return shift(block, "dp", lambda i: i // 8 * 8 + (i // 2 % 4 + k) % 4 * 2 + i % 2)


def around_x(block, k):
    return shift(block, "dp", lambda i: (i // 8 + k) % 4 * 8 + i % 8)


def other_core(block):
    return shift(block, "dp", lambda i: i ^ 1)


def sum_dp(value):
    for around in (around_z, around_x):
        value = value + sum(around(value, k) for k in (2, 1, 3))
    return value + other_core(value)


def pack(gate, up, down):
    def body(gate_hbm, up_hbm, down_hbm, out, g, u, d, sems):
        copies = [
            pltpu.make_async_copy(src, dst, sems.at[j])
            for j, (src, dst) in enumerate(((gate_hbm, g), (up_hbm, u), (down_hbm, d)))
        ]
        for copy in copies:
            copy.start()
        for copy in copies:
            copy.wait()
        out[0:64, 0:H] = g[...].astype(BF16)
        out[0:64, H:] = u[...].astype(BF16)
        out[64:80, :] = d[:, : D // 2].astype(BF16)
        out[80:96, :] = d[:, D // 2 :].astype(BF16)

    return pl.pallas_call(
        body,
        name="pack",
        out_shape=struct((96, 1024), BF16),
        in_specs=[pl.BlockSpec(memory_space=pl.ANY)] * 3,
        out_specs=vmem(),
        scratch_shapes=[
            pltpu.VMEM((64, H), F32),
            pltpu.VMEM((64, H), F32),
            pltpu.VMEM((16, D), F32),
            pltpu.SemaphoreType.DMA((3,)),
        ],
        compiler_params=pltpu.CompilerParams(vmem_limit_bytes=8 * MIB),
        cost_estimate=pl.CostEstimate(flops=2**17, bytes_accessed=MIB, transcendentals=0),
    )(gate, up, down)


def along(turn, step):
    def to(i):
        x, z, c = i // 8, i // 2 % 4, i % 2
        return x * 8 + (z + step) % 4 * 2 + c if c == turn else (x + step) % 4 * 8 + z * 2 + c

    return to


def to_others(blocks, turn):
    out = {k: shift(blocks[k], "dp", along(turn, k)) for k in (2, 1, 3)}
    return [out[1], out[2], out[3]]


def spread(block, turn):
    return to_others([block] * 4, turn)


def place(turn):
    at = lax.axis_index("dp")
    x, z, c = at // 8, lax.rem(at // 2, 4), lax.rem(at, 2)
    return c, jnp.where(c == turn, z, x)


def bundle(blocks):
    def body(*refs):
        _, at = place(0)
        for k in range(4):
            refs[4][lax.rem(at + 4 - k, 4)] = refs[k][...]

    return call(body, "bundle", 4, struct((4, 96, 1024), BF16), 2**10, 2 * MIB)(*blocks)


def half_of_weights(bundles):
    def body(*refs):
        c, at = place(1)
        for k in range(4):
            other = lax.rem(at + 4 - k, 4)
            for j in range(4):
                refs[4][jnp.where(c == 0, other * 4 + j, j * 4 + other)] = refs[k][j]

    return call(body, "half_of_weights", 4, struct((N_CHIP, 96, 1024), BF16), 2**10, 6 * MIB)(*bundles)


def whole_weights(own, other):
    def body(a, b, out):
        c = lax.rem(lax.axis_index("dp"), 2)

        @pl.loop(0, N_CHIP)
        def _(q):
            out[2 * q + c] = a[q]
            out[2 * q + 1 - c] = b[q]

    return call(body, "whole_weights", 2, struct((2 * N_CHIP, 96, 1024), BF16), 2**10, 12 * MIB)(own, other)


def local(
    pool_tokens,
    pool_cotangent,
    token_ids,
    route_weights,
    gate_weight,
    up_weight,
    down_weight,
    momentum_gate,
    momentum_up,
    momentum_down,
):
    tie = lax.optimization_barrier

    def picked(k, pool):
        return pick_rows(ids[k : k + 1], [pool])[0]

    ids = [token_ids] + [around_y(token_ids, N_EXPERT - k) for k in (1, 2, 3)]
    x, c = [None] * 4, [None] * 4
    x[1], x[3] = picked(1, pool_tokens), picked(3, pool_tokens)
    ids, x[1], x[3], shards = tie((ids, x[1], x[3], (gate_weight[0], up_weight[0], down_weight[0])))

    packed = pack(*shards)
    blocks = spread(packed, 0)
    x[1], x[3] = around_y(x[1], 1), around_y(x[3], 3)
    (x[2],) = pick_rows(ids[2:3], [pool_tokens, pool_cotangent], stacked=True)
    ids, blocks, x[1:] = tie((ids, blocks, x[1:]))

    block = bundle((packed, *blocks))
    blocks = spread(block, 1)
    x[2] = c[2] = around_y(x[2], 2)
    c[1], c[3] = picked(1, pool_cotangent), picked(3, pool_cotangent)
    x[0], c[0] = pick_rows(ids[:1], [pool_tokens, pool_cotangent])
    blocks, x, c = tie((blocks, x, [c[0], c[1], c[3]]))
    c = [c[0], c[1], x[2], c[2]]

    mine = half_of_weights((block, *blocks))
    weights = whole_weights(mine, other_core(mine))
    c[1], c[3] = around_y(c[1], 1), around_y(c[3], 3)

    hidden_t, gate_factor, act, xt = forward(x, weights)
    early, downs = backward_early((c[0], c[2]), route_weights, hidden_t, weights)
    keep_down, send_down, hidden_grad = backward_down((c[1], c[3]), route_weights, hidden_t, early, downs, weights)
    keep_in, send_in, both = backward_in(hidden_grad, gate_factor, act, xt)
    received_down, both = tie((other_core(send_down), both))
    keep, received = (keep_in, keep_down), (other_core(send_in), received_down)
    slots = slot_gradients(both, weights)
    received, slots = lax.optimization_barrier((received, list(slots)))

    mine = pair_moments(keep, received)
    sent = pair_merge(keep, received, mine, other_core(mine))
    parts = [sent[0], *to_others(sent, 0)]
    back = [slots[0], around_y(slots[1], 3), None, around_y(slots[3], 1)]
    parts, back[1], back[3] = tie((parts, back[1], back[3]))
    sent, slots[2] = tie((turn_over(parts), slots[2]))
    parts = [sent[0], *to_others(sent, 1)]
    back[2] = around_y(slots[2], 2)
    pool_grad = scatter_rows(ids, back)
    parts, pool_grad = tie((parts, pool_grad))
    products = sum_dp(gram(parts))
    outs = finish(
        parts,
        products,
        gate_weight[0],
        up_weight[0],
        down_weight[0],
        momentum_gate[0],
        momentum_up[0],
        momentum_down[0],
    )
    return (*(a[None] for a in outs), pool_grad)


def solution(mesh):
    in_specs = (
        P("dp", "expert"),
        P("dp", "expert"),
        P("expert", "dp"),
        P("expert", "dp"),
        P("expert", "dp", None),
        P("expert", "dp", None),
        P("expert", "dp", None),
        P("expert", "dp", None),
        P("expert", "dp", None),
        P("expert", "dp", None),
    )
    out_specs = (
        P("expert", "dp", None),
        P("expert", "dp", None),
        P("expert", "dp", None),
        P("expert", "dp", None),
        P("expert", "dp", None),
        P("expert", "dp", None),
        P("dp", "expert"),
    )
    return jax.shard_map(local, mesh=mesh, in_specs=in_specs, out_specs=out_specs, check_vma=False)
```

```python
import jax
import jax.numpy as jnp
from jax import lax
from jax.experimental import pallas as pl
from jax.experimental.pallas import tpu as pltpu
from jax.sharding import PartitionSpec as P

TOK_DEV = 512
POOL = 2048
D = 2048
H = 512
N_EXPERT = 4
N_CHIP = 16
SLICE = 512
ROWS = 192

momentum_decay = 0.9
learning_rate = 0.05
epsilon = 1e-06

MIB = 1 << 20
F32 = jnp.float32
BF16 = jnp.bfloat16
NT = (((1,), (1,)), ((), ()))


def vmem():
    return pl.BlockSpec(memory_space=pltpu.VMEM)


def call(body, name, n_in, out_shapes, flops, nbytes, scratch=(), limit=20):
    return pl.pallas_call(
        body,
        name=name,
        out_shape=out_shapes,
        in_specs=[vmem()] * n_in,
        out_specs=jax.tree.map(lambda _: vmem(), out_shapes),
        scratch_shapes=list(scratch),
        compiler_params=pltpu.CompilerParams(vmem_limit_bytes=limit * MIB),
        cost_estimate=pl.CostEstimate(flops=flops, bytes_accessed=nbytes, transcendentals=0),
    )


def struct(shape, dtype):
    return jax.ShapeDtypeStruct(shape, dtype)


def column(row):
    return jnp.broadcast_to(row, (128, row.shape[1])).T


def pick_rows(ids_rows, pools, stacked=False):
    n_ids, n_pool = len(ids_rows), len(pools)

    def body(*refs):
        ids, src = refs[:n_ids], refs[n_ids : n_ids + n_pool]
        out, hot = refs[n_ids + n_pool : -1], refs[-1]
        lane = lax.broadcasted_iota(jnp.int32, (TOK_DEV, 128), 1)
        for k in range(n_ids):
            named = column(ids[k][...])
            for j in range(POOL // 128):
                hot[:, 128 * j : 128 * (j + 1)] = jnp.where(named == lane + 128 * j, 1.0, 0.0).astype(BF16)
            for a in range(n_pool):
                rows = jnp.dot(hot[...], src[a][...], preferred_element_type=F32).astype(BF16)
                if stacked:
                    out[k][TOK_DEV * a : TOK_DEV * (a + 1), :] = rows
                else:
                    out[k * n_pool + a][...] = rows

    shapes = [struct((TOK_DEV, SLICE), BF16)] * (n_ids * n_pool)
    if stacked:
        shapes = [struct((n_pool * TOK_DEV, SLICE), BF16)] * n_ids
    return call(
        body,
        "pick_rows",
        n_ids + n_pool,
        shapes,
        2 * TOK_DEV * POOL * SLICE * n_ids * n_pool,
        (4 + 2 * n_ids) * MIB // 2,
        [pltpu.VMEM((TOK_DEV, POOL), BF16)],
    )(*ids_rows, *pools)


def slice_of(k):
    me = lax.axis_index("expert")
    return lax.rem(me + N_EXPERT - k, N_EXPERT)


def in_up_block(w, s):
    return w[pl.ds(pl.multiple_of(8 * s, 8), 8), 0:64, :].reshape(SLICE, 2 * H)


def down_block(w, s):
    row = pl.multiple_of(64 + 16 * (s // 2), 16)
    col = pl.multiple_of(SLICE * (s % 2), SLICE)
    return w[:, pl.ds(row, 16), pl.ds(col, SLICE)].reshape(H, SLICE)


def forward(tokens, weights):
    def body(x0, x1, x2, x3, w, hidden_t, gate_factor, act_out, xt, acc, hid):
        for k, x in enumerate((x0, x1, x2, x3)):
            part = jnp.dot(x[0:TOK_DEV, :], in_up_block(w, slice_of(k)), preferred_element_type=F32)
            if k == 0:
                acc[...] = part
            else:
                acc[...] += part
            xt[k] = x[0:TOK_DEV, :].T

        @pl.loop(0, TOK_DEV // 64)
        def _(i):
            rows = pl.ds(pl.multiple_of(i * 64, 64), 64)
            gate, up = acc[rows, :H], acc[rows, H:]
            sig = jax.nn.sigmoid(gate)
            act = gate * sig
            hid[rows, :] = (act * up).astype(BF16)
            gate_factor[rows, :] = up * sig * (1.0 + gate * (1.0 - sig))
            act_out[rows, :] = act

        hidden_t[...] = hid[...].T

    shapes = [
        struct((H, TOK_DEV), BF16),
        struct((TOK_DEV, H), F32),
        struct((TOK_DEV, H), F32),
        struct((N_EXPERT, SLICE, TOK_DEV), BF16),
    ]
    return call(
        body,
        "forward",
        5,
        shapes,
        2 * TOK_DEV * D * 2 * H,
        10 * MIB,
        [pltpu.VMEM((TOK_DEV, 2 * H), F32), pltpu.VMEM((TOK_DEV, H), BF16)],
    )(*tokens, weights)


def of_cotangents(first, ks, cots, route, hid_t, w, hg, scaled, put):
    scale = column(route[...])
    for k, c in zip(ks, cots):
        for j in range(SLICE // 128):
            cols = slice(128 * j, 128 * (j + 1))
            rows = slice(c.shape[0] - TOK_DEV, c.shape[0])
            scaled[:, cols] = (scale * c[rows, cols].astype(F32)).astype(BF16)
        part = lax.dot_general(scaled[...], down_block(w, slice_of(k)), NT, preferred_element_type=F32)
        if first and k == ks[0]:
            hg[...] = part
        else:
            hg[...] += part
        down = jnp.dot(hid_t[...], scaled[...], preferred_element_type=F32) / TOK_DEV
        put(k, down.astype(BF16))


def backward_early(cots, route, hidden_t, weights):
    def body(c0, c2, route_ref, hid_t, w, hg, downs, scaled):
        def put(k, down):
            downs[k // 2] = down

        of_cotangents(True, (0, 2), (c0, c2), route_ref, hid_t, w, hg, scaled, put)

    shapes = [struct((TOK_DEV, H), F32), struct((2, H, SLICE), BF16)]
    scratch = [pltpu.VMEM((TOK_DEV, SLICE), BF16)]
    return call(body, "backward_early", 5, shapes, 2 * TOK_DEV * D * H, 8 * MIB, scratch)(
        *cots, route, hidden_t, weights
    )


def backward_down(cots, route, hidden_t, early, downs, weights):
    def body(c1, c3, route_ref, hid_t, hg0, down_ref, w, keep, send, hg, scaled):
        first = lax.axis_index("dp") % 2 == 0

        def put(k, down):
            down = down.reshape(N_CHIP, 2, 16, SLICE)
            rows = pl.ds(pl.multiple_of(16 * slice_of(k), 16), 16)
            keep[:, rows, :] = jnp.where(first, down[:, 0], down[:, 1])
            send[:, rows, :] = jnp.where(first, down[:, 1], down[:, 0])

        hg[...] = hg0[...]
        of_cotangents(False, (1, 3), (c1, c3), route_ref, hid_t, w, hg, scaled, put)
        put(0, down_ref[0])
        put(2, down_ref[1])

    half = struct((N_CHIP, 64, SLICE), BF16)
    shapes = [half, half, struct((TOK_DEV, H), F32)]
    scratch = [pltpu.VMEM((TOK_DEV, SLICE), BF16)]
    return call(body, "backward_down", 7, shapes, 2 * TOK_DEV * D * H, 10 * MIB, scratch)(
        *cots, route, hidden_t, early, downs, weights
    )


def backward_in(hidden_grad, gate_factor, act, xt):
    def body(hg, factor, act_ref, xt_ref, keep, send, both):
        first = lax.axis_index("dp") % 2 == 0

        @pl.loop(0, TOK_DEV // 64)
        def _(i):
            rows = pl.ds(pl.multiple_of(i * 64, 64), 64)
            g = hg[rows, :]
            both[rows, :H] = (g * factor[rows, :]).astype(BF16)
            both[rows, H:] = (g * act_ref[rows, :]).astype(BF16)

        for k in range(N_EXPERT):
            chips = pl.ds(pl.multiple_of(4 * slice_of(k), 4), 4)
            grad = jnp.dot(xt_ref[k], both[...], preferred_element_type=F32) / TOK_DEV
            grad = grad.astype(BF16).reshape(4, 2, 64, 2 * H)
            for a in range(2):
                own = grad[:, 0, :, a * H : (a + 1) * H]
                other = grad[:, 1, :, a * H : (a + 1) * H]
                keep[chips, 64 * a : 64 * (a + 1), :] = jnp.where(first, own, other)
                send[chips, 64 * a : 64 * (a + 1), :] = jnp.where(first, other, own)

    half = struct((N_CHIP, 128, SLICE), BF16)
    shapes = [half, half, struct((TOK_DEV, 2 * H), BF16)]
    return call(body, "backward_in", 4, shapes, 4 * TOK_DEV * D * H, 10 * MIB)(hidden_grad, gate_factor, act, xt)


def slot_gradients(both, weights):
    def body(both_ref, w, *out):
        for k in (2, 1, 3, 0):
            grad = lax.dot_general(both_ref[...], in_up_block(w, slice_of(k)), NT, preferred_element_type=F32)
            out[k][...] = grad.astype(BF16)

    shapes = [struct((TOK_DEV, SLICE), BF16)] * N_EXPERT
    return call(body, "slot_gradients", 2, shapes, 4 * TOK_DEV * D * H, 9 * MIB)(both, weights)


def rows_of(of_in, of_down, q, m):
    return of_down[q] if m == 2 else of_in[q, 64 * m : 64 * (m + 1), :]


def pair_moments(own, other):
    def body(a_in, a_down, b_in, b_down, out):
        def step(q, sums):
            new = []
            for m in range(3):
                a = rows_of(a_in, a_down, q, m).astype(F32)
                b = rows_of(b_in, b_down, q, m).astype(F32)
                for t in (a * b, a * a, b * b):
                    t = jnp.sum(t.reshape(8, 8, SLICE), axis=0)
                    new.append(t[:, :128] + t[:, 128:256] + t[:, 256:384] + t[:, 384:])
            return tuple(s + n for s, n in zip(sums, new))

        sums = lax.fori_loop(0, N_CHIP, step, (jnp.zeros((8, 128), F32),) * 9)
        for j in range(9):
            out[j] = sums[j]

    return call(body, "pair_moments", 4, struct((9, 8, 128), F32), 9 * 2**20, 6 * MIB)(*own, *other)


def pair_merge(own, other, mine, theirs):
    def body(a_in, a_down, b_in, b_down, m_ref, t_ref, *out):
        coefs = []
        for m in range(3):
            inner = jnp.sum(m_ref[3 * m] + t_ref[3 * m], keepdims=True)
            norm_a = jnp.sum(m_ref[3 * m + 1] + t_ref[3 * m + 2], keepdims=True)
            norm_b = jnp.sum(m_ref[3 * m + 2] + t_ref[3 * m + 1], keepdims=True)
            coef_a = 1.0 - inner / (2.0 * (norm_a + epsilon))
            coef_b = 1.0 - inner / (2.0 * (norm_b + epsilon))
            coefs.append((jnp.broadcast_to(coef_a, (64, SLICE)), jnp.broadcast_to(coef_b, (64, SLICE))))
        c, at = place(0)

        @pl.loop(0, 4)
        def _(j):
            for k in range(4):
                first = lax.rem(at + k, 4)
                q = jnp.where(c == 0, 4 * j + first, 4 * first + j)
                for m in range(3):
                    rows = slice(64 * m, 64 * (m + 1))
                    a = rows_of(a_in, a_down, q, m).astype(F32)
                    b = rows_of(b_in, b_down, q, m).astype(F32)
                    out[k][j, rows, :] = (coefs[m][0] * a + coefs[m][1] * b).astype(BF16)

    return call(body, "pair_merge", 6, [struct((4, ROWS, SLICE), BF16)] * 4, 9 * 2**20, 9 * MIB)(
        *own, *other, mine, theirs
    )


def turn_over(parts):
    def body(*refs):
        (_, first), (_, second) = place(0), place(1)
        for k in range(4):
            for m in range(4):
                refs[4 + k][lax.rem(first + 4 - m, 4)] = refs[m][lax.rem(second + k, 4)]

    return call(body, "turn_over", 4, [struct((4, ROWS, SLICE), BF16)] * 4, 2**10, 6 * MIB)(*parts)


def origin(index):
    c, second = place(1)
    other = (second + 4 - (index >> 2)) & 3
    return jnp.where(c == 0, other * 4 + (index & 3), (index & 3) * 4 + other)


def gram(parts):
    def body(*refs):
        x, out = refs[:4], refs[4]
        row = lax.broadcasted_iota(jnp.int32, (256, 256), 0)
        col = lax.broadcasted_iota(jnp.int32, (256, 256), 1)
        same = jnp.where(row % 16 == col % 16, 1.0, 0.0)
        fold = origin(lax.broadcasted_iota(jnp.int32, (256, 128), 0) // 16)
        fold = jnp.where(fold == lax.broadcasted_iota(jnp.int32, (256, 128), 1), 1.0, 0.0)
        order = origin(lax.broadcasted_iota(jnp.int32, (16, 16), 1))
        order = jnp.where(order == lax.broadcasted_iota(jnp.int32, (16, 16), 0), 1.0, 0.0)
        exact = dict(precision=lax.Precision.HIGHEST, preferred_element_type=F32)
        for m in range(3):
            acc = None
            for b in range(4):
                at = 64 * m + 16 * b
                block = jnp.concatenate([r[:, at : at + 16, :].reshape(64, SLICE) for r in x], axis=0)
                part = lax.dot_general(block, block, NT, preferred_element_type=F32)
                acc = part if acc is None else acc + part
            acc = jnp.sum((acc * same).reshape(16, 16, 256), axis=1)
            out[m] = jnp.dot(order, jnp.dot(acc, fold, **exact), **exact)

    return call(body, "gram", 4, struct((3, 16, 128), F32), 12 * 2 * 256 * 256 * 512, 3 * MIB)(*parts)


def finish(parts, products, gate, up, down, mom_gate, mom_up, mom_down):
    def body(x0, x1, x2, x3, g_ref, gate_w, up_w, down_w, gate_m, up_m, down_m, new_g, new_u, new_d, next_g, next_u, next_d):
        g = g_ref[...]
        i = lax.broadcasted_iota(jnp.int32, (3, 16, 128), 1)
        j = lax.broadcasted_iota(jnp.int32, (3, 16, 128), 2)
        c_col = jnp.ones((3, 16, 1), F32)
        c_row = jnp.ones((3, 1, 128), F32)
        for level in range(4):
            block_i, block_j = i >> level, j >> level
            same, sibling = block_i == block_j, (block_i ^ 1) == block_j
            weighted = g * c_col * c_row
            within = jnp.where(same, weighted, 0.0)
            across = jnp.where(sibling, weighted, 0.0)

            def coef(axis):
                norm = jnp.sum(jnp.where(same, jnp.sum(within, axis=3 - axis, keepdims=True), 0.0), axis=axis, keepdims=True)
                inner = jnp.sum(jnp.where(same, jnp.sum(across, axis=3 - axis, keepdims=True), 0.0), axis=axis, keepdims=True)
                return 1.0 - inner / (2.0 * (jnp.maximum(norm, 0.0) + epsilon))

            c_col, c_row = c_col * coef(2), c_row * coef(1)
        chip = origin(lax.broadcasted_iota(jnp.int32, (16, 128), 0))
        chip = chip == lax.broadcasted_iota(jnp.int32, (16, 128), 1)
        c_col = jnp.sum(jnp.where(chip, c_row, 0.0), axis=2, keepdims=True)
        olds = ((gate_w, gate_m, new_g, next_g), (up_w, up_m, new_u, next_u))
        for m in range(3):
            merged = jnp.zeros((64, SLICE), F32)
            for q in range(16):
                scale = jnp.broadcast_to(c_col[m, q : q + 1, :], (64, SLICE))
                x = (x0, x1, x2, x3)[q // 4]
                merged += scale * x[q % 4, 64 * m : 64 * (m + 1), :].astype(F32)
            if m < 2:
                w, mom, new, after = olds[m]
                step = momentum_decay * mom[...] + merged
                after[...] = step
                new[...] = w[...] - learning_rate * step
            else:
                for k in range(4):
                    cols = slice(SLICE * k, SLICE * (k + 1))
                    step = momentum_decay * down_m[:, cols] + merged[16 * k : 16 * (k + 1), :]
                    next_d[:, cols] = step
                    new_d[:, cols] = down_w[:, cols] - learning_rate * step

    wide, tall = struct((64, H), F32), struct((16, D), F32)
    return call(body, "finish", 11, [wide, wide, tall, wide, wide, tall], 2**22, 6 * MIB)(
        *parts, products, gate, up, down, mom_gate, mom_up, mom_down
    )


def scatter_rows(ids_rows, grads):
    block = 512

    def body(i0, i1, i2, i3, g0, g1, g2, g3, out):
        row = lax.broadcasted_iota(jnp.int32, (block, TOK_DEV), 0) + block * pl.program_id(0)
        acc = None
        for ids, g in zip((i0, i1, i2, i3), (g0, g1, g2, g3)):
            hot = jnp.where(jnp.broadcast_to(ids[...], row.shape) == row, 1.0, 0.0).astype(BF16)
            part = jnp.dot(hot, g[...], preferred_element_type=F32)
            acc = part if acc is None else acc + part
        out[...] = acc

    return pl.pallas_call(
        body,
        name="scatter_rows",
        grid=(POOL // block,),
        out_shape=struct((POOL, SLICE), F32),
        in_specs=[vmem()] * 8,
        out_specs=pl.BlockSpec((block, SLICE), lambda i: (i, 0)),
        compiler_params=pltpu.CompilerParams(vmem_limit_bytes=24 * MIB),
        cost_estimate=pl.CostEstimate(
            flops=2 * POOL * POOL * SLICE, bytes_accessed=6 * MIB, transcendentals=0
        ),
    )(*ids_rows, *grads)


def shift(block, axis, to):
    return lax.ppermute(block, axis, [(i, to(i)) for i in range(lax.axis_size(axis))])


def around_y(block, k):
    return shift(block, "expert", lambda i: (i + k) % N_EXPERT)


def around_z(block, k):
    return shift(block, "dp", lambda i: i // 8 * 8 + (i // 2 % 4 + k) % 4 * 2 + i % 2)


def around_x(block, k):
    return shift(block, "dp", lambda i: (i // 8 + k) % 4 * 8 + i % 8)


def other_core(block):
    return shift(block, "dp", lambda i: i ^ 1)


def sum_dp(value):
    for around in (around_z, around_x):
        value = value + sum(around(value, k) for k in (2, 1, 3))
    return value + other_core(value)


def pack(gate, up, down):
    def body(gate_hbm, up_hbm, down_hbm, out, g, u, d, sems):
        copies = [
            pltpu.make_async_copy(src, dst, sems.at[j])
            for j, (src, dst) in enumerate(((gate_hbm, g), (up_hbm, u), (down_hbm, d)))
        ]
        for copy in copies:
            copy.start()
        for copy in copies:
            copy.wait()
        out[0:64, 0:H] = g[...].astype(BF16)
        out[0:64, H:] = u[...].astype(BF16)
        out[64:80, :] = d[:, : D // 2].astype(BF16)
        out[80:96, :] = d[:, D // 2 :].astype(BF16)

    return pl.pallas_call(
        body,
        name="pack",
        out_shape=struct((96, 1024), BF16),
        in_specs=[pl.BlockSpec(memory_space=pl.ANY)] * 3,
        out_specs=vmem(),
        scratch_shapes=[
            pltpu.VMEM((64, H), F32),
            pltpu.VMEM((64, H), F32),
            pltpu.VMEM((16, D), F32),
            pltpu.SemaphoreType.DMA((3,)),
        ],
        compiler_params=pltpu.CompilerParams(vmem_limit_bytes=8 * MIB),
        cost_estimate=pl.CostEstimate(flops=2**17, bytes_accessed=MIB, transcendentals=0),
    )(gate, up, down)


def along(turn, step):
    def to(i):
        x, z, c = i // 8, i // 2 % 4, i % 2
        return x * 8 + (z + step) % 4 * 2 + c if c == turn else (x + step) % 4 * 8 + z * 2 + c

    return to


def to_others(blocks, turn):
    out = {k: shift(blocks[k], "dp", along(turn, k)) for k in (2, 1, 3)}
    return [out[1], out[2], out[3]]


def tie_far(items, others, last=False):
    order = (3, 1, 2, 0) if last else (2, 1, 3, 0)
    tied, others = lax.optimization_barrier(([items[k] for k in order], others))
    return [tied[order.index(k)] for k in range(4)], others


def spread(block, turn):
    return to_others([block] * 4, turn)


def place(turn):
    at = lax.axis_index("dp")
    x, z, c = at // 8, lax.rem(at // 2, 4), lax.rem(at, 2)
    return c, jnp.where(c == turn, z, x)


def bundle(blocks):
    def body(*refs):
        _, at = place(0)
        for k in range(4):
            refs[4][lax.rem(at + 4 - k, 4)] = refs[k][...]

    return call(body, "bundle", 4, struct((4, 96, 1024), BF16), 2**10, 2 * MIB)(*blocks)


def half_of_weights(bundles):
    def body(*refs):
        c, at = place(1)
        for k in range(4):
            other = lax.rem(at + 4 - k, 4)
            for j in range(4):
                refs[4][jnp.where(c == 0, other * 4 + j, j * 4 + other)] = refs[k][j]

    return call(body, "half_of_weights", 4, struct((N_CHIP, 96, 1024), BF16), 2**10, 6 * MIB)(*bundles)


def whole_weights(own, other):
    def body(a, b, out):
        c = lax.rem(lax.axis_index("dp"), 2)

        @pl.loop(0, N_CHIP)
        def _(q):
            out[2 * q + c] = a[q]
            out[2 * q + 1 - c] = b[q]

    return call(body, "whole_weights", 2, struct((2 * N_CHIP, 96, 1024), BF16), 2**10, 12 * MIB)(own, other)


def local(
    pool_tokens,
    pool_cotangent,
    token_ids,
    route_weights,
    gate_weight,
    up_weight,
    down_weight,
    momentum_gate,
    momentum_up,
    momentum_down,
):
    tie = lax.optimization_barrier

    def picked(k, pool):
        return pick_rows(ids[k : k + 1], [pool])[0]

    ids = [token_ids] + [around_y(token_ids, N_EXPERT - k) for k in (1, 2, 3)]
    x, c = [None] * 4, [None] * 4
    x[1], x[3] = picked(1, pool_tokens), picked(3, pool_tokens)
    ids, x[1], x[3], shards = tie((ids, x[1], x[3], (gate_weight[0], up_weight[0], down_weight[0])))

    packed = pack(*shards)
    blocks = spread(packed, 0)
    x[1], x[3] = around_y(x[1], 1), around_y(x[3], 3)
    (x[2],) = pick_rows(ids[2:3], [pool_tokens, pool_cotangent], stacked=True)
    blocks, (ids, x[1:]) = tie_far([packed, *blocks], (ids, x[1:]), last=True)

    block = bundle(blocks)
    blocks = spread(block, 1)
    x[2] = c[2] = around_y(x[2], 2)
    c[1], c[3] = picked(1, pool_cotangent), picked(3, pool_cotangent)
    x[0], c[0] = pick_rows(ids[:1], [pool_tokens, pool_cotangent])
    blocks, (x, c) = tie_far([block, *blocks], (x, [c[0], c[1], c[3]]), last=True)
    c = [c[0], c[1], x[2], c[2]]

    mine = half_of_weights(blocks)
    weights = whole_weights(mine, other_core(mine))
    c[1], c[3] = around_y(c[1], 1), around_y(c[3], 3)

    hidden_t, gate_factor, act, xt = forward(x, weights)
    early, downs = backward_early((c[0], c[2]), route_weights, hidden_t, weights)
    keep_down, send_down, hidden_grad = backward_down((c[1], c[3]), route_weights, hidden_t, early, downs, weights)
    keep_in, send_in, both = backward_in(hidden_grad, gate_factor, act, xt)
    received_down, send_in = tie((other_core(send_down), send_in))
    keep, received = (keep_in, keep_down), (other_core(send_in), received_down)
    slots = slot_gradients(both, weights)
    received, slots = lax.optimization_barrier((received, list(slots)))

    mine = pair_moments(keep, received)
    sent = pair_merge(keep, received, mine, other_core(mine))
    parts = [sent[0], *to_others(sent, 0)]
    back = [slots[0], around_y(slots[1], 3), None, around_y(slots[3], 1)]
    parts, (back[1], back[3]) = tie_far(parts, (back[1], back[3]))
    sent, slots[2] = tie((turn_over(parts), slots[2]))
    parts = [sent[0], *to_others(sent, 1)]
    back[2] = around_y(slots[2], 2)
    pool_grad = scatter_rows(ids, back)
    parts, pool_grad = tie_far(parts, pool_grad)
    products = sum_dp(gram(parts))
    outs = finish(
        parts,
        products,
        gate_weight[0],
        up_weight[0],
        down_weight[0],
        momentum_gate[0],
        momentum_up[0],
        momentum_down[0],
    )
    return (*(a[None] for a in outs), pool_grad)


def solution(mesh):
    in_specs = (
        P("dp", "expert"),
        P("dp", "expert"),
        P("expert", "dp"),
        P("expert", "dp"),
        P("expert", "dp", None),
        P("expert", "dp", None),
        P("expert", "dp", None),
        P("expert", "dp", None),
        P("expert", "dp", None),
        P("expert", "dp", None),
    )
    out_specs = (
        P("expert", "dp", None),
        P("expert", "dp", None),
        P("expert", "dp", None),
        P("expert", "dp", None),
        P("expert", "dp", None),
        P("expert", "dp", None),
        P("dp", "expert"),
    )
    return jax.shard_map(local, mesh=mesh, in_specs=in_specs, out_specs=out_specs, check_vma=False)
```

```python
import jax
import jax.numpy as jnp
from jax import lax
from jax.experimental import pallas as pl
from jax.experimental.pallas import tpu as pltpu
from jax.sharding import PartitionSpec as P

TOK_DEV = 512
POOL = 2048
D = 2048
H = 512
N_EXPERT = 4
N_CHIP = 16
SLICE = 512
ROWS = 192

momentum_decay = 0.9
learning_rate = 0.05
epsilon = 1e-06

MIB = 1 << 20
F32 = jnp.float32
BF16 = jnp.bfloat16
NT = (((1,), (1,)), ((), ()))


def vmem():
    return pl.BlockSpec(memory_space=pltpu.VMEM)


def call(body, name, n_in, out_shapes, flops, nbytes, scratch=(), limit=20):
    return pl.pallas_call(
        body,
        name=name,
        out_shape=out_shapes,
        in_specs=[vmem()] * n_in,
        out_specs=jax.tree.map(lambda _: vmem(), out_shapes),
        scratch_shapes=list(scratch),
        compiler_params=pltpu.CompilerParams(vmem_limit_bytes=limit * MIB),
        cost_estimate=pl.CostEstimate(flops=flops, bytes_accessed=nbytes, transcendentals=0),
    )


def struct(shape, dtype):
    return jax.ShapeDtypeStruct(shape, dtype)


def column(row):
    return jnp.broadcast_to(row, (128, row.shape[1])).T


def pick_rows(ids_rows, pools, stacked=False):
    n_ids, n_pool = len(ids_rows), len(pools)

    def body(*refs):
        ids, src = refs[:n_ids], refs[n_ids : n_ids + n_pool]
        out, hot = refs[n_ids + n_pool : -1], refs[-1]
        lane = lax.broadcasted_iota(jnp.int32, (TOK_DEV, 128), 1)
        for k in range(n_ids):
            named = column(ids[k][...])
            for j in range(POOL // 128):
                hot[:, 128 * j : 128 * (j + 1)] = jnp.where(named == lane + 128 * j, 1.0, 0.0).astype(BF16)
            for a in range(n_pool):
                rows = jnp.dot(hot[...], src[a][...], preferred_element_type=F32).astype(BF16)
                if stacked:
                    out[k][TOK_DEV * a : TOK_DEV * (a + 1), :] = rows
                else:
                    out[k * n_pool + a][...] = rows

    shapes = [struct((TOK_DEV, SLICE), BF16)] * (n_ids * n_pool)
    if stacked:
        shapes = [struct((n_pool * TOK_DEV, SLICE), BF16)] * n_ids
    return call(
        body,
        "pick_rows",
        n_ids + n_pool,
        shapes,
        2 * TOK_DEV * POOL * SLICE * n_ids * n_pool,
        (4 + 2 * n_ids) * MIB // 2,
        [pltpu.VMEM((TOK_DEV, POOL), BF16)],
    )(*ids_rows, *pools)


def slice_of(k):
    me = lax.axis_index("expert")
    return lax.rem(me + N_EXPERT - k, N_EXPERT)


def in_up_block(w, s):
    return w[pl.ds(pl.multiple_of(8 * s, 8), 8), 0:64, :].reshape(SLICE, 2 * H)


def down_block(w, s):
    row = pl.multiple_of(64 + 16 * (s // 2), 16)
    col = pl.multiple_of(SLICE * (s % 2), SLICE)
    return w[:, pl.ds(row, 16), pl.ds(col, SLICE)].reshape(H, SLICE)


def forward(tokens, weights):
    def body(x0, x1, x2, x3, w, hidden_t, gate_factor, act_out, xt, acc, hid):
        for k, x in enumerate((x0, x1, x2, x3)):
            part = jnp.dot(x[0:TOK_DEV, :], in_up_block(w, slice_of(k)), preferred_element_type=F32)
            if k == 0:
                acc[...] = part
            else:
                acc[...] += part
            xt[k] = x[0:TOK_DEV, :].T

        @pl.loop(0, TOK_DEV // 64)
        def _(i):
            rows = pl.ds(pl.multiple_of(i * 64, 64), 64)
            gate, up = acc[rows, :H], acc[rows, H:]
            sig = jax.nn.sigmoid(gate)
            act = gate * sig
            hid[rows, :] = (act * up).astype(BF16)
            gate_factor[rows, :] = up * sig * (1.0 + gate * (1.0 - sig))
            act_out[rows, :] = act

        hidden_t[...] = hid[...].T

    shapes = [
        struct((H, TOK_DEV), BF16),
        struct((TOK_DEV, H), F32),
        struct((TOK_DEV, H), F32),
        struct((N_EXPERT, SLICE, TOK_DEV), BF16),
    ]
    return call(
        body,
        "forward",
        5,
        shapes,
        2 * TOK_DEV * D * 2 * H,
        10 * MIB,
        [pltpu.VMEM((TOK_DEV, 2 * H), F32), pltpu.VMEM((TOK_DEV, H), BF16)],
    )(*tokens, weights)


def of_cotangents(first, ks, cots, route, hid_t, w, hg, scaled, put):
    scale = column(route[...])
    for k, c in zip(ks, cots):
        for j in range(SLICE // 128):
            cols = slice(128 * j, 128 * (j + 1))
            rows = slice(c.shape[0] - TOK_DEV, c.shape[0])
            scaled[:, cols] = (scale * c[rows, cols].astype(F32)).astype(BF16)
        part = lax.dot_general(scaled[...], down_block(w, slice_of(k)), NT, preferred_element_type=F32)
        if first and k == ks[0]:
            hg[...] = part
        else:
            hg[...] += part
        down = jnp.dot(hid_t[...], scaled[...], preferred_element_type=F32) / TOK_DEV
        put(k, down.astype(BF16))


def backward_early(cots, route, hidden_t, weights):
    def body(c0, c2, route_ref, hid_t, w, hg, downs, scaled):
        def put(k, down):
            downs[k // 2] = down

        of_cotangents(True, (0, 2), (c0, c2), route_ref, hid_t, w, hg, scaled, put)

    shapes = [struct((TOK_DEV, H), F32), struct((2, H, SLICE), BF16)]
    scratch = [pltpu.VMEM((TOK_DEV, SLICE), BF16)]
    return call(body, "backward_early", 5, shapes, 2 * TOK_DEV * D * H, 8 * MIB, scratch)(
        *cots, route, hidden_t, weights
    )


def backward_down(cots, route, hidden_t, early, downs, weights):
    def body(c1, c3, route_ref, hid_t, hg0, down_ref, w, keep, send, hg, scaled):
        first = lax.axis_index("dp") % 2 == 0

        def put(k, down):
            down = down.reshape(N_CHIP, 2, 16, SLICE)
            rows = pl.ds(pl.multiple_of(16 * slice_of(k), 16), 16)
            keep[:, rows, :] = jnp.where(first, down[:, 0], down[:, 1])
            send[:, rows, :] = jnp.where(first, down[:, 1], down[:, 0])

        hg[...] = hg0[...]
        of_cotangents(False, (1, 3), (c1, c3), route_ref, hid_t, w, hg, scaled, put)
        put(0, down_ref[0])
        put(2, down_ref[1])

    half = struct((N_CHIP, 64, SLICE), BF16)
    shapes = [half, half, struct((TOK_DEV, H), F32)]
    scratch = [pltpu.VMEM((TOK_DEV, SLICE), BF16)]
    return call(body, "backward_down", 7, shapes, 2 * TOK_DEV * D * H, 10 * MIB, scratch)(
        *cots, route, hidden_t, early, downs, weights
    )


def backward_in(hidden_grad, gate_factor, act, xt):
    def body(hg, factor, act_ref, xt_ref, keep, send, both):
        first = lax.axis_index("dp") % 2 == 0

        @pl.loop(0, TOK_DEV // 64)
        def _(i):
            rows = pl.ds(pl.multiple_of(i * 64, 64), 64)
            g = hg[rows, :]
            both[rows, :H] = (g * factor[rows, :]).astype(BF16)
            both[rows, H:] = (g * act_ref[rows, :]).astype(BF16)

        for k in range(N_EXPERT):
            chips = pl.ds(pl.multiple_of(4 * slice_of(k), 4), 4)
            grad = jnp.dot(xt_ref[k], both[...], preferred_element_type=F32) / TOK_DEV
            grad = grad.astype(BF16).reshape(4, 2, 64, 2 * H)
            for a in range(2):
                own = grad[:, 0, :, a * H : (a + 1) * H]
                other = grad[:, 1, :, a * H : (a + 1) * H]
                keep[chips, 64 * a : 64 * (a + 1), :] = jnp.where(first, own, other)
                send[chips, 64 * a : 64 * (a + 1), :] = jnp.where(first, other, own)

    half = struct((N_CHIP, 128, SLICE), BF16)
    shapes = [half, half, struct((TOK_DEV, 2 * H), BF16)]
    return call(body, "backward_in", 4, shapes, 4 * TOK_DEV * D * H, 10 * MIB)(hidden_grad, gate_factor, act, xt)


def slot_gradients(both, weights):
    def body(both_ref, w, *out):
        for k in (2, 1, 3, 0):
            grad = lax.dot_general(both_ref[...], in_up_block(w, slice_of(k)), NT, preferred_element_type=F32)
            out[k][...] = grad.astype(BF16)

    shapes = [struct((TOK_DEV, SLICE), BF16)] * N_EXPERT
    return call(body, "slot_gradients", 2, shapes, 4 * TOK_DEV * D * H, 9 * MIB)(both, weights)


def rows_of(of_in, of_down, q, m):
    return of_down[q] if m == 2 else of_in[q, 64 * m : 64 * (m + 1), :]


def pair_moments(own, other):
    def body(a_in, a_down, b_in, b_down, out):
        def step(q, sums):
            new = []
            for m in range(3):
                a = rows_of(a_in, a_down, q, m).astype(F32)
                b = rows_of(b_in, b_down, q, m).astype(F32)
                for t in (a * b, a * a, b * b):
                    t = jnp.sum(t.reshape(8, 8, SLICE), axis=0)
                    new.append(t[:, :128] + t[:, 128:256] + t[:, 256:384] + t[:, 384:])
            return tuple(s + n for s, n in zip(sums, new))

        sums = lax.fori_loop(0, N_CHIP, step, (jnp.zeros((8, 128), F32),) * 9)
        for j in range(9):
            out[j] = sums[j]

    return call(body, "pair_moments", 4, struct((9, 8, 128), F32), 9 * 2**20, 6 * MIB)(*own, *other)


def pair_merge(own, other, mine, theirs):
    def body(a_in, a_down, b_in, b_down, m_ref, t_ref, *out):
        coefs = []
        for m in range(3):
            inner = jnp.sum(m_ref[3 * m] + t_ref[3 * m], keepdims=True)
            norm_a = jnp.sum(m_ref[3 * m + 1] + t_ref[3 * m + 2], keepdims=True)
            norm_b = jnp.sum(m_ref[3 * m + 2] + t_ref[3 * m + 1], keepdims=True)
            coef_a = 1.0 - inner / (2.0 * (norm_a + epsilon))
            coef_b = 1.0 - inner / (2.0 * (norm_b + epsilon))
            coefs.append((jnp.broadcast_to(coef_a, (64, SLICE)), jnp.broadcast_to(coef_b, (64, SLICE))))
        c, at = place(0)

        @pl.loop(0, 4)
        def _(j):
            for k in range(4):
                first = lax.rem(at + k, 4)
                q = jnp.where(c == 0, 4 * j + first, 4 * first + j)
                for m in range(3):
                    rows = slice(64 * m, 64 * (m + 1))
                    a = rows_of(a_in, a_down, q, m).astype(F32)
                    b = rows_of(b_in, b_down, q, m).astype(F32)
                    out[k][j, rows, :] = (coefs[m][0] * a + coefs[m][1] * b).astype(BF16)

    return call(body, "pair_merge", 6, [struct((4, ROWS, SLICE), BF16)] * 4, 9 * 2**20, 9 * MIB)(
        *own, *other, mine, theirs
    )


def turn_over(parts):
    def body(*refs):
        (_, first), (_, second) = place(0), place(1)
        for k in range(4):
            for m in range(4):
                refs[4 + k][lax.rem(first + 4 - m, 4)] = refs[m][lax.rem(second + k, 4)]

    return call(body, "turn_over", 4, [struct((4, ROWS, SLICE), BF16)] * 4, 2**10, 6 * MIB)(*parts)


def origin(index):
    c, second = place(1)
    other = (second + 4 - (index >> 2)) & 3
    return jnp.where(c == 0, other * 4 + (index & 3), (index & 3) * 4 + other)


def gram(parts):
    def body(*refs):
        x, out = refs[:4], refs[4]
        row = lax.broadcasted_iota(jnp.int32, (256, 256), 0)
        col = lax.broadcasted_iota(jnp.int32, (256, 256), 1)
        same = jnp.where(row % 16 == col % 16, 1.0, 0.0)
        fold = origin(lax.broadcasted_iota(jnp.int32, (256, 128), 0) // 16)
        fold = jnp.where(fold == lax.broadcasted_iota(jnp.int32, (256, 128), 1), 1.0, 0.0)
        order = origin(lax.broadcasted_iota(jnp.int32, (16, 16), 1))
        order = jnp.where(order == lax.broadcasted_iota(jnp.int32, (16, 16), 0), 1.0, 0.0)
        exact = dict(precision=lax.Precision.HIGHEST, preferred_element_type=F32)
        for m in range(3):
            acc = None
            for b in range(4):
                at = 64 * m + 16 * b
                block = jnp.concatenate([r[:, at : at + 16, :].reshape(64, SLICE) for r in x], axis=0)
                part = lax.dot_general(block, block, NT, preferred_element_type=F32)
                acc = part if acc is None else acc + part
            acc = jnp.sum((acc * same).reshape(16, 16, 256), axis=1)
            out[m] = jnp.dot(order, jnp.dot(acc, fold, **exact), **exact)

    return call(body, "gram", 4, struct((3, 16, 128), F32), 12 * 2 * 256 * 256 * 512, 3 * MIB)(*parts)


def finish(parts, products, gate, up, down, mom_gate, mom_up, mom_down):
    def body(x0, x1, x2, x3, g_ref, gate_w, up_w, down_w, gate_m, up_m, down_m, new_g, new_u, new_d, next_g, next_u, next_d):
        g = g_ref[...]
        i = lax.broadcasted_iota(jnp.int32, (3, 16, 128), 1)
        j = lax.broadcasted_iota(jnp.int32, (3, 16, 128), 2)
        c_col = jnp.ones((3, 16, 1), F32)
        c_row = jnp.ones((3, 1, 128), F32)
        for level in range(4):
            block_i, block_j = i >> level, j >> level
            same, sibling = block_i == block_j, (block_i ^ 1) == block_j
            weighted = g * c_col * c_row
            within = jnp.where(same, weighted, 0.0)
            across = jnp.where(sibling, weighted, 0.0)

            def coef(axis):
                norm = jnp.sum(jnp.where(same, jnp.sum(within, axis=3 - axis, keepdims=True), 0.0), axis=axis, keepdims=True)
                inner = jnp.sum(jnp.where(same, jnp.sum(across, axis=3 - axis, keepdims=True), 0.0), axis=axis, keepdims=True)
                return 1.0 - inner / (2.0 * (jnp.maximum(norm, 0.0) + epsilon))

            c_col, c_row = c_col * coef(2), c_row * coef(1)
        chip = origin(lax.broadcasted_iota(jnp.int32, (16, 128), 0))
        chip = chip == lax.broadcasted_iota(jnp.int32, (16, 128), 1)
        c_col = jnp.sum(jnp.where(chip, c_row, 0.0), axis=2, keepdims=True)
        olds = ((gate_w, gate_m, new_g, next_g), (up_w, up_m, new_u, next_u))
        for m in range(3):
            merged = jnp.zeros((64, SLICE), F32)
            for q in range(16):
                scale = jnp.broadcast_to(c_col[m, q : q + 1, :], (64, SLICE))
                x = (x0, x1, x2, x3)[q // 4]
                merged += scale * x[q % 4, 64 * m : 64 * (m + 1), :].astype(F32)
            if m < 2:
                w, mom, new, after = olds[m]
                step = momentum_decay * mom[...] + merged
                after[...] = step
                new[...] = w[...] - learning_rate * step
            else:
                for k in range(4):
                    cols = slice(SLICE * k, SLICE * (k + 1))
                    step = momentum_decay * down_m[:, cols] + merged[16 * k : 16 * (k + 1), :]
                    next_d[:, cols] = step
                    new_d[:, cols] = down_w[:, cols] - learning_rate * step

    wide, tall = struct((64, H), F32), struct((16, D), F32)
    return call(body, "finish", 11, [wide, wide, tall, wide, wide, tall], 2**22, 6 * MIB)(
        *parts, products, gate, up, down, mom_gate, mom_up, mom_down
    )


def scatter_rows(ids_rows, grads, half, into=()):
    block, steps = 512, POOL // 1024

    def body(*refs):
        row = lax.broadcasted_iota(jnp.int32, (block, TOK_DEV), 0)
        row += block * (pl.program_id(0) + steps * half)
        acc = None
        for ids, g in zip(refs[:4], refs[4:8]):
            hot = jnp.where(jnp.broadcast_to(ids[...], row.shape) == row, 1.0, 0.0).astype(BF16)
            part = jnp.dot(hot, g[...], preferred_element_type=F32)
            acc = part if acc is None else acc + part
        refs[-1][...] = acc

    return pl.pallas_call(
        body,
        name="scatter_rows",
        grid=(steps,),
        out_shape=struct((POOL, SLICE), F32),
        in_specs=[vmem()] * 8 + [pl.BlockSpec(memory_space=pl.ANY)] * len(into),
        out_specs=pl.BlockSpec((block, SLICE), lambda i: (i + steps * half, 0)),
        input_output_aliases={8: 0} if into else {},
        compiler_params=pltpu.CompilerParams(vmem_limit_bytes=24 * MIB),
        cost_estimate=pl.CostEstimate(flops=POOL * POOL * SLICE, bytes_accessed=4 * MIB, transcendentals=0),
    )(*ids_rows, *grads, *into)


def shift(block, axis, to):
    return lax.ppermute(block, axis, [(i, to(i)) for i in range(lax.axis_size(axis))])


def around_y(block, k):
    return shift(block, "expert", lambda i: (i + k) % N_EXPERT)


def around_z(block, k):
    return shift(block, "dp", lambda i: i // 8 * 8 + (i // 2 % 4 + k) % 4 * 2 + i % 2)


def around_x(block, k):
    return shift(block, "dp", lambda i: (i // 8 + k) % 4 * 8 + i % 8)


def other_core(block):
    return shift(block, "dp", lambda i: i ^ 1)


def sum_dp(value, ids, grads):
    pool = ()
    for half, around in enumerate((around_z, around_x)):
        others = [around(value, k) for k in (1, 3, 2)]
        others, pool = lax.optimization_barrier((others, (scatter_rows(ids, grads, half, pool),)))
        value = value + sum(others)
    return value + other_core(value), pool[0]


def pack(gate, up, down):
    def body(gate_hbm, up_hbm, down_hbm, out, g, u, d, sems):
        copies = [
            pltpu.make_async_copy(src, dst, sems.at[j])
            for j, (src, dst) in enumerate(((gate_hbm, g), (up_hbm, u), (down_hbm, d)))
        ]
        for copy in copies:
            copy.start()
        for copy in copies:
            copy.wait()
        out[0:64, 0:H] = g[...].astype(BF16)
        out[0:64, H:] = u[...].astype(BF16)
        out[64:80, :] = d[:, : D // 2].astype(BF16)
        out[80:96, :] = d[:, D // 2 :].astype(BF16)

    return pl.pallas_call(
        body,
        name="pack",
        out_shape=struct((96, 1024), BF16),
        in_specs=[pl.BlockSpec(memory_space=pl.ANY)] * 3,
        out_specs=vmem(),
        scratch_shapes=[
            pltpu.VMEM((64, H), F32),
            pltpu.VMEM((64, H), F32),
            pltpu.VMEM((16, D), F32),
            pltpu.SemaphoreType.DMA((3,)),
        ],
        compiler_params=pltpu.CompilerParams(vmem_limit_bytes=8 * MIB),
        cost_estimate=pl.CostEstimate(flops=2**17, bytes_accessed=MIB, transcendentals=0),
    )(gate, up, down)


def along(turn, step):
    def to(i):
        x, z, c = i // 8, i // 2 % 4, i % 2
        return x * 8 + (z + step) % 4 * 2 + c if c == turn else (x + step) % 4 * 8 + z * 2 + c

    return to


def to_others(blocks, turn):
    out = {k: shift(blocks[k], "dp", along(turn, k)) for k in (2, 1, 3)}
    return [out[1], out[2], out[3]]


def tie_far(items, others, last=False):
    order = (3, 1, 2, 0) if last else (2, 1, 3, 0)
    tied, others = lax.optimization_barrier(([items[k] for k in order], others))
    return [tied[order.index(k)] for k in range(4)], others


def spread(block, turn):
    return to_others([block] * 4, turn)


def place(turn):
    at = lax.axis_index("dp")
    x, z, c = at // 8, lax.rem(at // 2, 4), lax.rem(at, 2)
    return c, jnp.where(c == turn, z, x)


def bundle(blocks):
    def body(*refs):
        _, at = place(0)
        for k in range(4):
            refs[4][lax.rem(at + 4 - k, 4)] = refs[k][...]

    return call(body, "bundle", 4, struct((4, 96, 1024), BF16), 2**10, 2 * MIB)(*blocks)


def half_of_weights(bundles):
    def body(*refs):
        c, at = place(1)
        for k in range(4):
            other = lax.rem(at + 4 - k, 4)
            for j in range(4):
                refs[4][jnp.where(c == 0, other * 4 + j, j * 4 + other)] = refs[k][j]

    return call(body, "half_of_weights", 4, struct((N_CHIP, 96, 1024), BF16), 2**10, 6 * MIB)(*bundles)


def whole_weights(own, other):
    def body(a, b, out):
        c = lax.rem(lax.axis_index("dp"), 2)

        @pl.loop(0, N_CHIP)
        def _(q):
            out[2 * q + c] = a[q]
            out[2 * q + 1 - c] = b[q]

    return call(body, "whole_weights", 2, struct((2 * N_CHIP, 96, 1024), BF16), 2**10, 12 * MIB)(own, other)


def local(
    pool_tokens,
    pool_cotangent,
    token_ids,
    route_weights,
    gate_weight,
    up_weight,
    down_weight,
    momentum_gate,
    momentum_up,
    momentum_down,
):
    tie = lax.optimization_barrier

    def picked(k, pool):
        return pick_rows(ids[k : k + 1], [pool])[0]

    ids = [token_ids] + [around_y(token_ids, N_EXPERT - k) for k in (1, 2, 3)]
    x, c = [None] * 4, [None] * 4
    x[1], x[3] = picked(1, pool_tokens), picked(3, pool_tokens)
    ids, x[1], x[3], shards = tie((ids, x[1], x[3], (gate_weight[0], up_weight[0], down_weight[0])))

    packed = pack(*shards)
    blocks = spread(packed, 0)
    x[1], x[3] = around_y(x[1], 1), around_y(x[3], 3)
    (x[2],) = pick_rows(ids[2:3], [pool_tokens, pool_cotangent], stacked=True)
    blocks, (ids, x[1:]) = tie_far([packed, *blocks], (ids, x[1:]), last=True)

    block = bundle(blocks)
    blocks = spread(block, 1)
    x[2] = c[2] = around_y(x[2], 2)
    c[1], c[3] = picked(1, pool_cotangent), picked(3, pool_cotangent)
    x[0], c[0] = pick_rows(ids[:1], [pool_tokens, pool_cotangent])
    blocks, (x, c) = tie_far([block, *blocks], (x, [c[0], c[1], c[3]]), last=True)
    c = [c[0], c[1], x[2], c[2]]

    mine = half_of_weights(blocks)
    weights = whole_weights(mine, other_core(mine))
    c[1], c[3] = around_y(c[1], 1), around_y(c[3], 3)

    hidden_t, gate_factor, act, xt = forward(x, weights)
    early, downs = backward_early((c[0], c[2]), route_weights, hidden_t, weights)
    keep_down, send_down, hidden_grad = backward_down((c[1], c[3]), route_weights, hidden_t, early, downs, weights)
    keep_in, send_in, both = backward_in(hidden_grad, gate_factor, act, xt)
    received_down, send_in = tie((other_core(send_down), send_in))
    keep, received = (keep_in, keep_down), (other_core(send_in), received_down)
    slots = slot_gradients(both, weights)
    received, slots = lax.optimization_barrier((received, list(slots)))

    mine = pair_moments(keep, received)
    sent = pair_merge(keep, received, mine, other_core(mine))
    parts = [sent[0], *to_others(sent, 0)]
    back = [slots[0], around_y(slots[1], 3), None, around_y(slots[3], 1)]
    parts, (back[1], back[3]) = tie_far(parts, (back[1], back[3]))
    sent, slots[2] = tie((turn_over(parts), slots[2]))
    parts = [sent[0], *to_others(sent, 1)]
    back[2] = around_y(slots[2], 2)
    parts, back[2] = tie_far(parts, back[2])
    products, pool_grad = sum_dp(gram(parts), ids, back)
    outs = finish(
        parts,
        products,
        gate_weight[0],
        up_weight[0],
        down_weight[0],
        momentum_gate[0],
        momentum_up[0],
        momentum_down[0],
    )
    return (*(a[None] for a in outs), pool_grad)


def solution(mesh):
    in_specs = (
        P("dp", "expert"),
        P("dp", "expert"),
        P("expert", "dp"),
        P("expert", "dp"),
        P("expert", "dp", None),
        P("expert", "dp", None),
        P("expert", "dp", None),
        P("expert", "dp", None),
        P("expert", "dp", None),
        P("expert", "dp", None),
    )
    out_specs = (
        P("expert", "dp", None),
        P("expert", "dp", None),
        P("expert", "dp", None),
        P("expert", "dp", None),
        P("expert", "dp", None),
        P("expert", "dp", None),
        P("dp", "expert"),
    )
    return jax.shard_map(local, mesh=mesh, in_specs=in_specs, out_specs=out_specs, check_vma=False)
```

```python
import jax
import jax.numpy as jnp
from jax import lax
from jax.experimental import pallas as pl
from jax.experimental.pallas import tpu as pltpu
from jax.sharding import PartitionSpec as P

TOK_DEV = 512
POOL = 2048
D = 2048
H = 512
N_EXPERT = 4
N_CHIP = 16
SLICE = 512
ROWS = 192

momentum_decay = 0.9
learning_rate = 0.05
epsilon = 1e-06

MIB = 1 << 20
F32 = jnp.float32
BF16 = jnp.bfloat16
NT = (((1,), (1,)), ((), ()))


def vmem():
    return pl.BlockSpec(memory_space=pltpu.VMEM)


def call(body, name, n_in, out_shapes, flops, nbytes, scratch=(), limit=20):
    return pl.pallas_call(
        body,
        name=name,
        out_shape=out_shapes,
        in_specs=[vmem()] * n_in,
        out_specs=jax.tree.map(lambda _: vmem(), out_shapes),
        scratch_shapes=list(scratch),
        compiler_params=pltpu.CompilerParams(vmem_limit_bytes=limit * MIB),
        cost_estimate=pl.CostEstimate(flops=flops, bytes_accessed=nbytes, transcendentals=0),
    )


def struct(shape, dtype):
    return jax.ShapeDtypeStruct(shape, dtype)


def column(row):
    return jnp.broadcast_to(row, (128, row.shape[1])).T


def pick_rows(ids_rows, pools, stacked=False):
    n_ids, n_pool = len(ids_rows), len(pools)

    def body(*refs):
        ids, src = refs[:n_ids], refs[n_ids : n_ids + n_pool]
        out, hot = refs[n_ids + n_pool : -1], refs[-1]
        lane = lax.broadcasted_iota(jnp.int32, (TOK_DEV, 128), 1)
        for k in range(n_ids):
            named = column(ids[k][...])
            for j in range(POOL // 128):
                hot[:, 128 * j : 128 * (j + 1)] = jnp.where(named == lane + 128 * j, 1.0, 0.0).astype(BF16)
            for a in range(n_pool):
                rows = jnp.dot(hot[...], src[a][...], preferred_element_type=F32).astype(BF16)
                if stacked:
                    out[k][TOK_DEV * a : TOK_DEV * (a + 1), :] = rows
                else:
                    out[k * n_pool + a][...] = rows

    shapes = [struct((TOK_DEV, SLICE), BF16)] * (n_ids * n_pool)
    if stacked:
        shapes = [struct((n_pool * TOK_DEV, SLICE), BF16)] * n_ids
    return call(
        body,
        "pick_rows",
        n_ids + n_pool,
        shapes,
        2 * TOK_DEV * POOL * SLICE * n_ids * n_pool,
        (4 + 2 * n_ids) * MIB // 2,
        [pltpu.VMEM((TOK_DEV, POOL), BF16)],
    )(*ids_rows, *pools)


def pick_two(ids_a, ids_b, pool):
    block = 512

    def body(a_ref, b_ref, src, out_a, out_b, hot, acc, named):
        i = pl.program_id(0)
        both = slice(0, TOK_DEV), slice(TOK_DEV, 2 * TOK_DEV)

        @pl.when(i == 0)
        def _():
            for rows, ids in zip(both, (a_ref, b_ref)):
                named[rows, :] = column(ids[...])

        lane = lax.broadcasted_iota(jnp.int32, (2 * TOK_DEV, 128), 1) + block * i
        for j in range(block // 128):
            hot[:, 128 * j : 128 * (j + 1)] = jnp.where(named[...] == lane + 128 * j, 1.0, 0.0).astype(BF16)
        part = jnp.dot(hot[...], src[...], preferred_element_type=F32)

        @pl.when(i == 0)
        def _():
            acc[...] = part

        @pl.when(i > 0)
        def _():
            acc[...] += part

        @pl.when(i == POOL // block - 1)
        def _():
            for rows, out in zip(both, (out_a, out_b)):
                out[...] = acc[rows, :].astype(BF16)

    return pl.pallas_call(
        body,
        name="pick_two",
        grid=(POOL // block,),
        out_shape=[struct((TOK_DEV, SLICE), BF16)] * 2,
        in_specs=[vmem(), vmem(), pl.BlockSpec((block, SLICE), lambda i: (i, 0))],
        out_specs=[vmem(), vmem()],
        scratch_shapes=[
            pltpu.VMEM((2 * TOK_DEV, block), BF16),
            pltpu.VMEM((2 * TOK_DEV, SLICE), F32),
            pltpu.VMEM((2 * TOK_DEV, 128), jnp.int32),
        ],
        compiler_params=pltpu.CompilerParams(vmem_limit_bytes=20 * MIB),
        cost_estimate=pl.CostEstimate(flops=4 * TOK_DEV * POOL * SLICE, bytes_accessed=3 * MIB, transcendentals=0),
    )(ids_a, ids_b, pltpu.with_memory_space_constraint(pool, pltpu.HBM))


def slice_of(k):
    me = lax.axis_index("expert")
    return lax.rem(me + N_EXPERT - k, N_EXPERT)


def in_up_block(w, s):
    return w[pl.ds(pl.multiple_of(8 * s, 8), 8), 0:64, :].reshape(SLICE, 2 * H)


def down_block(w, s):
    row = pl.multiple_of(64 + 16 * (s // 2), 16)
    col = pl.multiple_of(SLICE * (s % 2), SLICE)
    return w[:, pl.ds(row, 16), pl.ds(col, SLICE)].reshape(H, SLICE)


def forward(tokens, weights):
    def body(x0, x1, x2, x3, w, hidden_t, gate_factor, act_out, xt, acc, hid):
        for k, x in enumerate((x0, x1, x2, x3)):
            part = jnp.dot(x[0:TOK_DEV, :], in_up_block(w, slice_of(k)), preferred_element_type=F32)
            if k == 0:
                acc[...] = part
            else:
                acc[...] += part
            xt[k] = x[0:TOK_DEV, :].T

        @pl.loop(0, TOK_DEV // 64)
        def _(i):
            rows = pl.ds(pl.multiple_of(i * 64, 64), 64)
            gate, up = acc[rows, :H], acc[rows, H:]
            sig = jax.nn.sigmoid(gate)
            act = gate * sig
            hid[rows, :] = (act * up).astype(BF16)
            gate_factor[rows, :] = up * sig * (1.0 + gate * (1.0 - sig))
            act_out[rows, :] = act

        hidden_t[...] = hid[...].T

    shapes = [
        struct((H, TOK_DEV), BF16),
        struct((TOK_DEV, H), F32),
        struct((TOK_DEV, H), F32),
        struct((N_EXPERT, SLICE, TOK_DEV), BF16),
    ]
    return call(
        body,
        "forward",
        5,
        shapes,
        2 * TOK_DEV * D * 2 * H,
        10 * MIB,
        [pltpu.VMEM((TOK_DEV, 2 * H), F32), pltpu.VMEM((TOK_DEV, H), BF16)],
    )(*tokens, weights)


def of_cotangents(first, ks, cots, route, hid_t, w, hg, scaled, put):
    scale = column(route[...])
    for k, c in zip(ks, cots):
        for j in range(SLICE // 128):
            cols = slice(128 * j, 128 * (j + 1))
            rows = slice(c.shape[0] - TOK_DEV, c.shape[0])
            scaled[:, cols] = (scale * c[rows, cols].astype(F32)).astype(BF16)
        part = lax.dot_general(scaled[...], down_block(w, slice_of(k)), NT, preferred_element_type=F32)
        if first and k == ks[0]:
            hg[...] = part
        else:
            hg[...] += part
        down = jnp.dot(hid_t[...], scaled[...], preferred_element_type=F32) / TOK_DEV
        put(k, down.astype(BF16))


def backward_early(cots, route, hidden_t, weights):
    def body(c0, c2, route_ref, hid_t, w, hg, downs, scaled):
        def put(k, down):
            downs[k // 2] = down

        of_cotangents(True, (0, 2), (c0, c2), route_ref, hid_t, w, hg, scaled, put)

    shapes = [struct((TOK_DEV, H), F32), struct((2, H, SLICE), BF16)]
    scratch = [pltpu.VMEM((TOK_DEV, SLICE), BF16)]
    return call(body, "backward_early", 5, shapes, 2 * TOK_DEV * D * H, 8 * MIB, scratch)(
        *cots, route, hidden_t, weights
    )


def backward_down(cots, route, hidden_t, early, downs, weights):
    def body(c1, c3, route_ref, hid_t, hg0, down_ref, w, keep, send, hg, scaled):
        first = lax.axis_index("dp") % 2 == 0

        def put(k, down):
            down = down.reshape(N_CHIP, 2, 16, SLICE)
            rows = pl.ds(pl.multiple_of(16 * slice_of(k), 16), 16)
            keep[:, rows, :] = jnp.where(first, down[:, 0], down[:, 1])
            send[:, rows, :] = jnp.where(first, down[:, 1], down[:, 0])

        hg[...] = hg0[...]
        of_cotangents(False, (1, 3), (c1, c3), route_ref, hid_t, w, hg, scaled, put)
        put(0, down_ref[0])
        put(2, down_ref[1])

    half = struct((N_CHIP, 64, SLICE), BF16)
    shapes = [half, half, struct((TOK_DEV, H), F32)]
    scratch = [pltpu.VMEM((TOK_DEV, SLICE), BF16)]
    return call(body, "backward_down", 7, shapes, 2 * TOK_DEV * D * H, 10 * MIB, scratch)(
        *cots, route, hidden_t, early, downs, weights
    )


def backward_in(hidden_grad, gate_factor, act, xt):
    def body(hg, factor, act_ref, xt_ref, keep, send, both):
        first = lax.axis_index("dp") % 2 == 0

        @pl.loop(0, TOK_DEV // 64)
        def _(i):
            rows = pl.ds(pl.multiple_of(i * 64, 64), 64)
            g = hg[rows, :]
            both[rows, :H] = (g * factor[rows, :]).astype(BF16)
            both[rows, H:] = (g * act_ref[rows, :]).astype(BF16)

        for k in range(N_EXPERT):
            chips = pl.ds(pl.multiple_of(4 * slice_of(k), 4), 4)
            grad = jnp.dot(xt_ref[k], both[...], preferred_element_type=F32) / TOK_DEV
            grad = grad.astype(BF16).reshape(4, 2, 64, 2 * H)
            for a in range(2):
                own = grad[:, 0, :, a * H : (a + 1) * H]
                other = grad[:, 1, :, a * H : (a + 1) * H]
                keep[chips, 64 * a : 64 * (a + 1), :] = jnp.where(first, own, other)
                send[chips, 64 * a : 64 * (a + 1), :] = jnp.where(first, other, own)

    half = struct((N_CHIP, 128, SLICE), BF16)
    shapes = [half, half, struct((TOK_DEV, 2 * H), BF16)]
    return call(body, "backward_in", 4, shapes, 4 * TOK_DEV * D * H, 10 * MIB)(hidden_grad, gate_factor, act, xt)


def slot_gradients(both, weights):
    def body(both_ref, w, *out):
        for k in (2, 1, 3, 0):
            grad = lax.dot_general(both_ref[...], in_up_block(w, slice_of(k)), NT, preferred_element_type=F32)
            out[k][...] = grad.astype(BF16)

    shapes = [struct((TOK_DEV, SLICE), BF16)] * N_EXPERT
    return call(body, "slot_gradients", 2, shapes, 4 * TOK_DEV * D * H, 9 * MIB)(both, weights)


def rows_of(of_in, of_down, q, m):
    return of_down[q] if m == 2 else of_in[q, 64 * m : 64 * (m + 1), :]


def pair_moments(own, other):
    def body(a_in, a_down, b_in, b_down, out):
        def step(q, sums):
            new = []
            for m in range(3):
                a = rows_of(a_in, a_down, q, m).astype(F32)
                b = rows_of(b_in, b_down, q, m).astype(F32)
                for t in (a * b, a * a, b * b):
                    t = jnp.sum(t.reshape(8, 8, SLICE), axis=0)
                    new.append(t[:, :128] + t[:, 128:256] + t[:, 256:384] + t[:, 384:])
            return tuple(s + n for s, n in zip(sums, new))

        sums = lax.fori_loop(0, N_CHIP, step, (jnp.zeros((8, 128), F32),) * 9)
        for j in range(9):
            out[j] = sums[j]

    return call(body, "pair_moments", 4, struct((9, 8, 128), F32), 9 * 2**20, 6 * MIB)(*own, *other)


def pair_merge(own, other, mine, theirs):
    def body(a_in, a_down, b_in, b_down, m_ref, t_ref, *out):
        coefs = []
        for m in range(3):
            inner = jnp.sum(m_ref[3 * m] + t_ref[3 * m], keepdims=True)
            norm_a = jnp.sum(m_ref[3 * m + 1] + t_ref[3 * m + 2], keepdims=True)
            norm_b = jnp.sum(m_ref[3 * m + 2] + t_ref[3 * m + 1], keepdims=True)
            coef_a = 1.0 - inner / (2.0 * (norm_a + epsilon))
            coef_b = 1.0 - inner / (2.0 * (norm_b + epsilon))
            coefs.append((jnp.broadcast_to(coef_a, (64, SLICE)), jnp.broadcast_to(coef_b, (64, SLICE))))
        c, at = place(0)

        @pl.loop(0, 4)
        def _(j):
            for k in range(4):
                first = lax.rem(at + k, 4)
                q = jnp.where(c == 0, 4 * j + first, 4 * first + j)
                for m in range(3):
                    rows = slice(64 * m, 64 * (m + 1))
                    a = rows_of(a_in, a_down, q, m).astype(F32)
                    b = rows_of(b_in, b_down, q, m).astype(F32)
                    out[k][j, rows, :] = (coefs[m][0] * a + coefs[m][1] * b).astype(BF16)

    return call(body, "pair_merge", 6, [struct((4, ROWS, SLICE), BF16)] * 4, 9 * 2**20, 9 * MIB)(
        *own, *other, mine, theirs
    )


def turn_over(parts):
    def body(*refs):
        (_, first), (_, second) = place(0), place(1)
        for k in range(4):
            for m in range(4):
                refs[4 + k][lax.rem(first + 4 - m, 4)] = refs[m][lax.rem(second + k, 4)]

    return call(body, "turn_over", 4, [struct((4, ROWS, SLICE), BF16)] * 4, 2**10, 6 * MIB)(*parts)


def origin(index):
    c, second = place(1)
    other = (second + 4 - (index >> 2)) & 3
    return jnp.where(c == 0, other * 4 + (index & 3), (index & 3) * 4 + other)


def gram(parts):
    def body(*refs):
        x, out = refs[:4], refs[4]
        row = lax.broadcasted_iota(jnp.int32, (256, 256), 0)
        col = lax.broadcasted_iota(jnp.int32, (256, 256), 1)
        same = jnp.where(row % 16 == col % 16, 1.0, 0.0)
        fold = origin(lax.broadcasted_iota(jnp.int32, (256, 128), 0) // 16)
        fold = jnp.where(fold == lax.broadcasted_iota(jnp.int32, (256, 128), 1), 1.0, 0.0)
        order = origin(lax.broadcasted_iota(jnp.int32, (16, 16), 1))
        order = jnp.where(order == lax.broadcasted_iota(jnp.int32, (16, 16), 0), 1.0, 0.0)
        exact = dict(precision=lax.Precision.HIGHEST, preferred_element_type=F32)
        for m in range(3):
            acc = None
            for b in range(4):
                at = 64 * m + 16 * b
                block = jnp.concatenate([r[:, at : at + 16, :].reshape(64, SLICE) for r in x], axis=0)
                part = lax.dot_general(block, block, NT, preferred_element_type=F32)
                acc = part if acc is None else acc + part
            acc = jnp.sum((acc * same).reshape(16, 16, 256), axis=1)
            out[m] = jnp.dot(order, jnp.dot(acc, fold, **exact), **exact)

    return call(body, "gram", 4, struct((3, 16, 128), F32), 12 * 2 * 256 * 256 * 512, 3 * MIB)(*parts)


def finish(parts, products, gate, up, down, mom_gate, mom_up, mom_down):
    def body(x0, x1, x2, x3, g_ref, gate_w, up_w, down_w, gate_m, up_m, down_m, new_g, new_u, new_d, next_g, next_u, next_d):
        g = g_ref[...]
        i = lax.broadcasted_iota(jnp.int32, (3, 16, 128), 1)
        j = lax.broadcasted_iota(jnp.int32, (3, 16, 128), 2)
        c_col = jnp.ones((3, 16, 1), F32)
        c_row = jnp.ones((3, 1, 128), F32)
        for level in range(4):
            block_i, block_j = i >> level, j >> level
            same, sibling = block_i == block_j, (block_i ^ 1) == block_j
            weighted = g * c_col * c_row
            within = jnp.where(same, weighted, 0.0)
            across = jnp.where(sibling, weighted, 0.0)

            def coef(axis):
                norm = jnp.sum(jnp.where(same, jnp.sum(within, axis=3 - axis, keepdims=True), 0.0), axis=axis, keepdims=True)
                inner = jnp.sum(jnp.where(same, jnp.sum(across, axis=3 - axis, keepdims=True), 0.0), axis=axis, keepdims=True)
                return 1.0 - inner / (2.0 * (jnp.maximum(norm, 0.0) + epsilon))

            c_col, c_row = c_col * coef(2), c_row * coef(1)
        chip = origin(lax.broadcasted_iota(jnp.int32, (16, 128), 0))
        chip = chip == lax.broadcasted_iota(jnp.int32, (16, 128), 1)
        c_col = jnp.sum(jnp.where(chip, c_row, 0.0), axis=2, keepdims=True)
        olds = ((gate_w, gate_m, new_g, next_g), (up_w, up_m, new_u, next_u))
        for m in range(3):
            merged = jnp.zeros((64, SLICE), F32)
            for q in range(16):
                scale = jnp.broadcast_to(c_col[m, q : q + 1, :], (64, SLICE))
                x = (x0, x1, x2, x3)[q // 4]
                merged += scale * x[q % 4, 64 * m : 64 * (m + 1), :].astype(F32)
            if m < 2:
                w, mom, new, after = olds[m]
                step = momentum_decay * mom[...] + merged
                after[...] = step
                new[...] = w[...] - learning_rate * step
            else:
                for k in range(4):
                    cols = slice(SLICE * k, SLICE * (k + 1))
                    step = momentum_decay * down_m[:, cols] + merged[16 * k : 16 * (k + 1), :]
                    next_d[:, cols] = step
                    new_d[:, cols] = down_w[:, cols] - learning_rate * step

    wide, tall = struct((64, H), F32), struct((16, D), F32)
    return call(body, "finish", 11, [wide, wide, tall, wide, wide, tall], 2**22, 6 * MIB)(
        *parts, products, gate, up, down, mom_gate, mom_up, mom_down
    )


def scatter_rows(ids_rows, grads, half, into=()):
    block, steps = 512, POOL // 1024

    def body(*refs):
        row = lax.broadcasted_iota(jnp.int32, (block, TOK_DEV), 0)
        row += block * (pl.program_id(0) + steps * half)
        acc = None
        for ids, g in zip(refs[:4], refs[4:8]):
            hot = jnp.where(jnp.broadcast_to(ids[...], row.shape) == row, 1.0, 0.0).astype(BF16)
            part = jnp.dot(hot, g[...], preferred_element_type=F32)
            acc = part if acc is None else acc + part
        refs[-1][...] = acc

    return pl.pallas_call(
        body,
        name="scatter_rows",
        grid=(steps,),
        out_shape=struct((POOL, SLICE), F32),
        in_specs=[vmem()] * 8 + [pl.BlockSpec(memory_space=pl.ANY)] * len(into),
        out_specs=pl.BlockSpec((block, SLICE), lambda i: (i + steps * half, 0)),
        input_output_aliases={8: 0} if into else {},
        compiler_params=pltpu.CompilerParams(vmem_limit_bytes=24 * MIB),
        cost_estimate=pl.CostEstimate(flops=POOL * POOL * SLICE, bytes_accessed=4 * MIB, transcendentals=0),
    )(*ids_rows, *grads, *into)


def shift(block, axis, to):
    return lax.ppermute(block, axis, [(i, to(i)) for i in range(lax.axis_size(axis))])


def around_y(block, k):
    return shift(block, "expert", lambda i: (i + k) % N_EXPERT)


def around_z(block, k):
    return shift(block, "dp", lambda i: i // 8 * 8 + (i // 2 % 4 + k) % 4 * 2 + i % 2)


def around_x(block, k):
    return shift(block, "dp", lambda i: (i // 8 + k) % 4 * 8 + i % 8)


def other_core(block):
    return shift(block, "dp", lambda i: i ^ 1)


def sum_dp(value, ids, grads):
    pool = ()
    for half, around in enumerate((around_z, around_x)):
        others = [around(value, k) for k in (1, 3, 2)]
        others, pool = lax.optimization_barrier((others, (scatter_rows(ids, grads, half, pool),)))
        value = value + sum(others)
    return value + other_core(value), pool[0]


def pack(gate, up, down):
    def body(gate_hbm, up_hbm, down_hbm, out, g, u, d, sems):
        copies = [
            pltpu.make_async_copy(src, dst, sems.at[j])
            for j, (src, dst) in enumerate(((gate_hbm, g), (up_hbm, u), (down_hbm, d)))
        ]
        for copy in copies:
            copy.start()
        for copy in copies:
            copy.wait()
        out[0:64, 0:H] = g[...].astype(BF16)
        out[0:64, H:] = u[...].astype(BF16)
        out[64:80, :] = d[:, : D // 2].astype(BF16)
        out[80:96, :] = d[:, D // 2 :].astype(BF16)

    return pl.pallas_call(
        body,
        name="pack",
        out_shape=struct((96, 1024), BF16),
        in_specs=[pl.BlockSpec(memory_space=pl.ANY)] * 3,
        out_specs=vmem(),
        scratch_shapes=[
            pltpu.VMEM((64, H), F32),
            pltpu.VMEM((64, H), F32),
            pltpu.VMEM((16, D), F32),
            pltpu.SemaphoreType.DMA((3,)),
        ],
        compiler_params=pltpu.CompilerParams(vmem_limit_bytes=8 * MIB),
        cost_estimate=pl.CostEstimate(flops=2**17, bytes_accessed=MIB, transcendentals=0),
    )(gate, up, down)


def along(turn, step):
    def to(i):
        x, z, c = i // 8, i // 2 % 4, i % 2
        return x * 8 + (z + step) % 4 * 2 + c if c == turn else (x + step) % 4 * 8 + z * 2 + c

    return to


def to_others(blocks, turn):
    out = {k: shift(blocks[k], "dp", along(turn, k)) for k in (2, 1, 3)}
    return [out[1], out[2], out[3]]


def tie_in_order(items, others, last=False):
    order = (3, 1, 2, 0) if last else (1, 3, 2, 0)
    tied, others = lax.optimization_barrier(([items[k] for k in order], others))
    return [tied[order.index(k)] for k in range(4)], others


def spread(block, turn):
    return to_others([block] * 4, turn)


def place(turn):
    at = lax.axis_index("dp")
    x, z, c = at // 8, lax.rem(at // 2, 4), lax.rem(at, 2)
    return c, jnp.where(c == turn, z, x)


def bundle(blocks):
    def body(*refs):
        _, at = place(0)
        for k in range(4):
            refs[4][lax.rem(at + 4 - k, 4)] = refs[k][...]

    return call(body, "bundle", 4, struct((4, 96, 1024), BF16), 2**10, 2 * MIB)(*blocks)


def half_of_weights(bundles):
    def body(*refs):
        c, at = place(1)
        for k in range(4):
            other = lax.rem(at + 4 - k, 4)
            for j in range(4):
                refs[4][jnp.where(c == 0, other * 4 + j, j * 4 + other)] = refs[k][j]

    return call(body, "half_of_weights", 4, struct((N_CHIP, 96, 1024), BF16), 2**10, 6 * MIB)(*bundles)


def whole_weights(own, other):
    def body(a, b, out):
        c = lax.rem(lax.axis_index("dp"), 2)

        @pl.loop(0, N_CHIP)
        def _(q):
            out[2 * q + c] = a[q]
            out[2 * q + 1 - c] = b[q]

    return call(body, "whole_weights", 2, struct((2 * N_CHIP, 96, 1024), BF16), 2**10, 12 * MIB)(own, other)


def local(
    pool_tokens,
    pool_cotangent,
    token_ids,
    route_weights,
    gate_weight,
    up_weight,
    down_weight,
    momentum_gate,
    momentum_up,
    momentum_down,
):
    tie = lax.optimization_barrier

    def picked(k, pool):
        return pick_rows(ids[k : k + 1], [pool])[0]

    ids = [token_ids] + [around_y(token_ids, N_EXPERT - k) for k in (1, 2, 3)]
    x, c = [None] * 4, [None] * 4
    x[1], x[3] = pick_two(ids[1], ids[3], pool_tokens)
    ids, x[1], x[3], shards = tie((ids, x[1], x[3], (gate_weight[0], up_weight[0], down_weight[0])))

    packed = pack(*shards)
    blocks = spread(packed, 0)
    x[1], x[3] = around_y(x[1], 1), around_y(x[3], 3)
    (x[2],) = pick_rows(ids[2:3], [pool_tokens, pool_cotangent], stacked=True)
    blocks, (ids, x[1:]) = tie_in_order([packed, *blocks], (ids, x[1:]), last=True)

    block = bundle(blocks)
    blocks = spread(block, 1)
    x[2] = c[2] = around_y(x[2], 2)
    c[1], c[3] = picked(1, pool_cotangent), picked(3, pool_cotangent)
    x[0], c[0] = pick_rows(ids[:1], [pool_tokens, pool_cotangent])
    blocks, (x, c) = tie_in_order([block, *blocks], (x, [c[0], c[1], c[3]]), last=True)
    c = [c[0], c[1], x[2], c[2]]

    mine = half_of_weights(blocks)
    weights = whole_weights(mine, other_core(mine))
    c[1], c[3] = around_y(c[1], 1), around_y(c[3], 3)

    hidden_t, gate_factor, act, xt = forward(x, weights)
    early, downs = backward_early((c[0], c[2]), route_weights, hidden_t, weights)
    keep_down, send_down, hidden_grad = backward_down((c[1], c[3]), route_weights, hidden_t, early, downs, weights)
    keep_in, send_in, both = backward_in(hidden_grad, gate_factor, act, xt)
    received_down, send_in = tie((other_core(send_down), send_in))
    keep, received = (keep_in, keep_down), (other_core(send_in), received_down)
    slots = slot_gradients(both, weights)
    received, slots = lax.optimization_barrier((received, list(slots)))

    mine = pair_moments(keep, received)
    sent = pair_merge(keep, received, mine, other_core(mine))
    parts = [sent[0], *to_others(sent, 0)]
    back = [slots[0], around_y(slots[1], 3), None, around_y(slots[3], 1)]
    parts, (back[1], back[3]) = tie_in_order(parts, (back[1], back[3]))
    sent, slots[2] = tie((turn_over(parts), slots[2]))
    parts = [sent[0], *to_others(sent, 1)]
    back[2] = around_y(slots[2], 2)
    parts, back[2] = tie_in_order(parts, back[2])
    products, pool_grad = sum_dp(gram(parts), ids, back)
    outs = finish(
        parts,
        products,
        gate_weight[0],
        up_weight[0],
        down_weight[0],
        momentum_gate[0],
        momentum_up[0],
        momentum_down[0],
    )
    return (*(a[None] for a in outs), pool_grad)


def solution(mesh):
    in_specs = (
        P("dp", "expert"),
        P("dp", "expert"),
        P("expert", "dp"),
        P("expert", "dp"),
        P("expert", "dp", None),
        P("expert", "dp", None),
        P("expert", "dp", None),
        P("expert", "dp", None),
        P("expert", "dp", None),
        P("expert", "dp", None),
    )
    out_specs = (
        P("expert", "dp", None),
        P("expert", "dp", None),
        P("expert", "dp", None),
        P("expert", "dp", None),
        P("expert", "dp", None),
        P("expert", "dp", None),
        P("dp", "expert"),
    )
    return jax.shard_map(local, mesh=mesh, in_specs=in_specs, out_specs=out_specs, check_vma=False)
```

```python
import jax
import jax.numpy as jnp
from jax import lax
from jax.experimental import pallas as pl
from jax.experimental.pallas import tpu as pltpu
from jax.sharding import PartitionSpec as P

TOK_DEV = 512
POOL = 2048
D = 2048
H = 512
N_EXPERT = 4
N_CHIP = 16
SLICE = 512
ROWS = 192

momentum_decay = 0.9
learning_rate = 0.05
epsilon = 1e-06

MIB = 1 << 20
F32 = jnp.float32
BF16 = jnp.bfloat16
NT = (((1,), (1,)), ((), ()))


def vmem():
    return pl.BlockSpec(memory_space=pltpu.VMEM)


def call(body, name, n_in, out_shapes, flops, nbytes, scratch=(), limit=20):
    return pl.pallas_call(
        body,
        name=name,
        out_shape=out_shapes,
        in_specs=[vmem()] * n_in,
        out_specs=jax.tree.map(lambda _: vmem(), out_shapes),
        scratch_shapes=list(scratch),
        compiler_params=pltpu.CompilerParams(vmem_limit_bytes=limit * MIB),
        cost_estimate=pl.CostEstimate(flops=flops, bytes_accessed=nbytes, transcendentals=0),
    )


def struct(shape, dtype):
    return jax.ShapeDtypeStruct(shape, dtype)


def column(row):
    return jnp.broadcast_to(row, (128, row.shape[1])).T


def pick_rows(ids_rows, pools, stacked=False):
    n_ids, n_pool = len(ids_rows), len(pools)

    def body(*refs):
        ids, src = refs[:n_ids], refs[n_ids : n_ids + n_pool]
        out, hot = refs[n_ids + n_pool : -1], refs[-1]
        lane = lax.broadcasted_iota(jnp.int32, (TOK_DEV, 128), 1)
        for k in range(n_ids):
            named = column(ids[k][...])
            for j in range(POOL // 128):
                hot[:, 128 * j : 128 * (j + 1)] = jnp.where(named == lane + 128 * j, 1.0, 0.0).astype(BF16)
            for a in range(n_pool):
                rows = jnp.dot(hot[...], src[a][...], preferred_element_type=F32).astype(BF16)
                if stacked:
                    out[k][TOK_DEV * a : TOK_DEV * (a + 1), :] = rows
                else:
                    out[k * n_pool + a][...] = rows

    shapes = [struct((TOK_DEV, SLICE), BF16)] * (n_ids * n_pool)
    if stacked:
        shapes = [struct((n_pool * TOK_DEV, SLICE), BF16)] * n_ids
    return call(
        body,
        "pick_rows",
        n_ids + n_pool,
        shapes,
        2 * TOK_DEV * POOL * SLICE * n_ids * n_pool,
        (4 + 2 * n_ids) * MIB // 2,
        [pltpu.VMEM((TOK_DEV, POOL), BF16)],
    )(*ids_rows, *pools)


def slice_of(k):
    me = lax.axis_index("expert")
    return lax.rem(me + N_EXPERT - k, N_EXPERT)


def in_up_block(w, s):
    return w[pl.ds(pl.multiple_of(8 * s, 8), 8), 0:64, :].reshape(SLICE, 2 * H)


def down_block(w, s):
    row = pl.multiple_of(64 + 16 * (s // 2), 16)
    col = pl.multiple_of(SLICE * (s % 2), SLICE)
    return w[:, pl.ds(row, 16), pl.ds(col, SLICE)].reshape(H, SLICE)


def forward(tokens, weights):
    def body(x0, x1, x2, x3, w, hidden_t, gate_factor, act_out, xt, acc, hid):
        for k, x in enumerate((x0, x1, x2, x3)):
            part = jnp.dot(x[0:TOK_DEV, :], in_up_block(w, slice_of(k)), preferred_element_type=F32)
            if k == 0:
                acc[...] = part
            else:
                acc[...] += part
            xt[k] = x[0:TOK_DEV, :].T

        @pl.loop(0, TOK_DEV // 64)
        def _(i):
            rows = pl.ds(pl.multiple_of(i * 64, 64), 64)
            gate, up = acc[rows, :H], acc[rows, H:]
            sig = jax.nn.sigmoid(gate)
            act = gate * sig
            hid[rows, :] = (act * up).astype(BF16)
            gate_factor[rows, :] = up * sig * (1.0 + gate * (1.0 - sig))
            act_out[rows, :] = act

        hidden_t[...] = hid[...].T

    shapes = [
        struct((H, TOK_DEV), BF16),
        struct((TOK_DEV, H), F32),
        struct((TOK_DEV, H), F32),
        struct((N_EXPERT, SLICE, TOK_DEV), BF16),
    ]
    return call(
        body,
        "forward",
        5,
        shapes,
        2 * TOK_DEV * D * 2 * H,
        10 * MIB,
        [pltpu.VMEM((TOK_DEV, 2 * H), F32), pltpu.VMEM((TOK_DEV, H), BF16)],
    )(*tokens, weights)


def of_cotangents(first, ks, cots, route, hid_t, w, hg, scaled, put):
    scale = column(route[...])
    for k, c in zip(ks, cots):
        for j in range(SLICE // 128):
            cols = slice(128 * j, 128 * (j + 1))
            rows = slice(c.shape[0] - TOK_DEV, c.shape[0])
            scaled[:, cols] = (scale * c[rows, cols].astype(F32)).astype(BF16)
        part = lax.dot_general(scaled[...], down_block(w, slice_of(k)), NT, preferred_element_type=F32)
        if first and k == ks[0]:
            hg[...] = part
        else:
            hg[...] += part
        down = jnp.dot(hid_t[...], scaled[...], preferred_element_type=F32) / TOK_DEV
        put(k, down.astype(BF16))


def backward_early(cots, route, hidden_t, weights):
    def body(c0, c2, route_ref, hid_t, w, hg, downs, scaled):
        def put(k, down):
            downs[k // 2] = down

        of_cotangents(True, (0, 2), (c0, c2), route_ref, hid_t, w, hg, scaled, put)

    shapes = [struct((TOK_DEV, H), F32), struct((2, H, SLICE), BF16)]
    scratch = [pltpu.VMEM((TOK_DEV, SLICE), BF16)]
    return call(body, "backward_early", 5, shapes, 2 * TOK_DEV * D * H, 8 * MIB, scratch)(
        *cots, route, hidden_t, weights
    )


def backward_down(cots, route, hidden_t, early, downs, weights):
    def body(c1, c3, route_ref, hid_t, hg0, down_ref, w, keep, send, hg, scaled):
        first = lax.axis_index("dp") % 2 == 0

        def put(k, down):
            down = down.reshape(N_CHIP, 2, 16, SLICE)
            rows = pl.ds(pl.multiple_of(16 * slice_of(k), 16), 16)
            keep[:, rows, :] = jnp.where(first, down[:, 0], down[:, 1])
            send[:, rows, :] = jnp.where(first, down[:, 1], down[:, 0])

        hg[...] = hg0[...]
        of_cotangents(False, (1, 3), (c1, c3), route_ref, hid_t, w, hg, scaled, put)
        put(0, down_ref[0])
        put(2, down_ref[1])

    half = struct((N_CHIP, 64, SLICE), BF16)
    shapes = [half, half, struct((TOK_DEV, H), F32)]
    scratch = [pltpu.VMEM((TOK_DEV, SLICE), BF16)]
    return call(body, "backward_down", 7, shapes, 2 * TOK_DEV * D * H, 10 * MIB, scratch)(
        *cots, route, hidden_t, early, downs, weights
    )


def backward_in(hidden_grad, gate_factor, act, xt):
    def body(hg, factor, act_ref, xt_ref, keep, send, both):
        first = lax.axis_index("dp") % 2 == 0

        @pl.loop(0, TOK_DEV // 64)
        def _(i):
            rows = pl.ds(pl.multiple_of(i * 64, 64), 64)
            g = hg[rows, :]
            both[rows, :H] = (g * factor[rows, :]).astype(BF16)
            both[rows, H:] = (g * act_ref[rows, :]).astype(BF16)

        for k in range(N_EXPERT):
            chips = pl.ds(pl.multiple_of(4 * slice_of(k), 4), 4)
            grad = jnp.dot(xt_ref[k], both[...], preferred_element_type=F32) / TOK_DEV
            grad = grad.astype(BF16).reshape(4, 2, 64, 2 * H)
            for a in range(2):
                own = grad[:, 0, :, a * H : (a + 1) * H]
                other = grad[:, 1, :, a * H : (a + 1) * H]
                keep[chips, 64 * a : 64 * (a + 1), :] = jnp.where(first, own, other)
                send[chips, 64 * a : 64 * (a + 1), :] = jnp.where(first, other, own)

    half = struct((N_CHIP, 128, SLICE), BF16)
    shapes = [half, half, struct((TOK_DEV, 2 * H), BF16)]
    return call(body, "backward_in", 4, shapes, 4 * TOK_DEV * D * H, 10 * MIB)(hidden_grad, gate_factor, act, xt)


def slot_gradients(both, weights):
    def body(both_ref, w, *out):
        for k in (2, 1, 3, 0):
            grad = lax.dot_general(both_ref[...], in_up_block(w, slice_of(k)), NT, preferred_element_type=F32)
            out[k][...] = grad.astype(BF16)

    shapes = [struct((TOK_DEV, SLICE), BF16)] * N_EXPERT
    return call(body, "slot_gradients", 2, shapes, 4 * TOK_DEV * D * H, 9 * MIB)(both, weights)


def rows_of(of_in, of_down, q, m):
    return of_down[q] if m == 2 else of_in[q, 64 * m : 64 * (m + 1), :]


def pair_moments(own, other):
    def body(a_in, a_down, b_in, b_down, out):
        def step(q, sums):
            new = []
            for m in range(3):
                a = rows_of(a_in, a_down, q, m).astype(F32)
                b = rows_of(b_in, b_down, q, m).astype(F32)
                for t in (a * b, a * a, b * b):
                    t = jnp.sum(t.reshape(8, 8, SLICE), axis=0)
                    new.append(t[:, :128] + t[:, 128:256] + t[:, 256:384] + t[:, 384:])
            return tuple(s + n for s, n in zip(sums, new))

        sums = lax.fori_loop(0, N_CHIP, step, (jnp.zeros((8, 128), F32),) * 9)
        for j in range(9):
            out[j] = sums[j]

    return call(body, "pair_moments", 4, struct((9, 8, 128), F32), 9 * 2**20, 6 * MIB)(*own, *other)


def pair_merge(own, other, mine, theirs):
    def body(a_in, a_down, b_in, b_down, m_ref, t_ref, *out):
        coefs = []
        for m in range(3):
            inner = jnp.sum(m_ref[3 * m] + t_ref[3 * m], keepdims=True)
            norm_a = jnp.sum(m_ref[3 * m + 1] + t_ref[3 * m + 2], keepdims=True)
            norm_b = jnp.sum(m_ref[3 * m + 2] + t_ref[3 * m + 1], keepdims=True)
            coef_a = 1.0 - inner / (2.0 * (norm_a + epsilon))
            coef_b = 1.0 - inner / (2.0 * (norm_b + epsilon))
            coefs.append((jnp.broadcast_to(coef_a, (64, SLICE)), jnp.broadcast_to(coef_b, (64, SLICE))))
        c, at = place(0)

        @pl.loop(0, 4)
        def _(j):
            for k in range(4):
                first = lax.rem(at + k, 4)
                q = jnp.where(c == 0, 4 * j + first, 4 * first + j)
                for m in range(3):
                    rows = slice(64 * m, 64 * (m + 1))
                    a = rows_of(a_in, a_down, q, m).astype(F32)
                    b = rows_of(b_in, b_down, q, m).astype(F32)
                    out[k][j, rows, :] = (coefs[m][0] * a + coefs[m][1] * b).astype(BF16)

    return call(body, "pair_merge", 6, [struct((4, ROWS, SLICE), BF16)] * 4, 9 * 2**20, 9 * MIB)(
        *own, *other, mine, theirs
    )


def turn_over(parts):
    def body(*refs):
        (_, first), (_, second) = place(0), place(1)
        for k in range(4):
            for m in range(4):
                refs[4 + k][lax.rem(first + 4 - m, 4)] = refs[m][lax.rem(second + k, 4)]

    return call(body, "turn_over", 4, [struct((4, ROWS, SLICE), BF16)] * 4, 2**10, 6 * MIB)(*parts)


def origin(index):
    c, second = place(1)
    other = (second + 4 - (index >> 2)) & 3
    return jnp.where(c == 0, other * 4 + (index & 3), (index & 3) * 4 + other)


def gram(parts):
    def body(*refs):
        x, out = refs[:4], refs[4]
        row = lax.broadcasted_iota(jnp.int32, (256, 256), 0)
        col = lax.broadcasted_iota(jnp.int32, (256, 256), 1)
        same = jnp.where(row % 16 == col % 16, 1.0, 0.0)
        fold = origin(lax.broadcasted_iota(jnp.int32, (256, 128), 0) // 16)
        fold = jnp.where(fold == lax.broadcasted_iota(jnp.int32, (256, 128), 1), 1.0, 0.0)
        order = origin(lax.broadcasted_iota(jnp.int32, (16, 16), 1))
        order = jnp.where(order == lax.broadcasted_iota(jnp.int32, (16, 16), 0), 1.0, 0.0)
        exact = dict(precision=lax.Precision.HIGHEST, preferred_element_type=F32)
        for m in range(3):
            acc = None
            for b in range(4):
                at = 64 * m + 16 * b
                block = jnp.concatenate([r[:, at : at + 16, :].reshape(64, SLICE) for r in x], axis=0)
                part = lax.dot_general(block, block, NT, preferred_element_type=F32)
                acc = part if acc is None else acc + part
            acc = jnp.sum((acc * same).reshape(16, 16, 256), axis=1)
            out[m] = jnp.dot(order, jnp.dot(acc, fold, **exact), **exact)

    return call(body, "gram", 4, struct((3, 16, 128), F32), 12 * 2 * 256 * 256 * 512, 3 * MIB)(*parts)


def finish(parts, products, gate, up, down, mom_gate, mom_up, mom_down):
    def body(x0, x1, x2, x3, g_ref, g_other, gate_w, up_w, down_w, gate_m, up_m, down_m, new_g, new_u, new_d, next_g, next_u, next_d):
        g = g_ref[...] + g_other[...]
        i = lax.broadcasted_iota(jnp.int32, (3, 16, 128), 1)
        j = lax.broadcasted_iota(jnp.int32, (3, 16, 128), 2)
        c_col = jnp.ones((3, 16, 1), F32)
        c_row = jnp.ones((3, 1, 128), F32)
        for level in range(4):
            block_i, block_j = i >> level, j >> level
            same, sibling = block_i == block_j, (block_i ^ 1) == block_j
            weighted = g * c_col * c_row
            within = jnp.where(same, weighted, 0.0)
            across = jnp.where(sibling, weighted, 0.0)

            def coef(axis):
                norm = jnp.sum(jnp.where(same, jnp.sum(within, axis=3 - axis, keepdims=True), 0.0), axis=axis, keepdims=True)
                inner = jnp.sum(jnp.where(same, jnp.sum(across, axis=3 - axis, keepdims=True), 0.0), axis=axis, keepdims=True)
                return 1.0 - inner / (2.0 * (jnp.maximum(norm, 0.0) + epsilon))

            c_col, c_row = c_col * coef(2), c_row * coef(1)
        chip = origin(lax.broadcasted_iota(jnp.int32, (16, 128), 0))
        chip = chip == lax.broadcasted_iota(jnp.int32, (16, 128), 1)
        c_col = jnp.sum(jnp.where(chip, c_row, 0.0), axis=2, keepdims=True)
        olds = ((gate_w, gate_m, new_g, next_g), (up_w, up_m, new_u, next_u))
        for m in range(3):
            merged = jnp.zeros((64, SLICE), F32)
            for q in range(16):
                scale = jnp.broadcast_to(c_col[m, q : q + 1, :], (64, SLICE))
                x = (x0, x1, x2, x3)[q // 4]
                merged += scale * x[q % 4, 64 * m : 64 * (m + 1), :].astype(F32)
            if m < 2:
                w, mom, new, after = olds[m]
                step = momentum_decay * mom[...] + merged
                after[...] = step
                new[...] = w[...] - learning_rate * step
            else:
                for k in range(4):
                    cols = slice(SLICE * k, SLICE * (k + 1))
                    step = momentum_decay * down_m[:, cols] + merged[16 * k : 16 * (k + 1), :]
                    next_d[:, cols] = step
                    new_d[:, cols] = down_w[:, cols] - learning_rate * step

    wide, tall = struct((64, H), F32), struct((16, D), F32)
    return call(body, "finish", 12, [wide, wide, tall, wide, wide, tall], 2**22, 6 * MIB)(
        *parts, *products, gate, up, down, mom_gate, mom_up, mom_down
    )


def scatter_rows(ids_rows, grads, half, into=()):
    block, steps = 512, POOL // 1024

    def body(*refs):
        row = lax.broadcasted_iota(jnp.int32, (block, TOK_DEV), 0)
        row += block * (pl.program_id(0) + steps * half)
        acc = None
        for ids, g in zip(refs[:4], refs[4:8]):
            hot = jnp.where(jnp.broadcast_to(ids[...], row.shape) == row, 1.0, 0.0).astype(BF16)
            part = jnp.dot(hot, g[...], preferred_element_type=F32)
            acc = part if acc is None else acc + part
        refs[-1][...] = acc

    return pl.pallas_call(
        body,
        name="scatter_rows",
        grid=(steps,),
        out_shape=struct((POOL, SLICE), F32),
        in_specs=[vmem()] * 8 + [pl.BlockSpec(memory_space=pl.ANY)] * len(into),
        out_specs=pl.BlockSpec((block, SLICE), lambda i: (i + steps * half, 0)),
        input_output_aliases={8: 0} if into else {},
        compiler_params=pltpu.CompilerParams(vmem_limit_bytes=24 * MIB),
        cost_estimate=pl.CostEstimate(flops=POOL * POOL * SLICE, bytes_accessed=4 * MIB, transcendentals=0),
    )(*ids_rows, *grads, *into)


def shift(block, axis, to):
    return lax.ppermute(block, axis, [(i, to(i)) for i in range(lax.axis_size(axis))])


def around_y(block, k):
    return shift(block, "expert", lambda i: (i + k) % N_EXPERT)


def around_z(block, k):
    return shift(block, "dp", lambda i: i // 8 * 8 + (i // 2 % 4 + k) % 4 * 2 + i % 2)


def around_x(block, k):
    return shift(block, "dp", lambda i: (i // 8 + k) % 4 * 8 + i % 8)


def other_core(block):
    return shift(block, "dp", lambda i: i ^ 1)


def sum_dp(value, ids, grads):
    pool = ()
    for half, around in enumerate((around_z, around_x)):
        others = [around(value, k) for k in (2, 1, 3)]
        others, pool = lax.optimization_barrier((others, (scatter_rows(ids, grads, half, pool),)))
        value = value + sum(others)
    return (value, other_core(value)), pool[0]


def pack(gate, up, down):
    def body(gate_hbm, up_hbm, down_hbm, out, g, u, d, sems):
        copies = [
            pltpu.make_async_copy(src, dst, sems.at[j])
            for j, (src, dst) in enumerate(((gate_hbm, g), (up_hbm, u), (down_hbm, d)))
        ]
        for copy in copies:
            copy.start()
        for copy in copies:
            copy.wait()
        out[0:64, 0:H] = g[...].astype(BF16)
        out[0:64, H:] = u[...].astype(BF16)
        out[64:80, :] = d[:, : D // 2].astype(BF16)
        out[80:96, :] = d[:, D // 2 :].astype(BF16)

    return pl.pallas_call(
        body,
        name="pack",
        out_shape=struct((96, 1024), BF16),
        in_specs=[pl.BlockSpec(memory_space=pl.ANY)] * 3,
        out_specs=vmem(),
        scratch_shapes=[
            pltpu.VMEM((64, H), F32),
            pltpu.VMEM((64, H), F32),
            pltpu.VMEM((16, D), F32),
            pltpu.SemaphoreType.DMA((3,)),
        ],
        compiler_params=pltpu.CompilerParams(vmem_limit_bytes=8 * MIB),
        cost_estimate=pl.CostEstimate(flops=2**17, bytes_accessed=MIB, transcendentals=0),
    )(gate, up, down)


def along(turn, step):
    def to(i):
        x, z, c = i // 8, i // 2 % 4, i % 2
        return x * 8 + (z + step) % 4 * 2 + c if c == turn else (x + step) % 4 * 8 + z * 2 + c

    return to


def to_others(blocks, turn):
    out = {k: shift(blocks[k], "dp", along(turn, k)) for k in (2, 1, 3)}
    return [out[1], out[2], out[3]]


def tie_far(items, others, last=False):
    order = (3, 1, 2, 0) if last else (2, 1, 3, 0)
    tied, others = lax.optimization_barrier(([items[k] for k in order], others))
    return [tied[order.index(k)] for k in range(4)], others


def spread(block, turn):
    return to_others([block] * 4, turn)


def place(turn):
    at = lax.axis_index("dp")
    x, z, c = at // 8, lax.rem(at // 2, 4), lax.rem(at, 2)
    return c, jnp.where(c == turn, z, x)


def bundle(blocks):
    def body(*refs):
        _, at = place(0)
        for k in range(4):
            refs[4][lax.rem(at + 4 - k, 4)] = refs[k][...]

    return call(body, "bundle", 4, struct((4, 96, 1024), BF16), 2**10, 2 * MIB)(*blocks)


def half_of_weights(bundles):
    def body(*refs):
        c, at = place(1)
        for k in range(4):
            other = lax.rem(at + 4 - k, 4)
            for j in range(4):
                refs[4][jnp.where(c == 0, other * 4 + j, j * 4 + other)] = refs[k][j]

    return call(body, "half_of_weights", 4, struct((N_CHIP, 96, 1024), BF16), 2**10, 6 * MIB)(*bundles)


def whole_weights(own, other):
    def body(a, b, out):
        c = lax.rem(lax.axis_index("dp"), 2)

        @pl.loop(0, N_CHIP)
        def _(q):
            out[2 * q + c] = a[q]
            out[2 * q + 1 - c] = b[q]

    return call(body, "whole_weights", 2, struct((2 * N_CHIP, 96, 1024), BF16), 2**10, 12 * MIB)(own, other)


def local(
    pool_tokens,
    pool_cotangent,
    token_ids,
    route_weights,
    gate_weight,
    up_weight,
    down_weight,
    momentum_gate,
    momentum_up,
    momentum_down,
):
    tie = lax.optimization_barrier

    def picked(k, pool):
        return pick_rows(ids[k : k + 1], [pool])[0]

    ids = [token_ids] + [around_y(token_ids, N_EXPERT - k) for k in (1, 2, 3)]
    x, c = [None] * 4, [None] * 4
    x[1], x[3] = picked(1, pool_tokens), picked(3, pool_tokens)
    ids, x[1], x[3], shards = tie((ids, x[1], x[3], (gate_weight[0], up_weight[0], down_weight[0])))

    packed = pack(*shards)
    blocks = spread(packed, 0)
    x[1], x[3] = around_y(x[1], 1), around_y(x[3], 3)
    (x[2],) = pick_rows(ids[2:3], [pool_tokens, pool_cotangent], stacked=True)
    blocks, (ids, x[1:]) = tie_far([packed, *blocks], (ids, x[1:]), last=True)

    block = bundle(blocks)
    blocks = spread(block, 1)
    x[2] = c[2] = around_y(x[2], 2)
    c[1], c[3] = picked(1, pool_cotangent), picked(3, pool_cotangent)
    x[0], c[0] = pick_rows(ids[:1], [pool_tokens, pool_cotangent])
    blocks, (x, c) = tie_far([block, *blocks], (x, [c[0], c[1], c[3]]), last=True)
    c = [c[0], c[1], x[2], c[2]]

    mine = half_of_weights(blocks)
    weights = whole_weights(mine, other_core(mine))
    c[1], c[3] = around_y(c[1], 1), around_y(c[3], 3)

    hidden_t, gate_factor, act, xt = forward(x, weights)
    early, downs = backward_early((c[0], c[2]), route_weights, hidden_t, weights)
    keep_down, send_down, hidden_grad = backward_down((c[1], c[3]), route_weights, hidden_t, early, downs, weights)
    keep_in, send_in, both = backward_in(hidden_grad, gate_factor, act, xt)
    received_down, send_in = tie((other_core(send_down), send_in))
    keep, received = (keep_in, keep_down), (other_core(send_in), received_down)
    slots = slot_gradients(both, weights)
    received, slots = lax.optimization_barrier((received, list(slots)))

    mine = pair_moments(keep, received)
    sent = pair_merge(keep, received, mine, other_core(mine))
    parts = [sent[0], *to_others(sent, 0)]
    back = [slots[0], around_y(slots[1], 3), None, around_y(slots[3], 1)]
    parts, (back[1], back[3]) = tie_far(parts, (back[1], back[3]))
    sent, slots[2] = tie((turn_over(parts), slots[2]))
    parts = [sent[0], *to_others(sent, 1)]
    back[2] = around_y(slots[2], 2)
    parts, back[2] = tie_far(parts, back[2])
    products, pool_grad = sum_dp(gram(parts), ids, back)
    outs = finish(
        parts,
        products,
        gate_weight[0],
        up_weight[0],
        down_weight[0],
        momentum_gate[0],
        momentum_up[0],
        momentum_down[0],
    )
    return (*(a[None] for a in outs), pool_grad)


def solution(mesh):
    in_specs = (
        P("dp", "expert"),
        P("dp", "expert"),
        P("expert", "dp"),
        P("expert", "dp"),
        P("expert", "dp", None),
        P("expert", "dp", None),
        P("expert", "dp", None),
        P("expert", "dp", None),
        P("expert", "dp", None),
        P("expert", "dp", None),
    )
    out_specs = (
        P("expert", "dp", None),
        P("expert", "dp", None),
        P("expert", "dp", None),
        P("expert", "dp", None),
        P("expert", "dp", None),
        P("expert", "dp", None),
        P("dp", "expert"),
    )
    return jax.shard_map(local, mesh=mesh, in_specs=in_specs, out_specs=out_specs, check_vma=False)
```

```python
import jax
import jax.numpy as jnp
from jax import lax
from jax.experimental import pallas as pl
from jax.experimental.pallas import tpu as pltpu
from jax.sharding import PartitionSpec as P

TOK_DEV = 512
POOL = 2048
D = 2048
H = 512
N_EXPERT = 4
N_CHIP = 16
SLICE = 512
ROWS = 192

momentum_decay = 0.9
learning_rate = 0.05
epsilon = 1e-06

MIB = 1 << 20
F32 = jnp.float32
BF16 = jnp.bfloat16
NT = (((1,), (1,)), ((), ()))


def vmem():
    return pl.BlockSpec(memory_space=pltpu.VMEM)


def call(body, name, n_in, out_shapes, flops, nbytes, scratch=(), limit=20):
    return pl.pallas_call(
        body,
        name=name,
        out_shape=out_shapes,
        in_specs=[vmem()] * n_in,
        out_specs=jax.tree.map(lambda _: vmem(), out_shapes),
        scratch_shapes=list(scratch),
        compiler_params=pltpu.CompilerParams(vmem_limit_bytes=limit * MIB),
        cost_estimate=pl.CostEstimate(flops=flops, bytes_accessed=nbytes, transcendentals=0),
    )


def struct(shape, dtype):
    return jax.ShapeDtypeStruct(shape, dtype)


def column(row):
    return jnp.broadcast_to(row, (128, row.shape[1])).T


def pick_rows(ids_rows, pools, stacked=False):
    n_ids, n_pool = len(ids_rows), len(pools)

    def body(*refs):
        ids, src = refs[:n_ids], refs[n_ids : n_ids + n_pool]
        out, hot = refs[n_ids + n_pool : -1], refs[-1]
        lane = lax.broadcasted_iota(jnp.int32, (TOK_DEV, 128), 1)
        for k in range(n_ids):
            named = column(ids[k][...])
            for j in range(POOL // 128):
                hot[:, 128 * j : 128 * (j + 1)] = jnp.where(named == lane + 128 * j, 1.0, 0.0).astype(BF16)
            for a in range(n_pool):
                rows = jnp.dot(hot[...], src[a][...], preferred_element_type=F32).astype(BF16)
                if stacked:
                    out[k][TOK_DEV * a : TOK_DEV * (a + 1), :] = rows
                else:
                    out[k * n_pool + a][...] = rows

    shapes = [struct((TOK_DEV, SLICE), BF16)] * (n_ids * n_pool)
    if stacked:
        shapes = [struct((n_pool * TOK_DEV, SLICE), BF16)] * n_ids
    return call(
        body,
        "pick_rows",
        n_ids + n_pool,
        shapes,
        2 * TOK_DEV * POOL * SLICE * n_ids * n_pool,
        (4 + 2 * n_ids) * MIB // 2,
        [pltpu.VMEM((TOK_DEV, POOL), BF16)],
    )(*ids_rows, *pools)


def slice_of(k):
    me = lax.axis_index("expert")
    return lax.rem(me + N_EXPERT - k, N_EXPERT)


def in_up_block(w, s):
    return w[pl.ds(pl.multiple_of(8 * s, 8), 8), 0:64, :].reshape(SLICE, 2 * H)


def down_block(w, s):
    row = pl.multiple_of(64 + 16 * (s // 2), 16)
    col = pl.multiple_of(SLICE * (s % 2), SLICE)
    return w[:, pl.ds(row, 16), pl.ds(col, SLICE)].reshape(H, SLICE)


def forward(tokens, weights):
    def body(x0, x1, x2, x3, w, hidden_t, gate_factor, act_out, xt, acc, hid):
        for k, x in enumerate((x0, x1, x2, x3)):
            part = jnp.dot(x[0:TOK_DEV, :], in_up_block(w, slice_of(k)), preferred_element_type=F32)
            if k == 0:
                acc[...] = part
            else:
                acc[...] += part
            xt[k] = x[0:TOK_DEV, :].T

        @pl.loop(0, TOK_DEV // 64)
        def _(i):
            rows = pl.ds(pl.multiple_of(i * 64, 64), 64)
            gate, up = acc[rows, :H], acc[rows, H:]
            sig = jax.nn.sigmoid(gate)
            act = gate * sig
            hid[rows, :] = (act * up).astype(BF16)
            gate_factor[rows, :] = up * sig * (1.0 + gate * (1.0 - sig))
            act_out[rows, :] = act

        hidden_t[...] = hid[...].T

    shapes = [
        struct((H, TOK_DEV), BF16),
        struct((TOK_DEV, H), F32),
        struct((TOK_DEV, H), F32),
        struct((N_EXPERT, SLICE, TOK_DEV), BF16),
    ]
    return call(
        body,
        "forward",
        5,
        shapes,
        2 * TOK_DEV * D * 2 * H,
        10 * MIB,
        [pltpu.VMEM((TOK_DEV, 2 * H), F32), pltpu.VMEM((TOK_DEV, H), BF16)],
    )(*tokens, weights)


def of_cotangents(first, ks, cots, route, hid_t, w, hg, scaled, put):
    scale = column(route[...])
    for k, c in zip(ks, cots):
        for j in range(SLICE // 128):
            cols = slice(128 * j, 128 * (j + 1))
            rows = slice(c.shape[0] - TOK_DEV, c.shape[0])
            scaled[:, cols] = (scale * c[rows, cols].astype(F32)).astype(BF16)
        part = lax.dot_general(scaled[...], down_block(w, slice_of(k)), NT, preferred_element_type=F32)
        if first and k == ks[0]:
            hg[...] = part
        else:
            hg[...] += part
        down = jnp.dot(hid_t[...], scaled[...], preferred_element_type=F32) / TOK_DEV
        put(k, down.astype(BF16))


def backward_early(cots, route, hidden_t, weights):
    def body(c0, c2, route_ref, hid_t, w, hg, downs, scaled):
        def put(k, down):
            downs[k // 2] = down

        of_cotangents(True, (0, 2), (c0, c2), route_ref, hid_t, w, hg, scaled, put)

    shapes = [struct((TOK_DEV, H), F32), struct((2, H, SLICE), BF16)]
    scratch = [pltpu.VMEM((TOK_DEV, SLICE), BF16)]
    return call(body, "backward_early", 5, shapes, 2 * TOK_DEV * D * H, 8 * MIB, scratch)(
        *cots, route, hidden_t, weights
    )


def backward_down(cots, route, hidden_t, early, downs, weights):
    def body(c1, c3, route_ref, hid_t, hg0, down_ref, w, keep, send, hg, scaled):
        first = lax.axis_index("dp") % 2 == 0

        def put(k, down):
            down = down.reshape(N_CHIP, 2, 16, SLICE)
            rows = pl.ds(pl.multiple_of(16 * slice_of(k), 16), 16)
            keep[:, rows, :] = jnp.where(first, down[:, 0], down[:, 1])
            send[:, rows, :] = jnp.where(first, down[:, 1], down[:, 0])

        hg[...] = hg0[...]
        of_cotangents(False, (1, 3), (c1, c3), route_ref, hid_t, w, hg, scaled, put)
        put(0, down_ref[0])
        put(2, down_ref[1])

    half = struct((N_CHIP, 64, SLICE), BF16)
    shapes = [half, half, struct((TOK_DEV, H), F32)]
    scratch = [pltpu.VMEM((TOK_DEV, SLICE), BF16)]
    return call(body, "backward_down", 7, shapes, 2 * TOK_DEV * D * H, 10 * MIB, scratch)(
        *cots, route, hidden_t, early, downs, weights
    )


def backward_in(hidden_grad, gate_factor, act, xt):
    def body(hg, factor, act_ref, xt_ref, keep, send, both):
        first = lax.axis_index("dp") % 2 == 0

        @pl.loop(0, TOK_DEV // 64)
        def _(i):
            rows = pl.ds(pl.multiple_of(i * 64, 64), 64)
            g = hg[rows, :]
            both[rows, :H] = (g * factor[rows, :]).astype(BF16)
            both[rows, H:] = (g * act_ref[rows, :]).astype(BF16)

        for k in range(N_EXPERT):
            chips = pl.ds(pl.multiple_of(4 * slice_of(k), 4), 4)
            grad = jnp.dot(xt_ref[k], both[...], preferred_element_type=F32) / TOK_DEV
            grad = grad.astype(BF16).reshape(4, 2, 64, 2 * H)
            for a in range(2):
                own = grad[:, 0, :, a * H : (a + 1) * H]
                other = grad[:, 1, :, a * H : (a + 1) * H]
                keep[chips, 64 * a : 64 * (a + 1), :] = jnp.where(first, own, other)
                send[chips, 64 * a : 64 * (a + 1), :] = jnp.where(first, other, own)

    half = struct((N_CHIP, 128, SLICE), BF16)
    shapes = [half, half, struct((TOK_DEV, 2 * H), BF16)]
    return call(body, "backward_in", 4, shapes, 4 * TOK_DEV * D * H, 10 * MIB)(hidden_grad, gate_factor, act, xt)


def slot_gradients(both, weights):
    def body(both_ref, w, *out):
        for k in (2, 1, 3, 0):
            grad = lax.dot_general(both_ref[...], in_up_block(w, slice_of(k)), NT, preferred_element_type=F32)
            out[k][...] = grad.astype(BF16)

    shapes = [struct((TOK_DEV, SLICE), BF16)] * N_EXPERT
    return call(body, "slot_gradients", 2, shapes, 4 * TOK_DEV * D * H, 9 * MIB)(both, weights)


def rows_of(of_in, of_down, q, m):
    return of_down[q] if m == 2 else of_in[q, 64 * m : 64 * (m + 1), :]


def pair_moments(own, other):
    def body(a_in, a_down, b_in, b_down, out):
        def step(q, sums):
            new = []
            for m in range(3):
                a = rows_of(a_in, a_down, q, m).astype(F32)
                b = rows_of(b_in, b_down, q, m).astype(F32)
                for t in (a * b, a * a, b * b):
                    t = jnp.sum(t.reshape(8, 8, SLICE), axis=0)
                    new.append(t[:, :128] + t[:, 128:256] + t[:, 256:384] + t[:, 384:])
            return tuple(s + n for s, n in zip(sums, new))

        sums = lax.fori_loop(0, N_CHIP, step, (jnp.zeros((8, 128), F32),) * 9)
        for j in range(9):
            out[j] = sums[j]

    return call(body, "pair_moments", 4, struct((9, 8, 128), F32), 9 * 2**20, 6 * MIB)(*own, *other)


def pair_merge(own, other, mine, theirs):
    def body(a_in, a_down, b_in, b_down, m_ref, t_ref, *out):
        coefs = []
        for m in range(3):
            inner = jnp.sum(m_ref[3 * m] + t_ref[3 * m], keepdims=True)
            norm_a = jnp.sum(m_ref[3 * m + 1] + t_ref[3 * m + 2], keepdims=True)
            norm_b = jnp.sum(m_ref[3 * m + 2] + t_ref[3 * m + 1], keepdims=True)
            coef_a = 1.0 - inner / (2.0 * (norm_a + epsilon))
            coef_b = 1.0 - inner / (2.0 * (norm_b + epsilon))
            coefs.append((jnp.broadcast_to(coef_a, (64, SLICE)), jnp.broadcast_to(coef_b, (64, SLICE))))
        c, at = place(0)

        @pl.loop(0, 4)
        def _(j):
            for k in range(4):
                first = lax.rem(at + k, 4)
                q = jnp.where(c == 0, 4 * j + first, 4 * first + j)
                for m in range(3):
                    rows = slice(64 * m, 64 * (m + 1))
                    a = rows_of(a_in, a_down, q, m).astype(F32)
                    b = rows_of(b_in, b_down, q, m).astype(F32)
                    out[k][j, rows, :] = (coefs[m][0] * a + coefs[m][1] * b).astype(BF16)

    return call(body, "pair_merge", 6, [struct((4, ROWS, SLICE), BF16)] * 4, 9 * 2**20, 9 * MIB)(
        *own, *other, mine, theirs
    )


def turn_over(parts):
    def body(*refs):
        (_, first), (_, second) = place(0), place(1)
        for k in range(4):
            for m in range(4):
                refs[4 + k][lax.rem(first + 4 - m, 4)] = refs[m][lax.rem(second + k, 4)]

    return call(body, "turn_over", 4, [struct((4, ROWS, SLICE), BF16)] * 4, 2**10, 6 * MIB)(*parts)


def origin(index):
    c, second = place(1)
    other = (second + 4 - (index >> 2)) & 3
    return jnp.where(c == 0, other * 4 + (index & 3), (index & 3) * 4 + other)


def gram(parts):
    def body(*refs):
        x, out = refs[:4], refs[4]
        row = lax.broadcasted_iota(jnp.int32, (256, 256), 0)
        col = lax.broadcasted_iota(jnp.int32, (256, 256), 1)
        same = jnp.where(row % 16 == col % 16, 1.0, 0.0)
        fold = origin(lax.broadcasted_iota(jnp.int32, (256, 128), 0) // 16)
        fold = jnp.where(fold == lax.broadcasted_iota(jnp.int32, (256, 128), 1), 1.0, 0.0)
        order = origin(lax.broadcasted_iota(jnp.int32, (16, 16), 1))
        order = jnp.where(order == lax.broadcasted_iota(jnp.int32, (16, 16), 0), 1.0, 0.0)
        exact = dict(precision=lax.Precision.HIGHEST, preferred_element_type=F32)
        for m in range(3):
            spans = [slice(64 * m + 16 * b, 64 * m + 16 * (b + 1)) for b in range(4)]
            block = jnp.concatenate(
                [jnp.concatenate([r[:, rows, :].reshape(64, SLICE) for rows in spans], axis=1) for r in x], axis=0
            )
            acc = lax.dot_general(block, block, NT, preferred_element_type=F32)
            acc = jnp.sum((acc * same).reshape(16, 16, 256), axis=1)
            out[m] = jnp.dot(order, jnp.dot(acc, fold, **exact), **exact)

    return call(body, "gram", 4, struct((3, 16, 128), F32), 12 * 2 * 256 * 256 * 512, 3 * MIB)(*parts)


def finish(parts, products, gate, up, down, mom_gate, mom_up, mom_down):
    def body(x0, x1, x2, x3, g_ref, g_other, gate_w, up_w, down_w, gate_m, up_m, down_m, new_g, new_u, new_d, next_g, next_u, next_d):
        g = g_ref[...] + g_other[...]
        i = lax.broadcasted_iota(jnp.int32, (3, 16, 128), 1)
        j = lax.broadcasted_iota(jnp.int32, (3, 16, 128), 2)
        c_col = jnp.ones((3, 16, 1), F32)
        c_row = jnp.ones((3, 1, 128), F32)
        for level in range(4):
            block_i, block_j = i >> level, j >> level
            same, sibling = block_i == block_j, (block_i ^ 1) == block_j
            weighted = g * c_col * c_row
            within = jnp.where(same, weighted, 0.0)
            across = jnp.where(sibling, weighted, 0.0)

            def coef(axis):
                norm = jnp.sum(jnp.where(same, jnp.sum(within, axis=3 - axis, keepdims=True), 0.0), axis=axis, keepdims=True)
                inner = jnp.sum(jnp.where(same, jnp.sum(across, axis=3 - axis, keepdims=True), 0.0), axis=axis, keepdims=True)
                return 1.0 - inner / (2.0 * (jnp.maximum(norm, 0.0) + epsilon))

            c_col, c_row = c_col * coef(2), c_row * coef(1)
        chip = origin(lax.broadcasted_iota(jnp.int32, (16, 128), 0))
        chip = chip == lax.broadcasted_iota(jnp.int32, (16, 128), 1)
        c_col = jnp.sum(jnp.where(chip, c_row, 0.0), axis=2, keepdims=True)
        olds = ((gate_w, gate_m, new_g, next_g), (up_w, up_m, new_u, next_u))
        for m in range(3):
            merged = jnp.zeros((64, SLICE), F32)
            for q in range(16):
                scale = jnp.broadcast_to(c_col[m, q : q + 1, :], (64, SLICE))
                x = (x0, x1, x2, x3)[q // 4]
                merged += scale * x[q % 4, 64 * m : 64 * (m + 1), :].astype(F32)
            if m < 2:
                w, mom, new, after = olds[m]
                step = momentum_decay * mom[...] + merged
                after[...] = step
                new[...] = w[...] - learning_rate * step
            else:
                for k in range(4):
                    cols = slice(SLICE * k, SLICE * (k + 1))
                    step = momentum_decay * down_m[:, cols] + merged[16 * k : 16 * (k + 1), :]
                    next_d[:, cols] = step
                    new_d[:, cols] = down_w[:, cols] - learning_rate * step

    wide, tall = struct((64, H), F32), struct((16, D), F32)
    return call(body, "finish", 12, [wide, wide, tall, wide, wide, tall], 2**22, 6 * MIB)(
        *parts, *products, gate, up, down, mom_gate, mom_up, mom_down
    )


def scatter_rows(ids_rows, grads, half, into=()):
    block, steps = 512, POOL // 1024

    def body(*refs):
        row = lax.broadcasted_iota(jnp.int32, (block, TOK_DEV), 0)
        row += block * (pl.program_id(0) + steps * half)
        acc = None
        for ids, g in zip(refs[:4], refs[4:8]):
            hot = jnp.where(jnp.broadcast_to(ids[...], row.shape) == row, 1.0, 0.0).astype(BF16)
            part = jnp.dot(hot, g[...], preferred_element_type=F32)
            acc = part if acc is None else acc + part
        refs[-1][...] = acc

    return pl.pallas_call(
        body,
        name="scatter_rows",
        grid=(steps,),
        out_shape=struct((POOL, SLICE), F32),
        in_specs=[vmem()] * 8 + [pl.BlockSpec(memory_space=pl.ANY)] * len(into),
        out_specs=pl.BlockSpec((block, SLICE), lambda i: (i + steps * half, 0)),
        input_output_aliases={8: 0} if into else {},
        compiler_params=pltpu.CompilerParams(vmem_limit_bytes=24 * MIB),
        cost_estimate=pl.CostEstimate(flops=POOL * POOL * SLICE, bytes_accessed=4 * MIB, transcendentals=0),
    )(*ids_rows, *grads, *into)


def shift(block, axis, to):
    return lax.ppermute(block, axis, [(i, to(i)) for i in range(lax.axis_size(axis))])


def around_y(block, k):
    return shift(block, "expert", lambda i: (i + k) % N_EXPERT)


def around_z(block, k):
    return shift(block, "dp", lambda i: i // 8 * 8 + (i // 2 % 4 + k) % 4 * 2 + i % 2)


def around_x(block, k):
    return shift(block, "dp", lambda i: (i // 8 + k) % 4 * 8 + i % 8)


def other_core(block):
    return shift(block, "dp", lambda i: i ^ 1)


def sum_dp(value, ids, grads):
    pool = ()
    for half, around in enumerate((around_z, around_x)):
        others = [around(value, k) for k in (2, 1, 3)]
        others, pool = lax.optimization_barrier((others, (scatter_rows(ids, grads, half, pool),)))
        value = value + sum(others)
    return (value, other_core(value)), pool[0]


def pack(gate, up, down):
    def body(gate_hbm, up_hbm, down_hbm, out, g, u, d, sems):
        copies = [
            pltpu.make_async_copy(src, dst, sems.at[j])
            for j, (src, dst) in enumerate(((gate_hbm, g), (up_hbm, u), (down_hbm, d)))
        ]
        for copy in copies:
            copy.start()
        for copy in copies:
            copy.wait()
        out[0:64, 0:H] = g[...].astype(BF16)
        out[0:64, H:] = u[...].astype(BF16)
        out[64:80, :] = d[:, : D // 2].astype(BF16)
        out[80:96, :] = d[:, D // 2 :].astype(BF16)

    return pl.pallas_call(
        body,
        name="pack",
        out_shape=struct((96, 1024), BF16),
        in_specs=[pl.BlockSpec(memory_space=pl.ANY)] * 3,
        out_specs=vmem(),
        scratch_shapes=[
            pltpu.VMEM((64, H), F32),
            pltpu.VMEM((64, H), F32),
            pltpu.VMEM((16, D), F32),
            pltpu.SemaphoreType.DMA((3,)),
        ],
        compiler_params=pltpu.CompilerParams(vmem_limit_bytes=8 * MIB),
        cost_estimate=pl.CostEstimate(flops=2**17, bytes_accessed=MIB, transcendentals=0),
    )(gate, up, down)


def along(turn, step):
    def to(i):
        x, z, c = i // 8, i // 2 % 4, i % 2
        return x * 8 + (z + step) % 4 * 2 + c if c == turn else (x + step) % 4 * 8 + z * 2 + c

    return to


def to_others(blocks, turn):
    out = {k: shift(blocks[k], "dp", along(turn, k)) for k in (2, 1, 3)}
    return [out[1], out[2], out[3]]


def tie_in_order(items, others):
    order = (3, 1, 2, 0)
    tied, others = lax.optimization_barrier(([items[k] for k in order], others))
    return [tied[order.index(k)] for k in range(4)], others


def spread(block, turn):
    return to_others([block] * 4, turn)


def place(turn):
    at = lax.axis_index("dp")
    x, z, c = at // 8, lax.rem(at // 2, 4), lax.rem(at, 2)
    return c, jnp.where(c == turn, z, x)


def bundle(blocks):
    def body(*refs):
        _, at = place(0)
        for k in range(4):
            refs[4][lax.rem(at + 4 - k, 4)] = refs[k][...]

    return call(body, "bundle", 4, struct((4, 96, 1024), BF16), 2**10, 2 * MIB)(*blocks)


def half_of_weights(bundles):
    def body(*refs):
        c, at = place(1)
        for k in range(4):
            other = lax.rem(at + 4 - k, 4)
            for j in range(4):
                refs[4][jnp.where(c == 0, other * 4 + j, j * 4 + other)] = refs[k][j]

    return call(body, "half_of_weights", 4, struct((N_CHIP, 96, 1024), BF16), 2**10, 6 * MIB)(*bundles)


def whole_weights(own, other):
    def body(a, b, out):
        c = lax.rem(lax.axis_index("dp"), 2)

        @pl.loop(0, N_CHIP)
        def _(q):
            out[2 * q + c] = a[q]
            out[2 * q + 1 - c] = b[q]

    return call(body, "whole_weights", 2, struct((2 * N_CHIP, 96, 1024), BF16), 2**10, 12 * MIB)(own, other)


def local(
    pool_tokens,
    pool_cotangent,
    token_ids,
    route_weights,
    gate_weight,
    up_weight,
    down_weight,
    momentum_gate,
    momentum_up,
    momentum_down,
):
    tie = lax.optimization_barrier

    def picked(k, pool):
        return pick_rows(ids[k : k + 1], [pool])[0]

    ids = [token_ids] + [around_y(token_ids, N_EXPERT - k) for k in (1, 2, 3)]
    x, c = [None] * 4, [None] * 4
    x[1], x[3] = picked(1, pool_tokens), picked(3, pool_tokens)
    ids, x[1], x[3], shards = tie((ids, x[1], x[3], (gate_weight[0], up_weight[0], down_weight[0])))

    packed = pack(*shards)
    blocks = spread(packed, 0)
    x[1], x[3] = around_y(x[1], 1), around_y(x[3], 3)
    (x[2],) = pick_rows(ids[2:3], [pool_tokens, pool_cotangent], stacked=True)
    blocks, (ids, x[1:]) = tie_in_order([packed, *blocks], (ids, x[1:]))

    block = bundle(blocks)
    blocks = spread(block, 1)
    x[2] = c[2] = around_y(x[2], 2)
    c[1], c[3] = picked(1, pool_cotangent), picked(3, pool_cotangent)
    x[0], c[0] = pick_rows(ids[:1], [pool_tokens, pool_cotangent])
    blocks, (x, c) = tie_in_order([block, *blocks], (x, [c[0], c[1], c[3]]))
    c = [c[0], c[1], x[2], c[2]]

    mine = half_of_weights(blocks)
    weights = whole_weights(mine, other_core(mine))
    c[1], c[3] = around_y(c[1], 1), around_y(c[3], 3)

    hidden_t, gate_factor, act, xt = forward(x, weights)
    early, downs = backward_early((c[0], c[2]), route_weights, hidden_t, weights)
    keep_down, send_down, hidden_grad = backward_down((c[1], c[3]), route_weights, hidden_t, early, downs, weights)
    keep_in, send_in, both = backward_in(hidden_grad, gate_factor, act, xt)
    received_down, send_in = tie((other_core(send_down), send_in))
    keep, received = (keep_in, keep_down), (other_core(send_in), received_down)
    slots = slot_gradients(both, weights)
    received, slots = lax.optimization_barrier((received, list(slots)))

    mine = pair_moments(keep, received)
    sent = pair_merge(keep, received, mine, other_core(mine))
    parts = [sent[0], *to_others(sent, 0)]
    back = [slots[0], around_y(slots[1], 3), None, around_y(slots[3], 1)]
    parts, (back[1], back[3]) = tie_in_order(parts, (back[1], back[3]))
    sent, slots[2] = tie((turn_over(parts), slots[2]))
    parts = [sent[0], *to_others(sent, 1)]
    back[2] = around_y(slots[2], 2)
    parts, back[2] = tie_in_order(parts, back[2])
    products, pool_grad = sum_dp(gram(parts), ids, back)
    outs = finish(
        parts,
        products,
        gate_weight[0],
        up_weight[0],
        down_weight[0],
        momentum_gate[0],
        momentum_up[0],
        momentum_down[0],
    )
    return (*(a[None] for a in outs), pool_grad)


def solution(mesh):
    in_specs = (
        P("dp", "expert"),
        P("dp", "expert"),
        P("expert", "dp"),
        P("expert", "dp"),
        P("expert", "dp", None),
        P("expert", "dp", None),
        P("expert", "dp", None),
        P("expert", "dp", None),
        P("expert", "dp", None),
        P("expert", "dp", None),
    )
    out_specs = (
        P("expert", "dp", None),
        P("expert", "dp", None),
        P("expert", "dp", None),
        P("expert", "dp", None),
        P("expert", "dp", None),
        P("expert", "dp", None),
        P("dp", "expert"),
    )
    return jax.shard_map(local, mesh=mesh, in_specs=in_specs, out_specs=out_specs, check_vma=False)
```

```python
import jax
import jax.numpy as jnp
from jax import lax
from jax.experimental import pallas as pl
from jax.experimental.pallas import tpu as pltpu
from jax.sharding import PartitionSpec as P

TOK_DEV = 512
POOL = 2048
D = 2048
H = 512
N_EXPERT = 4
N_CHIP = 16
SLICE = 512
ROWS = 192

momentum_decay = 0.9
learning_rate = 0.05
epsilon = 1e-06

MIB = 1 << 20
F32 = jnp.float32
BF16 = jnp.bfloat16
NT = (((1,), (1,)), ((), ()))


def vmem():
    return pl.BlockSpec(memory_space=pltpu.VMEM)


def call(body, name, n_in, out_shapes, flops, nbytes, scratch=(), limit=20):
    return pl.pallas_call(
        body,
        name=name,
        out_shape=out_shapes,
        in_specs=[vmem()] * n_in,
        out_specs=jax.tree.map(lambda _: vmem(), out_shapes),
        scratch_shapes=list(scratch),
        compiler_params=pltpu.CompilerParams(vmem_limit_bytes=limit * MIB),
        cost_estimate=pl.CostEstimate(flops=flops, bytes_accessed=nbytes, transcendentals=0),
    )


def struct(shape, dtype):
    return jax.ShapeDtypeStruct(shape, dtype)


def column(row):
    return jnp.broadcast_to(row, (128, row.shape[1])).T


def pick_rows(ids_rows, pools, stacked=False):
    n_ids, n_pool = len(ids_rows), len(pools)

    def body(*refs):
        ids, src = refs[:n_ids], refs[n_ids : n_ids + n_pool]
        out, hot = refs[n_ids + n_pool : -1], refs[-1]
        lane = lax.broadcasted_iota(jnp.int32, (TOK_DEV, 128), 1)
        for k in range(n_ids):
            named = column(ids[k][...])
            for j in range(POOL // 128):
                hot[:, 128 * j : 128 * (j + 1)] = jnp.where(named == lane + 128 * j, 1.0, 0.0).astype(BF16)
            for a in range(n_pool):
                rows = jnp.dot(hot[...], src[a][...], preferred_element_type=F32).astype(BF16)
                if stacked:
                    out[k][TOK_DEV * a : TOK_DEV * (a + 1), :] = rows
                else:
                    out[k * n_pool + a][...] = rows

    shapes = [struct((TOK_DEV, SLICE), BF16)] * (n_ids * n_pool)
    if stacked:
        shapes = [struct((n_pool * TOK_DEV, SLICE), BF16)] * n_ids
    return call(
        body,
        "pick_rows",
        n_ids + n_pool,
        shapes,
        2 * TOK_DEV * POOL * SLICE * n_ids * n_pool,
        (4 + 2 * n_ids) * MIB // 2,
        [pltpu.VMEM((TOK_DEV, POOL), BF16)],
    )(*ids_rows, *pools)


def slice_of(k):
    me = lax.axis_index("expert")
    return lax.rem(me + N_EXPERT - k, N_EXPERT)


def in_up_block(w, s):
    return w[pl.ds(pl.multiple_of(8 * s, 8), 8), 0:64, :].reshape(SLICE, 2 * H)


def down_block(w, s):
    row = pl.multiple_of(64 + 16 * (s // 2), 16)
    col = pl.multiple_of(SLICE * (s % 2), SLICE)
    return w[:, pl.ds(row, 16), pl.ds(col, SLICE)].reshape(H, SLICE)


def forward(tokens, weights):
    def body(x0, x1, x2, x3, w, hidden_t, gate_factor, act_out, xt, acc, hid):
        for k, x in enumerate((x0, x1, x2, x3)):
            part = jnp.dot(x[0:TOK_DEV, :], in_up_block(w, slice_of(k)), preferred_element_type=F32)
            if k == 0:
                acc[...] = part
            else:
                acc[...] += part
            xt[k] = x[0:TOK_DEV, :].T

        @pl.loop(0, TOK_DEV // 64)
        def _(i):
            rows = pl.ds(pl.multiple_of(i * 64, 64), 64)
            gate, up = acc[rows, :H], acc[rows, H:]
            sig = jax.nn.sigmoid(gate)
            act = gate * sig
            hid[rows, :] = (act * up).astype(BF16)
            gate_factor[rows, :] = up * sig * (1.0 + gate * (1.0 - sig))
            act_out[rows, :] = act

        hidden_t[...] = hid[...].T

    shapes = [
        struct((H, TOK_DEV), BF16),
        struct((TOK_DEV, H), F32),
        struct((TOK_DEV, H), F32),
        struct((N_EXPERT, SLICE, TOK_DEV), BF16),
    ]
    return call(
        body,
        "forward",
        5,
        shapes,
        2 * TOK_DEV * D * 2 * H,
        10 * MIB,
        [pltpu.VMEM((TOK_DEV, 2 * H), F32), pltpu.VMEM((TOK_DEV, H), BF16)],
    )(*tokens, weights)


def of_cotangents(first, ks, cots, route, hid_t, w, hg, scaled, put):
    scale = column(route[...])
    for k, c in zip(ks, cots):
        for j in range(SLICE // 128):
            cols = slice(128 * j, 128 * (j + 1))
            rows = slice(c.shape[0] - TOK_DEV, c.shape[0])
            scaled[:, cols] = (scale * c[rows, cols].astype(F32)).astype(BF16)
        part = lax.dot_general(scaled[...], down_block(w, slice_of(k)), NT, preferred_element_type=F32)
        if first and k == ks[0]:
            hg[...] = part
        else:
            hg[...] += part
        down = jnp.dot(hid_t[...], scaled[...], preferred_element_type=F32) / TOK_DEV
        put(k, down.astype(BF16))


def backward_early(cots, route, hidden_t, weights):
    def body(c0, c2, route_ref, hid_t, w, hg, downs, scaled):
        def put(k, down):
            downs[k // 2] = down

        of_cotangents(True, (0, 2), (c0, c2), route_ref, hid_t, w, hg, scaled, put)

    shapes = [struct((TOK_DEV, H), F32), struct((2, H, SLICE), BF16)]
    scratch = [pltpu.VMEM((TOK_DEV, SLICE), BF16)]
    return call(body, "backward_early", 5, shapes, 2 * TOK_DEV * D * H, 8 * MIB, scratch)(
        *cots, route, hidden_t, weights
    )


def backward_down(cots, route, hidden_t, early, downs, weights):
    def body(c1, c3, route_ref, hid_t, hg0, down_ref, w, keep, send, hg, scaled):
        first = lax.axis_index("dp") % 2 == 0

        def put(k, down):
            down = down.reshape(N_CHIP, 2, 16, SLICE)
            rows = pl.ds(pl.multiple_of(16 * slice_of(k), 16), 16)
            keep[:, rows, :] = jnp.where(first, down[:, 0], down[:, 1])
            send[:, rows, :] = jnp.where(first, down[:, 1], down[:, 0])

        hg[...] = hg0[...]
        of_cotangents(False, (1, 3), (c1, c3), route_ref, hid_t, w, hg, scaled, put)
        put(0, down_ref[0])
        put(2, down_ref[1])

    half = struct((N_CHIP, 64, SLICE), BF16)
    shapes = [half, half, struct((TOK_DEV, H), F32)]
    scratch = [pltpu.VMEM((TOK_DEV, SLICE), BF16)]
    return call(body, "backward_down", 7, shapes, 2 * TOK_DEV * D * H, 10 * MIB, scratch)(
        *cots, route, hidden_t, early, downs, weights
    )


def backward_in(hidden_grad, gate_factor, act, xt):
    def body(hg, factor, act_ref, xt_ref, keep, send, both):
        first = lax.axis_index("dp") % 2 == 0

        @pl.loop(0, TOK_DEV // 64)
        def _(i):
            rows = pl.ds(pl.multiple_of(i * 64, 64), 64)
            g = hg[rows, :]
            both[rows, :H] = (g * factor[rows, :]).astype(BF16)
            both[rows, H:] = (g * act_ref[rows, :]).astype(BF16)

        for k in range(N_EXPERT):
            chips = pl.ds(pl.multiple_of(4 * slice_of(k), 4), 4)
            grad = jnp.dot(xt_ref[k], both[...], preferred_element_type=F32) / TOK_DEV
            grad = grad.astype(BF16).reshape(4, 2, 64, 2 * H)
            for a in range(2):
                own = grad[:, 0, :, a * H : (a + 1) * H]
                other = grad[:, 1, :, a * H : (a + 1) * H]
                keep[chips, 64 * a : 64 * (a + 1), :] = jnp.where(first, own, other)
                send[chips, 64 * a : 64 * (a + 1), :] = jnp.where(first, other, own)

    half = struct((N_CHIP, 128, SLICE), BF16)
    shapes = [half, half, struct((TOK_DEV, 2 * H), BF16)]
    return call(body, "backward_in", 4, shapes, 4 * TOK_DEV * D * H, 10 * MIB)(hidden_grad, gate_factor, act, xt)


def slot_gradients(both, weights):
    def body(both_ref, w, *out):
        for k in (2, 1, 3, 0):
            grad = lax.dot_general(both_ref[...], in_up_block(w, slice_of(k)), NT, preferred_element_type=F32)
            out[k][...] = grad.astype(BF16)

    shapes = [struct((TOK_DEV, SLICE), BF16)] * N_EXPERT
    return call(body, "slot_gradients", 2, shapes, 4 * TOK_DEV * D * H, 9 * MIB)(both, weights)


def rows_of(of_in, of_down, q, m):
    return of_down[q] if m == 2 else of_in[q, 64 * m : 64 * (m + 1), :]


def pair_moments(own, other):
    def body(a_in, a_down, b_in, b_down, out):
        def step(q, sums):
            new = []
            for m in range(3):
                a = rows_of(a_in, a_down, q, m).astype(F32)
                b = rows_of(b_in, b_down, q, m).astype(F32)
                for t in (a * b, a * a, b * b):
                    t = jnp.sum(t.reshape(8, 8, SLICE), axis=0)
                    new.append(t[:, :128] + t[:, 128:256] + t[:, 256:384] + t[:, 384:])
            return tuple(s + n for s, n in zip(sums, new))

        sums = lax.fori_loop(0, N_CHIP, step, (jnp.zeros((8, 128), F32),) * 9)
        for j in range(9):
            out[j] = sums[j]

    return call(body, "pair_moments", 4, struct((9, 8, 128), F32), 9 * 2**20, 6 * MIB)(*own, *other)


def pair_merge(own, other, mine, theirs):
    def body(a_in, a_down, b_in, b_down, m_ref, t_ref, *out):
        coefs = []
        for m in range(3):
            inner = jnp.sum(m_ref[3 * m] + t_ref[3 * m], keepdims=True)
            norm_a = jnp.sum(m_ref[3 * m + 1] + t_ref[3 * m + 2], keepdims=True)
            norm_b = jnp.sum(m_ref[3 * m + 2] + t_ref[3 * m + 1], keepdims=True)
            coef_a = 1.0 - inner / (2.0 * (norm_a + epsilon))
            coef_b = 1.0 - inner / (2.0 * (norm_b + epsilon))
            coefs.append((jnp.broadcast_to(coef_a, (64, SLICE)), jnp.broadcast_to(coef_b, (64, SLICE))))
        c, at = place(0)

        @pl.loop(0, 4)
        def _(j):
            for k in range(4):
                first = lax.rem(at + k, 4)
                q = jnp.where(c == 0, 4 * j + first, 4 * first + j)
                for m in range(3):
                    rows = slice(64 * m, 64 * (m + 1))
                    a = rows_of(a_in, a_down, q, m).astype(F32)
                    b = rows_of(b_in, b_down, q, m).astype(F32)
                    out[k][j, rows, :] = (coefs[m][0] * a + coefs[m][1] * b).astype(BF16)

    return call(body, "pair_merge", 6, [struct((4, ROWS, SLICE), BF16)] * 4, 9 * 2**20, 9 * MIB)(
        *own, *other, mine, theirs
    )


def turn_over(parts):
    def body(*refs):
        (_, first), (_, second) = place(0), place(1)
        for k in range(4):
            for m in range(4):
                refs[4 + k][lax.rem(first + 4 - m, 4)] = refs[m][lax.rem(second + k, 4)]

    return call(body, "turn_over", 4, [struct((4, ROWS, SLICE), BF16)] * 4, 2**10, 6 * MIB)(*parts)


def origin(index):
    c, second = place(1)
    other = (second + 4 - (index >> 2)) & 3
    return jnp.where(c == 0, other * 4 + (index & 3), (index & 3) * 4 + other)


def gram(parts):
    def body(*refs):
        x, out = refs[:4], refs[4]
        row = lax.broadcasted_iota(jnp.int32, (256, 256), 0)
        col = lax.broadcasted_iota(jnp.int32, (256, 256), 1)
        same = jnp.where(row % 16 == col % 16, 1.0, 0.0)
        fold = origin(lax.broadcasted_iota(jnp.int32, (256, 128), 0) // 16)
        fold = jnp.where(fold == lax.broadcasted_iota(jnp.int32, (256, 128), 1), 1.0, 0.0)
        order = origin(lax.broadcasted_iota(jnp.int32, (16, 16), 1))
        order = jnp.where(order == lax.broadcasted_iota(jnp.int32, (16, 16), 0), 1.0, 0.0)
        exact = dict(precision=lax.Precision.HIGHEST, preferred_element_type=F32)
        for m in range(3):
            acc = None
            for b in range(4):
                at = 64 * m + 16 * b
                block = jnp.concatenate([r[:, at : at + 16, :].reshape(64, SLICE) for r in x], axis=0)
                part = lax.dot_general(block, block, NT, preferred_element_type=F32)
                acc = part if acc is None else acc + part
            acc = jnp.sum((acc * same).reshape(16, 16, 256), axis=1)
            out[m] = jnp.dot(order, jnp.dot(acc, fold, **exact), **exact)

    return call(body, "gram", 4, struct((3, 16, 128), F32), 12 * 2 * 256 * 256 * 512, 3 * MIB)(*parts)


def finish(parts, products, gate, up, down, mom_gate, mom_up, mom_down):
    def body(x0, x1, x2, x3, g_ref, g_other, gate_w, up_w, down_w, gate_m, up_m, down_m, new_g, new_u, new_d, next_g, next_u, next_d):
        g = g_ref[...] + g_other[...]
        i = lax.broadcasted_iota(jnp.int32, (3, 16, 128), 1)
        j = lax.broadcasted_iota(jnp.int32, (3, 16, 128), 2)
        c_col = jnp.ones((3, 16, 1), F32)
        c_row = jnp.ones((3, 1, 128), F32)
        for level in range(4):
            block_i, block_j = i >> level, j >> level
            same, sibling = block_i == block_j, (block_i ^ 1) == block_j
            weighted = g * c_col * c_row
            within = jnp.where(same, weighted, 0.0)
            across = jnp.where(sibling, weighted, 0.0)

            def coef(axis):
                norm = jnp.sum(jnp.where(same, jnp.sum(within, axis=3 - axis, keepdims=True), 0.0), axis=axis, keepdims=True)
                inner = jnp.sum(jnp.where(same, jnp.sum(across, axis=3 - axis, keepdims=True), 0.0), axis=axis, keepdims=True)
                return 1.0 - inner / (2.0 * (jnp.maximum(norm, 0.0) + epsilon))

            c_col, c_row = c_col * coef(2), c_row * coef(1)
        chip = origin(lax.broadcasted_iota(jnp.int32, (16, 128), 0))
        chip = chip == lax.broadcasted_iota(jnp.int32, (16, 128), 1)
        c_col = jnp.sum(jnp.where(chip, c_row, 0.0), axis=2, keepdims=True)
        olds = ((gate_w, gate_m, new_g, next_g), (up_w, up_m, new_u, next_u))
        for m in range(3):
            merged = jnp.zeros((64, SLICE), F32)
            for q in range(16):
                scale = jnp.broadcast_to(c_col[m, q : q + 1, :], (64, SLICE))
                x = (x0, x1, x2, x3)[q // 4]
                merged += scale * x[q % 4, 64 * m : 64 * (m + 1), :].astype(F32)
            if m < 2:
                w, mom, new, after = olds[m]
                step = momentum_decay * mom[...] + merged
                after[...] = step
                new[...] = w[...] - learning_rate * step
            else:
                for k in range(4):
                    cols = slice(SLICE * k, SLICE * (k + 1))
                    step = momentum_decay * down_m[:, cols] + merged[16 * k : 16 * (k + 1), :]
                    next_d[:, cols] = step
                    new_d[:, cols] = down_w[:, cols] - learning_rate * step

    wide, tall = struct((64, H), F32), struct((16, D), F32)
    return call(body, "finish", 12, [wide, wide, tall, wide, wide, tall], 2**22, 6 * MIB)(
        *parts, *products, gate, up, down, mom_gate, mom_up, mom_down
    )


def scatter_rows(ids_rows, grads, half, into=()):
    block, steps = 512, POOL // 1024

    def body(*refs):
        row = lax.broadcasted_iota(jnp.int32, (block, TOK_DEV), 0)
        row += block * (pl.program_id(0) + steps * half)
        acc = None
        for ids, g in zip(refs[:4], refs[4:8]):
            hot = jnp.where(jnp.broadcast_to(ids[...], row.shape) == row, 1.0, 0.0).astype(BF16)
            part = jnp.dot(hot, g[...], preferred_element_type=F32)
            acc = part if acc is None else acc + part
        refs[-1][...] = acc

    return pl.pallas_call(
        body,
        name="scatter_rows",
        grid=(steps,),
        out_shape=struct((POOL, SLICE), F32),
        in_specs=[vmem()] * 8 + [pl.BlockSpec(memory_space=pl.ANY)] * len(into),
        out_specs=pl.BlockSpec((block, SLICE), lambda i: (i + steps * half, 0)),
        input_output_aliases={8: 0} if into else {},
        compiler_params=pltpu.CompilerParams(vmem_limit_bytes=24 * MIB),
        cost_estimate=pl.CostEstimate(flops=POOL * POOL * SLICE, bytes_accessed=4 * MIB, transcendentals=0),
    )(*ids_rows, *grads, *into)


def shift(block, axis, to):
    return lax.ppermute(block, axis, [(i, to(i)) for i in range(lax.axis_size(axis))])


def around_y(block, k):
    return shift(block, "expert", lambda i: (i + k) % N_EXPERT)


def around_z(block, k):
    return shift(block, "dp", lambda i: i // 8 * 8 + (i // 2 % 4 + k) % 4 * 2 + i % 2)


def around_x(block, k):
    return shift(block, "dp", lambda i: (i // 8 + k) % 4 * 8 + i % 8)


def other_core(block):
    return shift(block, "dp", lambda i: i ^ 1)


def sum_dp(value, ids, grads):
    pool = ()
    for half, around in enumerate((around_z, around_x)):
        others = [around(value, k) for k in (2, 1, 3)]
        others, pool = lax.optimization_barrier((others, (scatter_rows(ids, grads, half, pool),)))
        value = value + sum(others)
    return (value, other_core(value)), pool[0]


def pack(gate, up, down):
    def body(gate_hbm, up_hbm, down_hbm, out, g, u, d, sems):
        copies = [
            pltpu.make_async_copy(src, dst, sems.at[j])
            for j, (src, dst) in enumerate(((gate_hbm, g), (up_hbm, u), (down_hbm, d)))
        ]
        for copy in copies:
            copy.start()
        for copy in copies:
            copy.wait()
        out[0:64, 0:H] = g[...].astype(BF16)
        out[0:64, H:] = u[...].astype(BF16)
        out[64:80, :] = d[:, : D // 2].astype(BF16)
        out[80:96, :] = d[:, D // 2 :].astype(BF16)

    return pl.pallas_call(
        body,
        name="pack",
        out_shape=struct((96, 1024), BF16),
        in_specs=[pl.BlockSpec(memory_space=pl.ANY)] * 3,
        out_specs=vmem(),
        scratch_shapes=[
            pltpu.VMEM((64, H), F32),
            pltpu.VMEM((64, H), F32),
            pltpu.VMEM((16, D), F32),
            pltpu.SemaphoreType.DMA((3,)),
        ],
        compiler_params=pltpu.CompilerParams(vmem_limit_bytes=8 * MIB),
        cost_estimate=pl.CostEstimate(flops=2**17, bytes_accessed=MIB, transcendentals=0),
    )(gate, up, down)


def along(turn, step):
    def to(i):
        x, z, c = i // 8, i // 2 % 4, i % 2
        return x * 8 + (z + step) % 4 * 2 + c if c == turn else (x + step) % 4 * 8 + z * 2 + c

    return to


def to_others(blocks, turn):
    out = {k: shift(blocks[k], "dp", along(turn, k)) for k in (2, 1, 3)}
    return [out[1], out[2], out[3]]


def tie_far(items, others, last=False):
    order = (3, 1, 2, 0) if last else (2, 1, 3, 0)
    tied, others = lax.optimization_barrier(([items[k] for k in order], others))
    return [tied[order.index(k)] for k in range(4)], others


def spread(block, turn):
    return to_others([block] * 4, turn)


def place(turn):
    at = lax.axis_index("dp")
    x, z, c = at // 8, lax.rem(at // 2, 4), lax.rem(at, 2)
    return c, jnp.where(c == turn, z, x)


def bundle(blocks):
    def body(*refs):
        _, at = place(0)
        for k in range(4):
            refs[4][lax.rem(at + 4 - k, 4)] = refs[k][...]

    return call(body, "bundle", 4, struct((4, 96, 1024), BF16), 2**10, 2 * MIB)(*blocks)


def half_of_weights(bundles):
    def body(*refs):
        c, at = place(1)
        for k in range(4):
            other = lax.rem(at + 4 - k, 4)
            for j in range(4):
                refs[4][jnp.where(c == 0, other * 4 + j, j * 4 + other)] = refs[k][j]

    return call(body, "half_of_weights", 4, struct((N_CHIP, 96, 1024), BF16), 2**10, 6 * MIB)(*bundles)


def whole_weights(own, other):
    def body(a, b, out):
        c = lax.rem(lax.axis_index("dp"), 2)

        @pl.loop(0, N_CHIP)
        def _(q):
            out[2 * q + c] = a[q]
            out[2 * q + 1 - c] = b[q]

    return call(body, "whole_weights", 2, struct((2 * N_CHIP, 96, 1024), BF16), 2**10, 12 * MIB)(own, other)


def local(
    pool_tokens,
    pool_cotangent,
    token_ids,
    route_weights,
    gate_weight,
    up_weight,
    down_weight,
    momentum_gate,
    momentum_up,
    momentum_down,
):
    tie = lax.optimization_barrier

    def picked(k, pool):
        return pick_rows(ids[k : k + 1], [pool])[0]

    ids = [token_ids] + [around_y(token_ids, N_EXPERT - k) for k in (1, 2, 3)]
    x, c = [None] * 4, [None] * 4
    x[1], x[3] = picked(1, pool_tokens), picked(3, pool_tokens)
    ids, x[1], x[3], shards = tie((ids, x[1], x[3], (gate_weight[0], up_weight[0], down_weight[0])))

    packed = pack(*shards)
    blocks = spread(packed, 0)
    x[1], x[3] = around_y(x[1], 1), around_y(x[3], 3)
    (x[2],) = pick_rows(ids[2:3], [pool_tokens, pool_cotangent], stacked=True)
    blocks, (ids, x[1:]) = tie_far([packed, *blocks], (ids, x[1:]), last=True)

    block = bundle(blocks)
    blocks = spread(block, 1)
    x[2] = c[2] = around_y(x[2], 2)
    c[1], c[3] = picked(1, pool_cotangent), picked(3, pool_cotangent)
    x[0], c[0] = pick_rows(ids[:1], [pool_tokens, pool_cotangent])
    blocks, (x, c) = tie_far([block, *blocks], (x, [c[0], c[1], c[3]]), last=True)
    c = [c[0], c[1], x[2], c[2]]

    mine = half_of_weights(blocks)
    weights = whole_weights(mine, other_core(mine))
    c[1], c[3] = around_y(c[1], 1), around_y(c[3], 3)

    hidden_t, gate_factor, act, xt = forward(x, weights)
    early, downs = backward_early((c[0], c[2]), route_weights, hidden_t, weights)
    keep_down, send_down, hidden_grad = backward_down((c[1], c[3]), route_weights, hidden_t, early, downs, weights)
    keep_in, send_in, both = backward_in(hidden_grad, gate_factor, act, xt)
    received_down, send_in = tie((other_core(send_down), send_in))
    keep, received = (keep_in, keep_down), (other_core(send_in), received_down)
    slots = slot_gradients(both, weights)
    received, slots = lax.optimization_barrier((received, list(slots)))

    mine = pair_moments(keep, received)
    sent = pair_merge(keep, received, mine, other_core(mine))
    parts = [sent[0], *to_others(sent, 0)]
    back = [slots[0], None, around_y(slots[2], 2), None]
    parts, back[2] = tie_far(parts, back[2])
    sent, slots[1], slots[3] = tie((turn_over(parts), slots[1], slots[3]))
    parts = [sent[0], *to_others(sent, 1)]
    back[1], back[3] = around_y(slots[1], 3), around_y(slots[3], 1)
    parts, (back[1], back[3]) = tie_far(parts, (back[1], back[3]))
    products, pool_grad = sum_dp(gram(parts), ids, back)
    outs = finish(
        parts,
        products,
        gate_weight[0],
        up_weight[0],
        down_weight[0],
        momentum_gate[0],
        momentum_up[0],
        momentum_down[0],
    )
    return (*(a[None] for a in outs), pool_grad)


def solution(mesh):
    in_specs = (
        P("dp", "expert"),
        P("dp", "expert"),
        P("expert", "dp"),
        P("expert", "dp"),
        P("expert", "dp", None),
        P("expert", "dp", None),
        P("expert", "dp", None),
        P("expert", "dp", None),
        P("expert", "dp", None),
        P("expert", "dp", None),
    )
    out_specs = (
        P("expert", "dp", None),
        P("expert", "dp", None),
        P("expert", "dp", None),
        P("expert", "dp", None),
        P("expert", "dp", None),
        P("expert", "dp", None),
        P("dp", "expert"),
    )
    return jax.shard_map(local, mesh=mesh, in_specs=in_specs, out_specs=out_specs, check_vma=False)
```

```python
import jax
import jax.numpy as jnp
from jax import lax
from jax.experimental import pallas as pl
from jax.experimental.pallas import tpu as pltpu
from jax.sharding import PartitionSpec as P

TOK_DEV = 512
POOL = 2048
D = 2048
H = 512
N_EXPERT = 4
N_CHIP = 16
SLICE = 512
ROWS = 192

momentum_decay = 0.9
learning_rate = 0.05
epsilon = 1e-06

MIB = 1 << 20
F32 = jnp.float32
BF16 = jnp.bfloat16
NT = (((1,), (1,)), ((), ()))


def vmem():
    return pl.BlockSpec(memory_space=pltpu.VMEM)


def call(body, name, n_in, out_shapes, flops, nbytes, scratch=(), limit=20):
    return pl.pallas_call(
        body,
        name=name,
        out_shape=out_shapes,
        in_specs=[vmem()] * n_in,
        out_specs=jax.tree.map(lambda _: vmem(), out_shapes),
        scratch_shapes=list(scratch),
        compiler_params=pltpu.CompilerParams(vmem_limit_bytes=limit * MIB),
        cost_estimate=pl.CostEstimate(flops=flops, bytes_accessed=nbytes, transcendentals=0),
    )


def struct(shape, dtype):
    return jax.ShapeDtypeStruct(shape, dtype)


def column(row):
    return jnp.broadcast_to(row, (128, row.shape[1])).T


def pick_rows(ids_rows, pools, stacked=False):
    n_ids, n_pool = len(ids_rows), len(pools)

    def body(*refs):
        ids, src = refs[:n_ids], refs[n_ids : n_ids + n_pool]
        out, hot = refs[n_ids + n_pool : -1], refs[-1]
        lane = lax.broadcasted_iota(jnp.int32, (TOK_DEV, 128), 1)
        for k in range(n_ids):
            named = column(ids[k][...])
            for j in range(POOL // 128):
                hot[:, 128 * j : 128 * (j + 1)] = jnp.where(named == lane + 128 * j, 1.0, 0.0).astype(BF16)
            for a in range(n_pool):
                rows = jnp.dot(hot[...], src[a][...], preferred_element_type=F32).astype(BF16)
                if stacked:
                    out[k][TOK_DEV * a : TOK_DEV * (a + 1), :] = rows
                else:
                    out[k * n_pool + a][...] = rows

    shapes = [struct((TOK_DEV, SLICE), BF16)] * (n_ids * n_pool)
    if stacked:
        shapes = [struct((n_pool * TOK_DEV, SLICE), BF16)] * n_ids
    return call(
        body,
        "pick_rows",
        n_ids + n_pool,
        shapes,
        2 * TOK_DEV * POOL * SLICE * n_ids * n_pool,
        (4 + 2 * n_ids) * MIB // 2,
        [pltpu.VMEM((TOK_DEV, POOL), BF16)],
    )(*ids_rows, *pools)


def slice_of(k):
    me = lax.axis_index("expert")
    return lax.rem(me + N_EXPERT - k, N_EXPERT)


def in_up_block(w, s):
    return w[pl.ds(pl.multiple_of(8 * s, 8), 8), 0:64, :].reshape(SLICE, 2 * H)


def down_block(w, s):
    row = pl.multiple_of(64 + 16 * (s // 2), 16)
    col = pl.multiple_of(SLICE * (s % 2), SLICE)
    return w[:, pl.ds(row, 16), pl.ds(col, SLICE)].reshape(H, SLICE)


def forward(tokens, weights):
    def body(x0, x1, x2, x3, w, hidden_t, gate_factor, act_out, xt, acc, hid):
        for k, x in enumerate((x0, x1, x2, x3)):
            part = jnp.dot(x[0:TOK_DEV, :], in_up_block(w, slice_of(k)), preferred_element_type=F32)
            if k == 0:
                acc[...] = part
            else:
                acc[...] += part
            xt[k] = x[0:TOK_DEV, :].T

        @pl.loop(0, TOK_DEV // 64)
        def _(i):
            rows = pl.ds(pl.multiple_of(i * 64, 64), 64)
            gate, up = acc[rows, :H], acc[rows, H:]
            sig = jax.nn.sigmoid(gate)
            act = gate * sig
            hid[rows, :] = (act * up).astype(BF16)
            gate_factor[rows, :] = up * sig * (1.0 + gate * (1.0 - sig))
            act_out[rows, :] = act

        hidden_t[...] = hid[...].T

    shapes = [
        struct((H, TOK_DEV), BF16),
        struct((TOK_DEV, H), F32),
        struct((TOK_DEV, H), F32),
        struct((N_EXPERT, SLICE, TOK_DEV), BF16),
    ]
    return call(
        body,
        "forward",
        5,
        shapes,
        2 * TOK_DEV * D * 2 * H,
        10 * MIB,
        [pltpu.VMEM((TOK_DEV, 2 * H), F32), pltpu.VMEM((TOK_DEV, H), BF16)],
    )(*tokens, weights)


def of_cotangents(first, ks, cots, route, hid_t, w, hg, scaled, put):
    scale = column(route[...])
    for k, c in zip(ks, cots):
        for j in range(SLICE // 128):
            cols = slice(128 * j, 128 * (j + 1))
            rows = slice(c.shape[0] - TOK_DEV, c.shape[0])
            scaled[:, cols] = (scale * c[rows, cols].astype(F32)).astype(BF16)
        part = lax.dot_general(scaled[...], down_block(w, slice_of(k)), NT, preferred_element_type=F32)
        if first and k == ks[0]:
            hg[...] = part
        else:
            hg[...] += part
        down = jnp.dot(hid_t[...], scaled[...], preferred_element_type=F32) / TOK_DEV
        put(k, down.astype(BF16))


def backward_early(cots, route, hidden_t, weights):
    def body(c0, c2, route_ref, hid_t, w, hg, downs, scaled):
        def put(k, down):
            downs[k // 2] = down

        of_cotangents(True, (0, 2), (c0, c2), route_ref, hid_t, w, hg, scaled, put)

    shapes = [struct((TOK_DEV, H), F32), struct((2, H, SLICE), BF16)]
    scratch = [pltpu.VMEM((TOK_DEV, SLICE), BF16)]
    return call(body, "backward_early", 5, shapes, 2 * TOK_DEV * D * H, 8 * MIB, scratch)(
        *cots, route, hidden_t, weights
    )


def backward_down(cots, route, hidden_t, early, downs, weights):
    def body(c1, c3, route_ref, hid_t, hg0, down_ref, w, keep, send, hg, scaled):
        first = lax.axis_index("dp") % 2 == 0

        def put(k, down):
            down = down.reshape(N_CHIP, 2, 16, SLICE)
            rows = pl.ds(pl.multiple_of(16 * slice_of(k), 16), 16)
            keep[:, rows, :] = jnp.where(first, down[:, 0], down[:, 1])
            send[:, rows, :] = jnp.where(first, down[:, 1], down[:, 0])

        hg[...] = hg0[...]
        of_cotangents(False, (1, 3), (c1, c3), route_ref, hid_t, w, hg, scaled, put)
        put(0, down_ref[0])
        put(2, down_ref[1])

    half = struct((N_CHIP, 64, SLICE), BF16)
    shapes = [half, half, struct((TOK_DEV, H), F32)]
    scratch = [pltpu.VMEM((TOK_DEV, SLICE), BF16)]
    return call(body, "backward_down", 7, shapes, 2 * TOK_DEV * D * H, 10 * MIB, scratch)(
        *cots, route, hidden_t, early, downs, weights
    )


def backward_in(hidden_grad, gate_factor, act, xt):
    def body(hg, factor, act_ref, xt_ref, keep, send, both):
        first = lax.axis_index("dp") % 2 == 0

        @pl.loop(0, TOK_DEV // 64)
        def _(i):
            rows = pl.ds(pl.multiple_of(i * 64, 64), 64)
            g = hg[rows, :]
            both[rows, :H] = (g * factor[rows, :]).astype(BF16)
            both[rows, H:] = (g * act_ref[rows, :]).astype(BF16)

        for k in range(N_EXPERT):
            chips = pl.ds(pl.multiple_of(4 * slice_of(k), 4), 4)
            grad = jnp.dot(xt_ref[k], both[...], preferred_element_type=F32) / TOK_DEV
            grad = grad.astype(BF16).reshape(4, 2, 64, 2 * H)
            for a in range(2):
                own = grad[:, 0, :, a * H : (a + 1) * H]
                other = grad[:, 1, :, a * H : (a + 1) * H]
                keep[chips, 64 * a : 64 * (a + 1), :] = jnp.where(first, own, other)
                send[chips, 64 * a : 64 * (a + 1), :] = jnp.where(first, other, own)

    half = struct((N_CHIP, 128, SLICE), BF16)
    shapes = [half, half, struct((TOK_DEV, 2 * H), BF16)]
    return call(body, "backward_in", 4, shapes, 4 * TOK_DEV * D * H, 10 * MIB)(hidden_grad, gate_factor, act, xt)


def slot_gradients(both, weights):
    def body(both_ref, w, *out):
        for k in (2, 1, 3, 0):
            grad = lax.dot_general(both_ref[...], in_up_block(w, slice_of(k)), NT, preferred_element_type=F32)
            out[k][...] = grad.astype(BF16)

    shapes = [struct((TOK_DEV, SLICE), BF16)] * N_EXPERT
    return call(body, "slot_gradients", 2, shapes, 4 * TOK_DEV * D * H, 9 * MIB)(both, weights)


def rows_of(of_in, of_down, q, m):
    return of_down[q] if m == 2 else of_in[q, 64 * m : 64 * (m + 1), :]


def pair_moments(own, other):
    def body(a_in, a_down, b_in, b_down, out):
        def step(q, sums):
            new = []
            for m in range(3):
                a = rows_of(a_in, a_down, q, m).astype(F32)
                b = rows_of(b_in, b_down, q, m).astype(F32)
                for t in (a * b, a * a, b * b):
                    t = jnp.sum(t.reshape(8, 8, SLICE), axis=0)
                    new.append(t[:, :128] + t[:, 128:256] + t[:, 256:384] + t[:, 384:])
            return tuple(s + n for s, n in zip(sums, new))

        sums = lax.fori_loop(0, N_CHIP, step, (jnp.zeros((8, 128), F32),) * 9)
        for j in range(9):
            out[j] = sums[j]

    return call(body, "pair_moments", 4, struct((9, 8, 128), F32), 9 * 2**20, 6 * MIB)(*own, *other)


def pair_merge(own, other, mine, theirs):
    def body(a_in, a_down, b_in, b_down, m_ref, t_ref, *out):
        coefs = []
        for m in range(3):
            inner = jnp.sum(m_ref[3 * m] + t_ref[3 * m], keepdims=True)
            norm_a = jnp.sum(m_ref[3 * m + 1] + t_ref[3 * m + 2], keepdims=True)
            norm_b = jnp.sum(m_ref[3 * m + 2] + t_ref[3 * m + 1], keepdims=True)
            coef_a = 1.0 - inner / (2.0 * (norm_a + epsilon))
            coef_b = 1.0 - inner / (2.0 * (norm_b + epsilon))
            coefs.append((jnp.broadcast_to(coef_a, (64, SLICE)), jnp.broadcast_to(coef_b, (64, SLICE))))
        c, at = place(0)

        @pl.loop(0, 4)
        def _(j):
            for k in range(4):
                first = lax.rem(at + k, 4)
                q = jnp.where(c == 0, 4 * j + first, 4 * first + j)
                for m in range(3):
                    rows = slice(64 * m, 64 * (m + 1))
                    a = rows_of(a_in, a_down, q, m).astype(F32)
                    b = rows_of(b_in, b_down, q, m).astype(F32)
                    out[k][j, rows, :] = (coefs[m][0] * a + coefs[m][1] * b).astype(BF16)

    return call(body, "pair_merge", 6, [struct((4, ROWS, SLICE), BF16)] * 4, 9 * 2**20, 9 * MIB)(
        *own, *other, mine, theirs
    )


def turn_over(parts):
    def body(*refs):
        (_, first), (_, second) = place(0), place(1)
        for k in range(4):
            for m in range(4):
                refs[4 + k][lax.rem(first + 4 - m, 4)] = refs[m][lax.rem(second + k, 4)]

    return call(body, "turn_over", 4, [struct((4, ROWS, SLICE), BF16)] * 4, 2**10, 6 * MIB)(*parts)


def origin(index):
    c, second = place(1)
    other = (second + 4 - (index >> 2)) & 3
    return jnp.where(c == 0, other * 4 + (index & 3), (index & 3) * 4 + other)


def gram(parts):
    def body(*refs):
        x, out = refs[:4], refs[4]
        row = lax.broadcasted_iota(jnp.int32, (256, 256), 0)
        col = lax.broadcasted_iota(jnp.int32, (256, 256), 1)
        same = jnp.where(row % 16 == col % 16, 1.0, 0.0)
        fold = origin(lax.broadcasted_iota(jnp.int32, (256, 128), 0) // 16)
        fold = jnp.where(fold == lax.broadcasted_iota(jnp.int32, (256, 128), 1), 1.0, 0.0)
        order = origin(lax.broadcasted_iota(jnp.int32, (16, 16), 1))
        order = jnp.where(order == lax.broadcasted_iota(jnp.int32, (16, 16), 0), 1.0, 0.0)
        exact = dict(precision=lax.Precision.HIGHEST, preferred_element_type=F32)
        for m in range(3):
            acc = None
            for b in range(4):
                at = 64 * m + 16 * b
                block = jnp.concatenate([r[:, at : at + 16, :].reshape(64, SLICE) for r in x], axis=0)
                part = lax.dot_general(block, block, NT, preferred_element_type=F32)
                acc = part if acc is None else acc + part
            acc = jnp.sum((acc * same).reshape(16, 16, 256), axis=1)
            out[m] = jnp.dot(order, jnp.dot(acc, fold, **exact), **exact)

    return call(body, "gram", 4, struct((3, 16, 128), F32), 12 * 2 * 256 * 256 * 512, 3 * MIB)(*parts)


def finish(parts, products, gate, up, down, mom_gate, mom_up, mom_down):
    def body(x0, x1, x2, x3, g_ref, g_other, gate_w, up_w, down_w, gate_m, up_m, down_m, new_g, new_u, new_d, next_g, next_u, next_d):
        g = g_ref[...] + g_other[...]
        i = lax.broadcasted_iota(jnp.int32, (3, 16, 128), 1)
        j = lax.broadcasted_iota(jnp.int32, (3, 16, 128), 2)
        c_col = jnp.ones((3, 16, 1), F32)
        c_row = jnp.ones((3, 1, 128), F32)
        for level in range(4):
            block_i, block_j = i >> level, j >> level
            same, sibling = block_i == block_j, (block_i ^ 1) == block_j
            weighted = g * c_col * c_row
            within = jnp.where(same, weighted, 0.0)
            across = jnp.where(sibling, weighted, 0.0)

            def coef(axis):
                norm = jnp.sum(jnp.where(same, jnp.sum(within, axis=3 - axis, keepdims=True), 0.0), axis=axis, keepdims=True)
                inner = jnp.sum(jnp.where(same, jnp.sum(across, axis=3 - axis, keepdims=True), 0.0), axis=axis, keepdims=True)
                return 1.0 - inner / (2.0 * (jnp.maximum(norm, 0.0) + epsilon))

            c_col, c_row = c_col * coef(2), c_row * coef(1)
        chip = origin(lax.broadcasted_iota(jnp.int32, (16, 128), 0))
        chip = chip == lax.broadcasted_iota(jnp.int32, (16, 128), 1)
        c_col = jnp.sum(jnp.where(chip, c_row, 0.0), axis=2, keepdims=True)
        olds = ((gate_w, gate_m, new_g, next_g), (up_w, up_m, new_u, next_u))
        for m in range(3):
            merged = jnp.zeros((64, SLICE), F32)
            for q in range(16):
                scale = jnp.broadcast_to(c_col[m, q : q + 1, :], (64, SLICE))
                x = (x0, x1, x2, x3)[q // 4]
                merged += scale * x[q % 4, 64 * m : 64 * (m + 1), :].astype(F32)
            if m < 2:
                w, mom, new, after = olds[m]
                step = momentum_decay * mom[...] + merged
                after[...] = step
                new[...] = w[...] - learning_rate * step
            else:
                for k in range(4):
                    cols = slice(SLICE * k, SLICE * (k + 1))
                    step = momentum_decay * down_m[:, cols] + merged[16 * k : 16 * (k + 1), :]
                    next_d[:, cols] = step
                    new_d[:, cols] = down_w[:, cols] - learning_rate * step

    wide, tall = struct((64, H), F32), struct((16, D), F32)
    return call(body, "finish", 12, [wide, wide, tall, wide, wide, tall], 2**22, 6 * MIB)(
        *parts, *products, gate, up, down, mom_gate, mom_up, mom_down
    )


def scatter_rows(ids_rows, grads, half, into=()):
    block, steps = 512, POOL // 1024

    def body(*refs):
        row = lax.broadcasted_iota(jnp.int32, (block, TOK_DEV), 0)
        row += block * (pl.program_id(0) + steps * half)
        acc = None
        for ids, g in zip(refs[:4], refs[4:8]):
            hot = jnp.where(jnp.broadcast_to(ids[...], row.shape) == row, 1.0, 0.0).astype(BF16)
            part = jnp.dot(hot, g[...], preferred_element_type=F32)
            acc = part if acc is None else acc + part
        refs[-1][...] = acc

    return pl.pallas_call(
        body,
        name="scatter_rows",
        grid=(steps,),
        out_shape=struct((POOL, SLICE), F32),
        in_specs=[vmem()] * 8 + [pl.BlockSpec(memory_space=pl.ANY)] * len(into),
        out_specs=pl.BlockSpec((block, SLICE), lambda i: (i + steps * half, 0)),
        input_output_aliases={8: 0} if into else {},
        compiler_params=pltpu.CompilerParams(vmem_limit_bytes=24 * MIB),
        cost_estimate=pl.CostEstimate(flops=POOL * POOL * SLICE, bytes_accessed=4 * MIB, transcendentals=0),
    )(*ids_rows, *grads, *into)


def shift(block, axis, to):
    return lax.ppermute(block, axis, [(i, to(i)) for i in range(lax.axis_size(axis))])


def around_y(block, k):
    return shift(block, "expert", lambda i: (i + k) % N_EXPERT)


def around_z(block, k):
    return shift(block, "dp", lambda i: i // 8 * 8 + (i // 2 % 4 + k) % 4 * 2 + i % 2)


def around_x(block, k):
    return shift(block, "dp", lambda i: (i // 8 + k) % 4 * 8 + i % 8)


def other_core(block):
    return shift(block, "dp", lambda i: i ^ 1)


def sum_dp(value, ids, grads):
    pool = ()
    for half, around in enumerate((around_z, around_x)):
        others = [around(value, k) for k in (2, 1, 3)]
        others, pool = lax.optimization_barrier((others, (scatter_rows(ids, grads, half, pool),)))
        value = value + sum(others)
    return (value, other_core(value)), pool[0]


def pack(gate, up, down):
    def body(gate_hbm, up_hbm, down_hbm, out, g, u, d, sems):
        copies = [
            pltpu.make_async_copy(src, dst, sems.at[j])
            for j, (src, dst) in enumerate(((gate_hbm, g), (up_hbm, u), (down_hbm, d)))
        ]
        for copy in copies:
            copy.start()
        for copy in copies:
            copy.wait()
        out[0:64, 0:H] = g[...].astype(BF16)
        out[0:64, H:] = u[...].astype(BF16)
        out[64:80, :] = d[:, : D // 2].astype(BF16)
        out[80:96, :] = d[:, D // 2 :].astype(BF16)

    return pl.pallas_call(
        body,
        name="pack",
        out_shape=struct((96, 1024), BF16),
        in_specs=[pl.BlockSpec(memory_space=pl.ANY)] * 3,
        out_specs=vmem(),
        scratch_shapes=[
            pltpu.VMEM((64, H), F32),
            pltpu.VMEM((64, H), F32),
            pltpu.VMEM((16, D), F32),
            pltpu.SemaphoreType.DMA((3,)),
        ],
        compiler_params=pltpu.CompilerParams(vmem_limit_bytes=8 * MIB),
        cost_estimate=pl.CostEstimate(flops=2**17, bytes_accessed=MIB, transcendentals=0),
    )(gate, up, down)


def along(turn, step):
    def to(i):
        x, z, c = i // 8, i // 2 % 4, i % 2
        return x * 8 + (z + step) % 4 * 2 + c if c == turn else (x + step) % 4 * 8 + z * 2 + c

    return to


def to_others(blocks, turn):
    out = {k: shift(blocks[k], "dp", along(turn, k)) for k in (2, 1, 3)}
    return [out[1], out[2], out[3]]


def tie_far(items, others, last=False):
    order = (3, 1, 2, 0) if last else (2, 1, 3, 0)
    tied, others = lax.optimization_barrier(([items[k] for k in order], others))
    return [tied[order.index(k)] for k in range(4)], others


def spread(block, turn):
    return to_others([block] * 4, turn)


def place(turn):
    at = lax.axis_index("dp")
    x, z, c = at // 8, lax.rem(at // 2, 4), lax.rem(at, 2)
    return c, jnp.where(c == turn, z, x)


def bundle(blocks):
    def body(*refs):
        _, at = place(0)
        for k in range(4):
            refs[4][lax.rem(at + 4 - k, 4)] = refs[k][...]

    return call(body, "bundle", 4, struct((4, 96, 1024), BF16), 2**10, 2 * MIB)(*blocks)


def half_of_weights(bundles):
    def body(*refs):
        c, at = place(1)
        for k in range(4):
            other = lax.rem(at + 4 - k, 4)
            for j in range(4):
                refs[4][jnp.where(c == 0, other * 4 + j, j * 4 + other)] = refs[k][j]

    return call(body, "half_of_weights", 4, struct((N_CHIP, 96, 1024), BF16), 2**10, 6 * MIB)(*bundles)


def whole_weights(own, other):
    def body(a, b, out):
        c = lax.rem(lax.axis_index("dp"), 2)

        @pl.loop(0, N_CHIP)
        def _(q):
            out[2 * q + c] = a[q]
            out[2 * q + 1 - c] = b[q]

    return call(body, "whole_weights", 2, struct((2 * N_CHIP, 96, 1024), BF16), 2**10, 12 * MIB)(own, other)


def local(
    pool_tokens,
    pool_cotangent,
    token_ids,
    route_weights,
    gate_weight,
    up_weight,
    down_weight,
    momentum_gate,
    momentum_up,
    momentum_down,
):
    tie = lax.optimization_barrier

    def picked(k, pool):
        return pick_rows(ids[k : k + 1], [pool])[0]

    ids = [token_ids] + [around_y(token_ids, N_EXPERT - k) for k in (1, 2, 3)]
    x, c = [None] * 4, [None] * 4
    x[1], x[3] = picked(1, pool_tokens), picked(3, pool_tokens)
    ids, x[1], x[3], shards = tie((ids, x[1], x[3], (gate_weight[0], up_weight[0], down_weight[0])))

    packed = pack(*shards)
    blocks = spread(packed, 0)
    x[1], x[3] = around_y(x[1], 1), around_y(x[3], 3)
    (x[2],) = pick_rows(ids[2:3], [pool_tokens, pool_cotangent], stacked=True)
    blocks, (ids, x[1:]) = tie_far([packed, *blocks], (ids, x[1:]), last=True)

    block = bundle(blocks)
    blocks = spread(block, 1)
    x[2] = c[2] = around_y(x[2], 2)
    c[1], c[3] = picked(1, pool_cotangent), picked(3, pool_cotangent)
    x[0], c[0] = pick_rows(ids[:1], [pool_tokens, pool_cotangent])
    blocks, (x, c) = tie_far([block, *blocks], (x, [c[0], c[1], c[3]]), last=True)
    c = [c[0], c[1], x[2], c[2]]

    mine = half_of_weights(blocks)
    weights = whole_weights(mine, other_core(mine))
    c[1], c[3] = around_y(c[1], 1), around_y(c[3], 3)

    hidden_t, gate_factor, act, xt = forward(x, weights)
    early, downs = backward_early((c[0], c[2]), route_weights, hidden_t, weights)
    keep_down, send_down, hidden_grad = backward_down((c[1], c[3]), route_weights, hidden_t, early, downs, weights)
    keep_in, send_in, both = backward_in(hidden_grad, gate_factor, act, xt)
    received_down, send_in = tie((other_core(send_down), send_in))
    keep, received = (keep_in, keep_down), (other_core(send_in), received_down)
    slots = slot_gradients(both, weights)
    received, slots = lax.optimization_barrier((received, list(slots)))

    mine = pair_moments(keep, received)
    sent = pair_merge(keep, received, mine, other_core(mine))
    parts = [sent[0], *to_others(sent, 0)]
    back = [slots[0], None, around_y(slots[2], 2), None]
    parts, back[2] = tie_far(parts, back[2])
    sent, slots[1], slots[3] = tie((turn_over(parts), slots[1], slots[3]))
    parts = [sent[0], *to_others(sent, 1)]
    back[1], back[3] = around_y(slots[1], 3), around_y(slots[3], 1)
    parts, back[1] = tie_far(parts, back[1])
    products, pool_grad = sum_dp(gram(parts), ids, back)
    outs = finish(
        parts,
        products,
        gate_weight[0],
        up_weight[0],
        down_weight[0],
        momentum_gate[0],
        momentum_up[0],
        momentum_down[0],
    )
    return (*(a[None] for a in outs), pool_grad)


def solution(mesh):
    in_specs = (
        P("dp", "expert"),
        P("dp", "expert"),
        P("expert", "dp"),
        P("expert", "dp"),
        P("expert", "dp", None),
        P("expert", "dp", None),
        P("expert", "dp", None),
        P("expert", "dp", None),
        P("expert", "dp", None),
        P("expert", "dp", None),
    )
    out_specs = (
        P("expert", "dp", None),
        P("expert", "dp", None),
        P("expert", "dp", None),
        P("expert", "dp", None),
        P("expert", "dp", None),
        P("expert", "dp", None),
        P("dp", "expert"),
    )
    return jax.shard_map(local, mesh=mesh, in_specs=in_specs, out_specs=out_specs, check_vma=False)
```
